128 devices in a mesh: seq: 16 (over x, z), head: 8 (over y, core).
Axes of the slice: x: 4, y: 4, z: 4, core: 2. Of those that a mesh axis runs over, the one named last changes fastest.
Arguments:
- tokens: bfloat16 [2048, 4, 2048], P('seq', None, 'head'), may hold values from -6 to 6
- attn_gain: bfloat16 [2048], replicated, may hold values from 0.25 to 1.75
- query_weight: bfloat16 [2048, 2048], P(None, 'head'), may hold values from -0.125 to 0.125
- key_weight: bfloat16 [2048, 2048], P(None, 'head'), may hold values from -0.125 to 0.125
- value_weight: bfloat16 [2048, 2048], P(None, 'head'), may hold values from -0.125 to 0.125
- head_gain: bfloat16 [2048], P('head'), may hold values from 0.25 to 1.75
- out_weight: bfloat16 [2048, 2048], P('head'), may hold values from -0.125 to 0.125
- moe_gain: bfloat16 [2048], replicated, may hold values from 0.25 to 1.75
- route_ids: int32 [2048, 4, 8], P(('seq', 'head')), may hold values from 0 to 63, all different within a row; in each aligned block of 64 rows (0 to 63, 64 to 127, ..., all dimensions but the last counted through in order) at most 12 rows name the same one
- route_weight: float32 [2048, 4, 8], P(('seq', 'head')), may hold values from 0.05 to 0.3
- expert_gate: bfloat16 [128, 2048, 512], P(('seq', 'head')), may hold values from -0.125 to 0.125
- expert_up: bfloat16 [128, 2048, 512], P(('seq', 'head')), may hold values from -0.125 to 0.125
- expert_down: bfloat16 [128, 512, 2048], P(('seq', 'head')), may hold values from -0.1875 to 0.1875
Outputs:
- layer_output: bfloat16 [2048, 4, 2048], P(('seq', 'head'))
The draws below stay inside these ranges and needn't reach their ends.
Inputs may be any that keep to these rules, and one draw needn't show every extreme that they name: `route_ids`: the rows [position, sequence] taken position-major form aligned blocks of 64 rows, the rows of one device; within every block no expert is named by more than 12 routes, and in every draw some block has an expert named by exactly 12 routes. The 8 experts of a row differ.
All inputs are finite; a program needn't handle non-finite values.
Results may differ from the reference program's by a relative error of at most 0.017.
Values may be sent and summed in bfloat16 or wider, within the bound.
No kernel may reach another device: no remote copies, remote signals or barrier semaphores. Data moves between devices by JAX's collectives and lax.ppermute only.
A program may use at most 128 MiB of HBM per device.

```python
import math
import jax
import jax.numpy as jnp
import numpy as np
from jax import lax

D = 2048
HEADS = 16
HEAD_DIM = 128
FF = 1024
EXPERTS = 64
TOP = 8
BATCH = 4
SPAN = 128
LENGTH = 2048
ROWS = 64
CAP = 12
N_SEQ = 16
N_HEAD = 8
DEVICES = 128


def levels(stream_key, extent, cuts, least, largest):
    def one(dim, parts):
        draws = jax.random.uniform(jax.random.fold_in(jax.random.fold_in(stream_key, 6), dim), (parts,), jnp.float32, least / len(cuts), largest / len(cuts))
        return jnp.repeat(jnp.exp(draws), extent[dim] // parts).reshape((-1,) + (1,) * (len(extent) - dim - 1))

    factor_of = one(*cuts[0])
    for cut in cuts[1:]:
        factor_of = factor_of * one(*cut)
    return factor_of


def deal_out(rng, own, number, rows, count, top, most, lean):
    order = jax.random.permutation(rng, count)
    crowded, usual = load_shares(count, rows * top, most, lean, True), load_shares(count, rows * top, most, lean, False)
    places = jnp.arange(count)

    def named(tallies, turn):
        used = int((tallies > 0).sum())
        fixed = max(1, used // 4)
        moved = fixed + (places - fixed + turn * (used - fixed)) % max(1, count - fixed)
        return jnp.zeros((count,), jnp.int32).at[order[jnp.where(places < fixed, places, moved)]].set(jnp.asarray(tallies, jnp.int32))

    tallies = jnp.where(number % 4 == 0, named(crowded, number // 4), named(usual, number - number // 4 - 1))
    mixed = jax.random.permutation(jax.random.fold_in(own, 3), count)
    donor, taker = mixed[0:count // 2 * 2:2], mixed[1:count // 2 * 2:2]
    margin = jnp.minimum(tallies[donor] - 1, most - tallies[taker]) // 2
    margin = jnp.where((donor == order[0]) | (taker == order[0]) | (tallies[taker] == 0), 0, jnp.maximum(margin, 0))
    moved = jax.random.randint(jax.random.fold_in(own, 4), (count // 2,), 0, 1 << 20) % (margin + 1)
    tallies = tallies.at[donor].add(-moved).at[taker].add(moved)
    items = jnp.searchsorted(jnp.cumsum(tallies), jnp.arange(rows * top), side="right").astype(jnp.int32)
    grid = items.reshape(top, rows).T
    grid = grid[jax.random.permutation(jax.random.fold_in(own, 1), rows)]
    turn = jax.random.randint(jax.random.fold_in(own, 2), (rows, 1), 0, top)
    return jnp.take_along_axis(grid, (jnp.arange(top)[None, :] + turn) % top, axis=1)


def load_shares(amount, total, most, slope, full):
    portions = [(1 << 20) // math.isqrt(standing ** slope) + 1 for standing in range(1, amount + 1)]
    largest = most if full else min(most, max(-(-total // amount), total * portions[0] // sum(portions)))
    least = 1 if total - largest >= amount - 1 else 0
    holding, rest = [largest] + [least] * (amount - 1), total - largest - least * (amount - 1)
    while rest > 0:
        candidates = [i for i in range(1, amount) if holding[i] < largest] or [i for i in range(1, amount) if holding[i] < most]
        mass, remaining = sum([portions[i] for i in candidates]), rest
        for i in candidates:
            more = min(most - holding[i], max(1, remaining * portions[i] // mass), rest)
            holding[i] = holding[i] + more
            rest = rest - more
    return np.array(holding)


def bell_draw(key, shape, scale, reach, shards=(), kind=jnp.bfloat16):
    level = levels(key, shape, shards, -0.22, 0.18) if shards else 1.0
    values = jax.random.normal(key, shape, jnp.float32) * scale * level
    return jnp.minimum(jnp.maximum(values, -reach), reach).astype(kind)


def setup_inputs(seed: int = 0) -> dict:
    key_list = jax.random.split(jax.random.key(seed), 14)
    tokens = bell_draw(key_list[0], (LENGTH, BATCH, D), 1.0, 6.0, ((0, 16), (2, 8)))
    attn_gain = jnp.clip(1.0 + 0.15 * jax.random.normal(key_list[1], (D,), jnp.float32), 0.25, 1.75).astype(jnp.bfloat16)
    query_weight = bell_draw(key_list[2], (D, D), D ** -0.5, 0.125, ((1, 8),))
    key_weight = bell_draw(key_list[3], (D, D), D ** -0.5, 0.125, ((1, 8),))
    value_weight = bell_draw(key_list[4], (D, D), D ** -0.5, 0.125, ((1, 8),))
    head_gain = jnp.clip(1.0 + 0.15 * jax.random.normal(key_list[5], (D,), jnp.float32), 0.25, 1.75).astype(jnp.bfloat16)
    out_weight = bell_draw(key_list[6], (D, D), D ** -0.5, 0.125, ((0, 8),))
    moe_gain = jnp.clip(1.0 + 0.15 * jax.random.normal(key_list[7], (D,), jnp.float32), 0.25, 1.75).astype(jnp.bfloat16)
    route_ids_keys = jax.random.split(jax.random.fold_in(key_list[8], 1), LENGTH * BATCH // ROWS)
    route_ids_turns = jax.random.permutation(jax.random.fold_in(key_list[8], 3), LENGTH * BATCH // ROWS)
    route_ids = jax.vmap(lambda own, number: deal_out(jax.random.fold_in(key_list[8], 2), own, number, ROWS, EXPERTS, TOP, CAP, 2))(route_ids_keys, route_ids_turns).reshape((LENGTH, BATCH, TOP))
    route_weight = jnp.clip(0.05 + 0.25 * jax.random.uniform(key_list[9], (LENGTH, BATCH, TOP), jnp.float32) ** levels(key_list[9], (LENGTH, BATCH, TOP), ((0, 128),), -0.2, 0.2), 0.05, 0.3)
    expert_gate = bell_draw(key_list[10], (2 * EXPERTS, D, FF // 2), D ** -0.5, 0.125, ((0, 128),))
    expert_up = bell_draw(key_list[11], (2 * EXPERTS, D, FF // 2), D ** -0.5, 0.125, ((0, 128),))
    expert_down = bell_draw(key_list[12], (2 * EXPERTS, FF // 2, D), FF ** -0.5, 0.1875, ((0, 128),))
    return {"tokens": tokens, "attn_gain": attn_gain, "query_weight": query_weight, "key_weight": key_weight, "value_weight": value_weight, "head_gain": head_gain, "out_weight": out_weight, "moe_gain": moe_gain, "route_ids": route_ids, "route_weight": route_weight, "expert_gate": expert_gate, "expert_up": expert_up, "expert_down": expert_down}


norm_eps = 1e-05
head_eps = 1e-06

def root_scale(values, gain_values, epsilon):
    return values * lax.rsqrt(lax.optimization_barrier(jnp.mean(values * values, axis=-1, keepdims=True)) + epsilon) * gain_values.astype(jnp.float32)

def reference(tokens, attn_gain, query_weight, key_weight, value_weight, head_gain, out_weight, moe_gain, route_ids, route_weight, expert_gate, expert_up, expert_down):
    token_count = LENGTH * BATCH
    stream = tokens.astype(jnp.float32).reshape(token_count, D)
    normed = root_scale(stream, attn_gain, norm_eps).astype(jnp.bfloat16)
    block_shape = (N_SEQ, SPAN, BATCH, HEADS, HEAD_DIM)
    query_rows = jax.nn.silu(jnp.dot(normed, query_weight, preferred_element_type=jnp.float32)).astype(jnp.bfloat16).reshape(block_shape)
    key_rows = jax.nn.silu(jnp.dot(normed, key_weight, preferred_element_type=jnp.float32)).astype(jnp.bfloat16).reshape(block_shape)
    value_rows = jnp.dot(normed, value_weight, preferred_element_type=jnp.float32).astype(jnp.bfloat16).reshape(block_shape)

    def block_state(pair):
        return jnp.einsum('sbhd,sbhe->bhde', pair[0].astype(jnp.float32), pair[1].astype(jnp.float32))
    states = lax.map(block_state, (key_rows, value_rows))
    totals = jnp.cumsum(states, axis=0)
    carried = jnp.concatenate([jnp.zeros_like(states[:1]), totals[:-1]], axis=0)
    position = lax.broadcasted_iota(jnp.int32, (SPAN, SPAN), 0)
    key_position = lax.broadcasted_iota(jnp.int32, (SPAN, SPAN), 1)
    gain_heads = head_gain.reshape(HEADS, HEAD_DIM)

    def block_mix(group):
        query_block, key_block, value_block, carried_block = group
        scores = jnp.einsum('pbhd,sbhd->bhps', query_block.astype(jnp.float32), key_block.astype(jnp.float32))
        scores = jnp.where(position >= key_position, scores, 0.0).astype(jnp.bfloat16)
        local_mix = jnp.einsum('bhps,sbhd->pbhd', scores.astype(jnp.float32), value_block.astype(jnp.float32))
        carried_mix = jnp.einsum('pbhd,bhde->pbhe', query_block.astype(jnp.float32), carried_block, precision=lax.Precision.HIGHEST)
        return root_scale(local_mix + carried_mix, gain_heads, head_eps).astype(jnp.bfloat16)
    attended = lax.map(block_mix, (query_rows, key_rows, value_rows, carried)).reshape(token_count, D)
    group_width = D // N_HEAD
    projected = jnp.zeros((token_count, D), jnp.float32)
    for group_index in range(N_HEAD):
        lower_col = group_index * group_width
        group_term = jnp.dot(attended[:, lower_col:lower_col + group_width], out_weight[lower_col:lower_col + group_width], preferred_element_type=jnp.float32).astype(jnp.bfloat16)
        projected = projected + lax.optimization_barrier(group_term).astype(jnp.float32)
    residual_stream = stream + projected
    moe_input = root_scale(residual_stream, moe_gain, norm_eps).astype(jnp.bfloat16)
    route_count = ROWS * TOP
    expert_ids = route_ids.reshape(DEVICES, route_count)
    one_hot = (expert_ids[:, :, None] == jnp.arange(EXPERTS, dtype=jnp.int32)[None, None, :]).astype(jnp.int32)
    expert_slot = lax.optimization_barrier(jnp.sum(jnp.cumsum(one_hot, axis=1) * one_hot, axis=2)) - 1
    column = jnp.arange(DEVICES, dtype=jnp.int32)[:, None] * CAP + expert_slot
    token_index = (jnp.arange(DEVICES * route_count, dtype=jnp.int32) // TOP).reshape(DEVICES, route_count)
    row_table = jnp.full((EXPERTS, DEVICES * CAP), token_count, jnp.int32).at[expert_ids, column].set(token_index)
    weight_table = jnp.zeros((EXPERTS, DEVICES * CAP), jnp.float32).at[expert_ids, column].set(route_weight.reshape(DEVICES, route_count))
    padded_input = jnp.concatenate([moe_input, jnp.zeros((1, D), jnp.bfloat16)], axis=0)

    def expert_step(moe_total, expert_index):
        rows_index = row_table[expert_index]
        expert_rows = padded_input[rows_index]
        expert_sum = jnp.zeros((DEVICES * CAP, D), jnp.float32)
        for half_index in range(2):
            half_slot = 2 * expert_index + half_index
            gate_rows = jnp.dot(expert_rows, expert_gate[half_slot], preferred_element_type=jnp.float32)
            up_rows = jnp.dot(expert_rows, expert_up[half_slot], preferred_element_type=jnp.float32)
            activated = (jax.nn.silu(gate_rows) * up_rows).astype(jnp.bfloat16)
            half_output = jnp.dot(activated, expert_down[half_slot], preferred_element_type=jnp.float32).astype(jnp.bfloat16)
            expert_sum = expert_sum + lax.optimization_barrier(half_output).astype(jnp.float32)
        rounded_sum = lax.optimization_barrier(expert_sum.astype(jnp.bfloat16)).astype(jnp.float32)
        moe_total = moe_total.at[rows_index].add(rounded_sum * weight_table[expert_index][:, None])
        return (moe_total, None)
    moe_total, unused_out = lax.scan(expert_step, jnp.zeros((token_count + 1, D), jnp.float32), jnp.arange(EXPERTS, dtype=jnp.int32))
    moe_output = moe_total[:token_count]
    return (residual_stream + moe_output).astype(jnp.bfloat16).reshape(LENGTH, BATCH, D)
```

```python
import functools

import jax
import jax.numpy as jnp
import numpy as np
from jax import lax
from jax.experimental import pallas as pl
from jax.experimental.pallas import tpu as pltpu
from jax.sharding import Mesh, PartitionSpec as P

EXPERTS = 64
TOP = 8
CAP = 12
QUART = 4
PACK = CAP * QUART
COLS = EXPERTS * PACK
GROUP = 4

norm_eps = 1e-05
head_eps = 1e-06

BF = jnp.bfloat16
F32 = jnp.float32


def shifted(x, axis, by):
    count = lax.axis_size(axis)
    return lax.ppermute(x, axis, [(i, (i + by) % count) for i in range(count)])


def exchanged(x, axes):
    return lax.all_to_all(x, axes, split_axis=0, concat_axis=0, tiled=True)


def dot(a, b, dims=((1,), (0,))):
    return lax.dot_general(a, b, (dims, ((), ())), preferred_element_type=F32)


def silu(v):
    return v / (1.0 + jnp.exp(-v))


def vmem(count):
    return [pl.BlockSpec(memory_space=pltpu.VMEM)] * count


def call(kernel, name, out_shape, *args, scratch=()):
    several = isinstance(out_shape, (list, tuple))
    return pl.pallas_call(
        kernel,
        out_shape=out_shape,
        in_specs=vmem(len(args)),
        out_specs=vmem(len(out_shape)) if several else vmem(1)[0],
        scratch_shapes=list(scratch),
        name=name,
    )(*args)


def route_kernel(ids_ref, ids_t_ref, weight_ref, spread_ref, spread_t_ref, place_ref, place_t_ref, send_ref, high_ref, low_ref):
    rows = ids_ref.shape[0]
    ids = ids_ref[...]
    ids_t = ids_t_ref[...]
    weights = weight_ref[...]
    across = lax.broadcasted_iota(jnp.int32, (rows, EXPERTS), 1)
    down = lax.broadcasted_iota(jnp.int32, (EXPERTS, rows), 0)
    named = jnp.zeros((rows, EXPERTS), F32)
    named_t = jnp.zeros((EXPERTS, rows), F32)
    weight = jnp.zeros((rows, EXPERTS), F32)
    for j in range(TOP):
        hit = ids[:, j : j + 1] == across
        named = named + jnp.where(hit, 1.0, 0.0)
        weight = weight + jnp.where(hit, weights[:, j : j + 1], 0.0)
        named_t = named_t + jnp.where(ids_t[j : j + 1, :] == down, 1.0, 0.0)
    i0 = lax.broadcasted_iota(jnp.int32, (rows, rows), 0)
    i1 = lax.broadcasted_iota(jnp.int32, (rows, rows), 1)
    before = dot(jnp.where(i1 < i0, 1.0, 0.0).astype(BF), named.astype(BF))
    before_t = dot(named_t.astype(BF), jnp.where(i0 < i1, 1.0, 0.0).astype(BF))
    slot = jnp.where(named > 0.5, before, 128.0)
    slot_t = jnp.where(named_t > 0.5, before_t, 128.0)
    slot_all = jnp.concatenate([slot + float(CAP * q) for q in range(QUART)], axis=0).astype(BF)
    slot_all_t = jnp.concatenate([slot_t + float(CAP * q) for q in range(QUART)], axis=1).astype(BF)
    send_ref[...] = jnp.where(dot(spread_t_ref[...], slot_all_t) == place_t_ref[...], 1.0, 0.0).astype(BF)
    match = dot(slot_all, spread_ref[...]) == place_ref[...]
    high = weight.astype(BF)
    low = (weight - high.astype(F32)).astype(BF)
    for part, out_ref in ((high, high_ref), (low, low_ref)):
        spread = dot(part, spread_ref[...])
        out_ref[...] = jnp.where(match, jnp.concatenate([spread] * QUART, axis=0), 0.0).astype(BF)


def local_kernel(*refs):
    pieces, refs = refs[:10], refs[10:]
    wq_ref, wk_ref, wv_ref, gain_ref, q_ref, local_ref, state_ref, own_ref, normed_ref = refs
    y = lax.axis_index("y")
    c = lax.axis_index("c")
    rows, width = pieces[0].shape
    half = rows // 2
    blocks = []
    for part, core in ((pieces[:5], c), (pieces[5:], 1 - c)):
        for ref, away, lo, hi in (
            (part[0], 0, 0, rows),
            (part[1], 3, 0, rows),
            (part[2], 1, 0, rows),
            (part[3], 2, 0, half),
            (part[4], 2, half, rows),
        ):
            blocks.append((ref, ((y + away) & 3) * 2 + core, lo, hi))
    total = [jnp.zeros((half, 1), F32), jnp.zeros((half, 1), F32)]
    for ref, block, lo, hi in blocks:
        for h in range(lo // half, hi // half):
            values = ref[pl.ds(h * half - lo, half), :].astype(F32)
            total[h] = total[h] + jnp.sum(values * values, axis=1, keepdims=True)
    scale = [lax.rsqrt(t / (8 * width) + norm_eps) for t in total]
    mine = y * 2 + c
    own_rows = rows // 8
    for ref, block, lo, hi in blocks:
        gain = gain_ref[block]
        columns = pl.ds(pl.multiple_of(block * width, width), width)
        for h in range(lo // half, hi // half):
            values = ref[pl.ds(h * half - lo, half), :].astype(F32)
            normed_ref[pl.ds(h * half, half), columns] = (values * scale[h] * gain).astype(BF)
        if lo == 0 and hi == rows:
            own_ref[:, columns] = ref[pl.ds(pl.multiple_of(mine * own_rows, own_rows), own_rows), :]
        else:
            @pl.when((mine >= 4) == (lo > 0))
            def _():
                start = pl.multiple_of((mine & 3) * own_rows, own_rows)
                own_ref[:, columns] = ref[pl.ds(start, own_rows), :]
    normed = normed_ref[...]
    q = silu(dot(normed, wq_ref[...])).astype(BF)
    k = silu(dot(normed, wk_ref[...])).astype(BF)
    v = dot(normed, wv_ref[...]).astype(BF)
    q_ref[...] = q
    i0 = lax.broadcasted_iota(jnp.int32, (rows, rows), 0)
    i1 = lax.broadcasted_iota(jnp.int32, (rows, rows), 1)
    seen = (((i0 ^ i1) & 3) == 0) & (i1 <= i0)
    sequence = lax.broadcasted_iota(jnp.int32, (rows, 128), 0) & 3
    for h in range(2):
        cols = slice(h * 128, (h + 1) * 128)
        scores = jnp.where(seen, dot(q[:, cols], k[:, cols], ((1,), (1,))), 0.0).astype(BF)
        local_ref[:, cols] = dot(scores, v[:, cols])
        keys = k[:, cols].astype(F32)
        apart = jnp.concatenate([jnp.where(sequence == b, keys, 0.0).astype(BF) for b in range(4)], axis=1)
        state_ref[h * rows : (h + 1) * rows, :] = dot(apart, v[:, cols], ((0,), (0,))).astype(BF)


def prefix_kernel(states_ref, before_ref):
    running = jnp.zeros(states_ref.shape[1:], F32)
    for i in range(states_ref.shape[0]):
        before_ref[i] = running.astype(BF)
        running = running + states_ref[i].astype(F32)


def mix_kernel(q_ref, local_ref, carried_ref, gain_ref, keep_ref, pass_ref):
    c = lax.axis_index("c")
    rows = q_ref.shape[0]
    own_rows = rows // 8
    sequence = lax.broadcasted_iota(jnp.int32, (rows, 128), 0) & 3
    for h in range(2):
        cols = slice(h * 128, (h + 1) * 128)
        q = q_ref[:, cols].astype(F32)
        apart = jnp.concatenate([jnp.where(sequence == b, q, 0.0).astype(BF) for b in range(4)], axis=1)
        mixed = local_ref[:, cols] + dot(apart, carried_ref[h * rows : (h + 1) * rows, :])
        mean = jnp.mean(mixed * mixed, axis=1, keepdims=True)
        attended = mixed * lax.rsqrt(mean + head_eps) * gain_ref[:, cols].astype(F32)
        for i in range(4):
            even = attended[2 * i * own_rows : (2 * i + 1) * own_rows]
            odd = attended[(2 * i + 1) * own_rows : (2 * i + 2) * own_rows]
            target = slice(i * own_rows, (i + 1) * own_rows)
            keep_ref[target, cols] = jnp.where(c == 0, even, odd).astype(BF)
            pass_ref[target, cols] = jnp.where(c == 0, odd, even).astype(BF)


def project_kernel(keep_ref, other_ref, own_weight_ref, other_weight_ref, out_ref):
    out_ref[...] = (dot(keep_ref[...], own_weight_ref[...]) + dot(other_ref[...], other_weight_ref[...])).astype(BF)


def dispatch_kernel(parts_ref, own_ref, gain_ref, send_table_ref, residual_ref, out_ref):
    rows, width = own_ref.shape
    residual = own_ref[...].astype(F32)
    for i in range(parts_ref.shape[0]):
        residual = residual + parts_ref[i].astype(F32)
    residual_ref[...] = residual
    mean = jnp.mean(residual * residual, axis=1, keepdims=True)
    entering = (residual * lax.rsqrt(mean + norm_eps) * gain_ref[...].astype(F32)).astype(BF)
    step = width // QUART
    stacked = jnp.concatenate([entering[:, q * step : (q + 1) * step] for q in range(QUART)], axis=0)
    out_ref[...] = dot(send_table_ref[...], stacked).astype(BF)


def expert_kernel(rows_ref, order_ref, back_ref, gate_ref, up_ref, down_ref, gate_b_ref, up_b_ref, down_b_ref, out_ref, x_ref, sum_ref):
    step = rows_ref.shape[1]
    block = GROUP * PACK
    part = GROUP * CAP
    groups = rows_ref.shape[0] // block
    order = order_ref[...]
    back = back_ref[...]
    for g in range(groups):
        sorted_rows = dot(order, rows_ref[g * block : (g + 1) * block, :]).astype(BF)
        for q in range(QUART):
            x_ref[g * part : (g + 1) * part, q * step : (q + 1) * step] = sorted_rows[q * part : (q + 1) * part]
    x = x_ref[...]

    def half_output(gate, up, down):
        gated = dot(x, gate)
        active = (silu(gated) * dot(x, up)).astype(BF)
        return dot(active, down).astype(BF)

    sum_ref[...] = half_output(gate_ref[...], up_ref[...], down_ref[...])
    second = half_output(gate_b_ref[...], up_b_ref[...], down_b_ref[...])
    sum_ref[...] = (sum_ref[...].astype(F32) + second.astype(F32)).astype(BF)
    for g in range(groups):
        stacked = jnp.concatenate(
            [sum_ref[g * part : (g + 1) * part, q * step : (q + 1) * step] for q in range(QUART)], axis=0
        )
        out_ref[g * block : (g + 1) * block, :] = dot(back, stacked).astype(BF)


def combine_kernel(rows_ref, high_ref, low_ref, residual_ref, out_ref):
    rows = residual_ref.shape[0]
    step = rows_ref.shape[1]
    total = dot(high_ref[...], rows_ref[...]) + dot(low_ref[...], rows_ref[...])
    for q in range(QUART):
        cols = slice(q * step, (q + 1) * step)
        out_ref[:, cols] = (residual_ref[:, cols] + total[q * rows : (q + 1) * rows]).astype(BF)


def tables():
    column = np.arange(COLS)
    spread = (column[None, :] // PACK == np.arange(EXPERTS)[:, None]).astype(np.float32)
    place = (column % PACK).astype(np.float32)
    size = GROUP * PACK
    order = np.zeros((size, size), np.float32)
    for q in range(QUART):
        for s in range(GROUP):
            for r in range(CAP):
                order[(q * GROUP + s) * CAP + r, (s * QUART + q) * CAP + r] = 1.0
    return spread, place, order


def body(
    tokens, attn_gain, query_weight, key_weight, value_weight, head_gain, out_weight, moe_gain,
    route_ids, route_weight, expert_gate, expert_up, expert_down,
):
    shape = jax.ShapeDtypeStruct
    block_len, batch, width = tokens.shape
    rows = block_len * batch
    model = attn_gain.shape[0]
    own_rows = rows // 8
    hidden = expert_gate.shape[2]
    spread, place, order = tables()

    mine = tokens.reshape(rows, width)
    from_left = shifted(mine, "y", 1)
    from_right = shifted(mine, "y", -1)
    far_low = shifted(from_left[: rows // 2], "y", 1)
    far_high = shifted(from_right[rows // 2 :], "y", -1)
    pieces = [mine, from_left, from_right, far_low, far_high]
    pieces = pieces + [shifted(p, "c", 1) for p in pieces]

    other_out = shifted(out_weight, "c", 1)
    gate = expert_gate.reshape(model, hidden)
    up = expert_up.reshape(model, hidden)
    down = expert_down.reshape(hidden, model)
    other_gate = shifted(gate, "c", 1)
    other_up = shifted(up, "c", 1)
    other_down = shifted(down, "c", 1)

    ids = route_ids.reshape(own_rows, TOP)
    send_table, high, low = call(
        route_kernel,
        "route",
        (shape((COLS, QUART * own_rows), BF), shape((QUART * own_rows, COLS), BF), shape((QUART * own_rows, COLS), BF)),
        ids,
        ids.T,
        route_weight.reshape(own_rows, TOP),
        jnp.asarray(spread, BF),
        jnp.asarray(spread.T, BF),
        jnp.asarray(place[None, :]),
        jnp.asarray(place[:, None]),
    )

    q, local_mix, state, own = call(
        local_kernel,
        "local",
        (shape((rows, width), BF), shape((rows, width), F32), shape((2 * rows, 128), BF), shape((own_rows, model), BF)),
        *pieces,
        query_weight,
        key_weight,
        value_weight,
        attn_gain.astype(F32).reshape(8, 1, width),
        scratch=[pltpu.VMEM((rows, model), BF)],
    )
    blocks = lax.axis_size(("x", "z"))
    states = exchanged(state.reshape(blocks, 2 * rows // blocks, 128), ("x", "z"))
    before = call(prefix_kernel, "prefix", shape(states.shape, BF), states)
    carried = exchanged(before, ("x", "z")).reshape(2 * rows, 128)
    keep, passed = call(
        mix_kernel,
        "mix",
        (shape((rows // 2, width), BF), shape((rows // 2, width), BF)),
        q,
        local_mix,
        carried,
        head_gain.reshape(1, width),
    )
    other = shifted(passed, "c", 1)
    partial = call(
        project_kernel, "project", shape((rows // 2, model), BF), keep, other, out_weight, other_out
    )
    parts = exchanged(partial.reshape(4, own_rows, model), "y")
    residual, sending = call(
        dispatch_kernel,
        "dispatch",
        (shape((own_rows, model), F32), shape((COLS, model // QUART), BF)),
        parts,
        own,
        moe_gain.reshape(1, model),
        send_table,
    )
    chips = ("x", "z", "y")
    received = exchanged(sending.reshape(EXPERTS, PACK, model // QUART), chips).reshape(COLS, model // QUART)
    results = call(
        expert_kernel,
        "experts",
        shape((COLS, model // QUART), BF),
        received,
        jnp.asarray(order, BF),
        jnp.asarray(order.T, BF),
        gate,
        up,
        down,
        other_gate,
        other_up,
        other_down,
        scratch=[pltpu.VMEM((EXPERTS * CAP, model), BF), pltpu.VMEM((EXPERTS * CAP, model), BF)],
    )
    returned = exchanged(results.reshape(EXPERTS, PACK, model // QUART), chips).reshape(COLS, model // QUART)
    out = call(combine_kernel, "combine", shape((own_rows, model), BF), returned, high, low, residual)
    return out.reshape(own_rows // batch, batch, model)


def solution(mesh):
    fine = Mesh(mesh.devices.reshape(4, 4, 4, 2), ("x", "z", "y", "c"))
    seq, head, every = ("x", "z"), ("y", "c"), ("x", "z", "y", "c")
    in_specs = (
        P(seq, None, head),
        P(),
        P(None, head),
        P(None, head),
        P(None, head),
        P(head),
        P(head, None),
        P(),
        P(every, None, None),
        P(every, None, None),
        P(every, None, None),
        P(every, None, None),
        P(every, None, None),
    )
    return jax.shard_map(body, mesh=fine, in_specs=in_specs, out_specs=P(every, None, None), check_vma=False)
```

```python
import functools

import jax
import jax.numpy as jnp
import numpy as np
from jax import lax
from jax.experimental import pallas as pl
from jax.experimental.pallas import tpu as pltpu
from jax.sharding import Mesh, PartitionSpec as P

EXPERTS = 64
TOP = 8
CAP = 12
QUART = 4
PACK = CAP * QUART
COLS = EXPERTS * PACK
GROUP = 4
CHUNKS = 4
SPANS = 2
STEPS = 4

norm_eps = 1e-05
head_eps = 1e-06

BF = jnp.bfloat16
F32 = jnp.float32


def shifted(x, axis, by):
    count = lax.axis_size(axis)
    return lax.ppermute(x, axis, [(i, (i + by) % count) for i in range(count)])


def exchanged(x, axes):
    return lax.all_to_all(x, axes, split_axis=0, concat_axis=0, tiled=True)


def dot(a, b, dims=((1,), (0,))):
    return lax.dot_general(a, b, (dims, ((), ())), preferred_element_type=F32)


def silu(v):
    return v / (1.0 + jnp.exp(-v))


def vmem(count):
    return [pl.BlockSpec(memory_space=pltpu.VMEM)] * count


def call(kernel, name, out_shape, *args, scratch=()):
    several = isinstance(out_shape, (list, tuple))
    return pl.pallas_call(
        kernel,
        out_shape=out_shape,
        in_specs=vmem(len(args)),
        out_specs=vmem(len(out_shape)) if several else vmem(1)[0],
        scratch_shapes=list(scratch),
        name=name,
    )(*args)


def route_kernel(ids_ref, ids_t_ref, weight_ref, send_ref, sum_ref):
    rows = ids_ref.shape[0]
    ids = ids_ref[...]
    ids_t = ids_t_ref[...]
    weights = weight_ref[...]
    across = lax.broadcasted_iota(jnp.int32, (rows, EXPERTS), 1)
    down = lax.broadcasted_iota(jnp.int32, (EXPERTS, rows), 0)
    named = jnp.zeros((rows, EXPERTS), F32)
    named_t = jnp.zeros((EXPERTS, rows), F32)
    weight = jnp.zeros((rows, EXPERTS), F32)
    for j in range(TOP):
        hit = ids[:, j : j + 1] == across
        named = named + jnp.where(hit, 1.0, 0.0)
        weight = weight + jnp.where(hit, weights[:, j : j + 1], 0.0)
        named_t = named_t + jnp.where(ids_t[j : j + 1, :] == down, 1.0, 0.0)
    i0 = lax.broadcasted_iota(jnp.int32, (rows, rows), 0)
    i1 = lax.broadcasted_iota(jnp.int32, (rows, rows), 1)
    before = dot(jnp.where(i1 < i0, 1.0, 0.0).astype(BF), named.astype(BF))
    before_t = dot(named_t.astype(BF), jnp.where(i0 < i1, 1.0, 0.0).astype(BF))
    slot = jnp.where(named > 0.5, before, 128.0)
    slot_t = jnp.where(named_t > 0.5, before_t, 128.0)
    slot_all = jnp.concatenate([slot + float(CAP * q) for q in range(QUART)], axis=0).astype(BF)
    slot_all_t = jnp.concatenate([slot_t + float(CAP * q) for q in range(QUART)], axis=1).astype(BF)

    def split(shape, dim, other):
        index = lax.broadcasted_iota(jnp.int32, shape, dim).astype(F32)
        expert = jnp.floor((index + 0.5) * (1.0 / PACK))
        spread = jnp.where(expert == lax.broadcasted_iota(jnp.int32, shape, other).astype(F32), 1.0, 0.0)
        return spread.astype(BF), index - expert * PACK

    spread_t, place_t = split((COLS, EXPERTS), 0, 1)
    send_ref[...] = jnp.where(dot(spread_t, slot_all_t) == place_t[:, :1], 1.0, 0.0).astype(BF)
    spread, place = split((EXPERTS, COLS), 1, 0)
    match = dot(slot_all, spread) == place[:1, :]
    weight_all = dot(weight.astype(BF), spread)
    sum_ref[...] = jnp.where(match, jnp.concatenate([weight_all] * QUART, axis=0), 0.0).astype(BF)


def local_kernel(*refs):
    pieces, refs = refs[:10], refs[10:]
    wk_ref, wv_ref, gain_ref, normed_ref, k_ref, v_ref, state_ref, own_ref = refs
    y = lax.axis_index("y")
    c = lax.axis_index("c")
    rows, width = pieces[0].shape
    half = rows // 2
    blocks = []
    for part, core in ((pieces[:5], c), (pieces[5:], 1 - c)):
        for ref, away, lo, hi in (
            (part[0], 0, 0, rows),
            (part[1], 3, 0, rows),
            (part[2], 1, 0, rows),
            (part[3], 2, 0, half),
            (part[4], 2, half, rows),
        ):
            blocks.append((ref, ((y + away) & 3) * 2 + core, lo, hi))
    total = [jnp.zeros((half, 1), F32), jnp.zeros((half, 1), F32)]
    for ref, block, lo, hi in blocks:
        for h in range(lo // half, hi // half):
            values = ref[pl.ds(h * half - lo, half), :].astype(F32)
            total[h] = total[h] + jnp.sum(values * values, axis=1, keepdims=True)
    scale = [lax.rsqrt(t / (8 * width) + norm_eps) for t in total]
    mine = y * 2 + c
    own_rows = rows // 8
    for ref, block, lo, hi in blocks:
        gain = gain_ref[block]
        columns = pl.ds(pl.multiple_of(block * width, width), width)
        for h in range(lo // half, hi // half):
            values = ref[pl.ds(h * half - lo, half), :].astype(F32)
            normed_ref[pl.ds(h * half, half), columns] = (values * scale[h] * gain).astype(BF)
        if lo == 0 and hi == rows:
            own_ref[:, columns] = ref[pl.ds(pl.multiple_of(mine * own_rows, own_rows), own_rows), :]
        else:
            @pl.when((mine >= 4) == (lo > 0))
            def _():
                start = pl.multiple_of((mine & 3) * own_rows, own_rows)
                own_ref[:, columns] = ref[pl.ds(start, own_rows), :]
    normed = normed_ref[...]
    k = silu(dot(normed, wk_ref[...])).astype(BF)
    v = dot(normed, wv_ref[...]).astype(BF)
    k_ref[...] = k
    v_ref[...] = v
    sequence = lax.broadcasted_iota(jnp.int32, (rows, 128), 0) & 3
    for h in range(2):
        cols = slice(h * 128, (h + 1) * 128)
        keys = k[:, cols].astype(F32)
        apart = jnp.concatenate([jnp.where(sequence == b, keys, 0.0).astype(BF) for b in range(4)], axis=1)
        state_ref[h * rows : (h + 1) * rows, :] = dot(apart, v[:, cols], ((0,), (0,))).astype(BF)


def score_kernel(normed_ref, wq_ref, k_ref, v_ref, q_ref, local_ref):
    rows = normed_ref.shape[0]
    q = silu(dot(normed_ref[...], wq_ref[...])).astype(BF)
    q_ref[...] = q
    i0 = lax.broadcasted_iota(jnp.int32, (rows, rows), 0)
    i1 = lax.broadcasted_iota(jnp.int32, (rows, rows), 1)
    seen = (((i0 ^ i1) & 3) == 0) & (i1 <= i0)
    for h in range(2):
        cols = slice(h * 128, (h + 1) * 128)
        scores = jnp.where(seen, dot(q[:, cols], k_ref[:, cols], ((1,), (1,))), 0.0).astype(BF)
        local_ref[:, cols] = dot(scores, v_ref[:, cols])


def prefix_kernel(states_ref, before_ref):
    running = jnp.zeros(states_ref.shape[1:], F32)
    for i in range(states_ref.shape[0]):
        before_ref[i] = running.astype(BF)
        running = running + states_ref[i].astype(F32)


def mix_kernel(q_ref, local_ref, carried_ref, gain_ref, keep_ref, pass_ref):
    c = lax.axis_index("c")
    rows = q_ref.shape[0]
    own_rows = rows // 8
    sequence = lax.broadcasted_iota(jnp.int32, (rows, 128), 0) & 3
    for h in range(2):
        cols = slice(h * 128, (h + 1) * 128)
        q = q_ref[:, cols].astype(F32)
        apart = jnp.concatenate([jnp.where(sequence == b, q, 0.0).astype(BF) for b in range(4)], axis=1)
        mixed = local_ref[:, cols] + dot(apart, carried_ref[h * rows : (h + 1) * rows, :])
        mean = jnp.mean(mixed * mixed, axis=1, keepdims=True)
        attended = mixed * lax.rsqrt(mean + head_eps) * gain_ref[:, cols].astype(F32)
        for i in range(4):
            even = attended[2 * i * own_rows : (2 * i + 1) * own_rows]
            odd = attended[(2 * i + 1) * own_rows : (2 * i + 2) * own_rows]
            target = slice(i * own_rows, (i + 1) * own_rows)
            keep_ref[target, cols] = jnp.where(c == 0, even, odd).astype(BF)
            pass_ref[target, cols] = jnp.where(c == 0, odd, even).astype(BF)


def project_kernel(keep_ref, other_ref, own_weight_ref, other_weight_ref, out_ref):
    out_ref[...] = (dot(keep_ref[...], own_weight_ref[...]) + dot(other_ref[...], other_weight_ref[...])).astype(BF)


def dispatch_kernel(parts_ref, own_ref, gain_ref, send_table_ref, residual_ref, out_ref, stacked_ref):
    @pl.when(pl.program_id(0) == 0)
    def _():
        rows, width = own_ref.shape
        residual = own_ref[...].astype(F32)
        for i in range(parts_ref.shape[0]):
            residual = residual + parts_ref[i].astype(F32)
        residual_ref[...] = residual
        mean = jnp.mean(residual * residual, axis=1, keepdims=True)
        entering = (residual * lax.rsqrt(mean + norm_eps) * gain_ref[...].astype(F32)).astype(BF)
        step = width // QUART
        for q in range(QUART):
            stacked_ref[q * rows : (q + 1) * rows, :] = entering[:, q * step : (q + 1) * step]

    out_ref[...] = dot(send_table_ref[...], stacked_ref[...]).astype(BF)


def expert_kernel(
    rows_hbm, order_ref, back_ref, gate_hbm, up_hbm, down_hbm, gate_b_hbm, up_b_hbm, down_b_hbm, out_hbm,
    rows_ref, x_ref, out_ref, gate_ref, up_ref, down_ref, rows_sem, weight_sem, out_sem,
):
    step = rows_ref.shape[1]
    block = GROUP * PACK
    part = GROUP * CAP
    groups = rows_ref.shape[0] // block
    chunk = groups // CHUNKS
    row_copies = [
        pltpu.make_async_copy(
            rows_hbm.at[pl.ds(i * chunk * block, chunk * block)],
            rows_ref.at[pl.ds(i * chunk * block, chunk * block)],
            rows_sem.at[i],
        )
        for i in range(CHUNKS)
    ]
    weight_copies = [
        pltpu.make_async_copy(source, target.at[half], weight_sem.at[half, i])
        for half, sources in enumerate(((gate_hbm, up_hbm, down_hbm), (gate_b_hbm, up_b_hbm, down_b_hbm)))
        for i, (source, target) in enumerate(zip(sources, (gate_ref, up_ref, down_ref)))
    ]
    for copy in row_copies:
        copy.start()
    for copy in weight_copies:
        copy.start()
    order = order_ref[...]
    back = back_ref[...]
    for i in range(CHUNKS):
        row_copies[i].wait()
        for g in range(i * chunk, (i + 1) * chunk):
            sorted_rows = dot(order, rows_ref[g * block : (g + 1) * block, :]).astype(BF)
            for q in range(QUART):
                x_ref[g * part : (g + 1) * part, q * step : (q + 1) * step] = sorted_rows[q * part : (q + 1) * part]
    out_copies = []
    span = groups // SPANS
    for s in range(SPANS):
        lines = slice(s * span * part, (s + 1) * span * part)
        halves = []
        for half in range(2):
            if s == 0:
                weight_copies[3 * half].wait()
                weight_copies[3 * half + 1].wait()
            gated = dot(x_ref[lines, :], gate_ref[half])
            active = (silu(gated) * dot(x_ref[lines, :], up_ref[half])).astype(BF)
            if s == 0:
                weight_copies[3 * half + 2].wait()
            halves.append(dot(active, down_ref[half]).astype(BF))
        total = (halves[0].astype(F32) + halves[1].astype(F32)).astype(BF)
        for g in range(span):
            stacked = jnp.concatenate(
                [total[g * part : (g + 1) * part, q * step : (q + 1) * step] for q in range(QUART)], axis=0
            )
            at = (s * span + g) * block
            out_ref[at : at + block, :] = dot(back, stacked).astype(BF)
        size = span * block
        copy = pltpu.make_async_copy(
            out_ref.at[pl.ds(s * size, size)], out_hbm.at[pl.ds(s * size, size)], out_sem.at[s]
        )
        copy.start()
        out_copies.append(copy)
    for copy in out_copies:
        copy.wait()


def combine_kernel(rows_ref, table_ref, residual_ref, out_ref, total_ref):
    i = pl.program_id(0)
    product = dot(table_ref[...], rows_ref[...])

    @pl.when(i == 0)
    def _():
        total_ref[...] = product

    @pl.when(i > 0)
    def _():
        total_ref[...] += product

    @pl.when(i == pl.num_programs(0) - 1)
    def _():
        rows = residual_ref.shape[0]
        step = rows_ref.shape[1]
        for q in range(QUART):
            cols = slice(q * step, (q + 1) * step)
            out_ref[:, cols] = (residual_ref[:, cols] + total_ref[q * rows : (q + 1) * rows]).astype(BF)


def sorting():
    size = GROUP * PACK
    order = np.zeros((size, size), np.float32)
    for q in range(QUART):
        for s in range(GROUP):
            for r in range(CAP):
                order[(q * GROUP + s) * CAP + r, (s * QUART + q) * CAP + r] = 1.0
    return order


def body(
    tokens, attn_gain, query_weight, key_weight, value_weight, head_gain, out_weight, moe_gain,
    route_ids, route_weight, expert_gate, expert_up, expert_down,
):
    shape = jax.ShapeDtypeStruct
    block_len, batch, width = tokens.shape
    rows = block_len * batch
    model = attn_gain.shape[0]
    own_rows = rows // 8
    hidden = expert_gate.shape[2]
    order = sorting()

    mine = tokens.reshape(rows, width)
    from_left = shifted(mine, "y", 1)
    from_right = shifted(mine, "y", -1)
    far_low = shifted(from_left[: rows // 2], "y", 1)
    far_high = shifted(from_right[rows // 2 :], "y", -1)
    pieces = [mine, from_left, from_right, far_low, far_high]
    pieces = pieces + [shifted(p, "c", 1) for p in pieces]

    other_out = shifted(out_weight, "c", 1)
    gate = expert_gate.reshape(model, hidden)
    up = expert_up.reshape(model, hidden)
    down = expert_down.reshape(hidden, model)
    other_gate = shifted(gate, "c", 1)
    other_up = shifted(up, "c", 1)
    other_down = shifted(down, "c", 1)

    ids = route_ids.reshape(own_rows, TOP)
    send_table, sum_table = call(
        route_kernel,
        "route",
        (shape((COLS, QUART * own_rows), BF), shape((QUART * own_rows, COLS), BF)),
        ids,
        ids.T,
        route_weight.reshape(own_rows, TOP),
    )

    normed, k, v, state, own = call(
        local_kernel,
        "local",
        (
            shape((rows, model), BF),
            shape((rows, width), BF),
            shape((rows, width), BF),
            shape((2 * rows, 128), BF),
            shape((own_rows, model), BF),
        ),
        *pieces,
        key_weight,
        value_weight,
        attn_gain.astype(F32).reshape(8, 1, width),
    )
    q, local_mix = call(
        score_kernel,
        "score",
        (shape((rows, width), BF), shape((rows, width), F32)),
        normed,
        query_weight,
        k,
        v,
    )
    blocks = lax.axis_size(("x", "z"))
    states = exchanged(state.reshape(blocks, 2 * rows // blocks, 128), ("x", "z"))
    before = call(prefix_kernel, "prefix", shape(states.shape, BF), states)
    carried = exchanged(before, ("x", "z")).reshape(2 * rows, 128)
    keep, passed = call(
        mix_kernel,
        "mix",
        (shape((rows // 2, width), BF), shape((rows // 2, width), BF)),
        q,
        local_mix,
        carried,
        head_gain.reshape(1, width),
    )
    other = shifted(passed, "c", 1)
    partial = call(
        project_kernel, "project", shape((rows // 2, model), BF), keep, other, out_weight, other_out
    )
    parts = exchanged(partial.reshape(4, own_rows, model), "y")
    step = model // QUART
    residual, sending = pl.pallas_call(
        dispatch_kernel,
        out_shape=(shape((own_rows, model), F32), shape((COLS, step), BF)),
        grid=(STEPS,),
        in_specs=[
            pl.BlockSpec((4, own_rows, model), lambda i: (0, 0, 0)),
            pl.BlockSpec((own_rows, model), lambda i: (0, 0)),
            pl.BlockSpec((1, model), lambda i: (0, 0)),
            pl.BlockSpec((COLS // STEPS, QUART * own_rows), lambda i: (i, 0)),
        ],
        out_specs=(
            pl.BlockSpec((own_rows, model), lambda i: (0, 0)),
            pl.BlockSpec((COLS // STEPS, step), lambda i: (i, 0)),
        ),
        scratch_shapes=[pltpu.VMEM((QUART * own_rows, step), BF)],
        name="dispatch",
    )(parts, own, moe_gain.reshape(1, model), send_table)
    chips = ("x", "z", "y")
    received = exchanged(sending.reshape(EXPERTS, PACK, step), chips).reshape(COLS, step)
    anywhere = pl.BlockSpec(memory_space=pl.ANY)
    inside = pl.BlockSpec(memory_space=pltpu.VMEM)
    results = pl.pallas_call(
        expert_kernel,
        out_shape=shape((COLS, step), BF),
        in_specs=[anywhere, inside, inside] + [anywhere] * 6,
        out_specs=anywhere,
        scratch_shapes=[
            pltpu.VMEM((COLS, step), BF),
            pltpu.VMEM((EXPERTS * CAP, model), BF),
            pltpu.VMEM((COLS, step), BF),
            pltpu.VMEM((2, model, hidden), BF),
            pltpu.VMEM((2, model, hidden), BF),
            pltpu.VMEM((2, hidden, model), BF),
            pltpu.SemaphoreType.DMA((CHUNKS,)),
            pltpu.SemaphoreType.DMA((2, 3)),
            pltpu.SemaphoreType.DMA((SPANS,)),
        ],
        name="experts",
    )(received, jnp.asarray(order, BF), jnp.asarray(order.T, BF), gate, up, down, other_gate, other_up, other_down)
    returned = exchanged(results.reshape(EXPERTS, PACK, step), chips).reshape(COLS, step)
    out = pl.pallas_call(
        combine_kernel,
        out_shape=shape((own_rows, model), BF),
        grid=(STEPS,),
        in_specs=[
            pl.BlockSpec((COLS // STEPS, step), lambda i: (i, 0)),
            pl.BlockSpec((QUART * own_rows, COLS // STEPS), lambda i: (0, i)),
            pl.BlockSpec((own_rows, model), lambda i: (0, 0)),
        ],
        out_specs=pl.BlockSpec((own_rows, model), lambda i: (0, 0)),
        scratch_shapes=[pltpu.VMEM((QUART * own_rows, step), F32)],
        name="combine",
    )(returned, sum_table, residual)
    return out.reshape(own_rows // batch, batch, model)


def solution(mesh):
    fine = Mesh(mesh.devices.reshape(4, 4, 4, 2), ("x", "z", "y", "c"))
    seq, head, every = ("x", "z"), ("y", "c"), ("x", "z", "y", "c")
    in_specs = (
        P(seq, None, head),
        P(),
        P(None, head),
        P(None, head),
        P(None, head),
        P(head),
        P(head, None),
        P(),
        P(every, None, None),
        P(every, None, None),
        P(every, None, None),
        P(every, None, None),
        P(every, None, None),
    )
    return jax.shard_map(body, mesh=fine, in_specs=in_specs, out_specs=P(every, None, None), check_vma=False)
```

```python
import functools

import jax
import jax.numpy as jnp
import numpy as np
from jax import lax
from jax.experimental import pallas as pl
from jax.experimental.pallas import tpu as pltpu
from jax.sharding import Mesh, PartitionSpec as P

EXPERTS = 64
TOP = 8
CAP = 12
QUART = 4
PACK = CAP * QUART
COLS = EXPERTS * PACK
WIDE = 8
REST = CAP - WIDE
GROUP = 16
STEPS = 4

norm_eps = 1e-05
head_eps = 1e-06

BF = jnp.bfloat16
F32 = jnp.float32


def shifted(x, axis, by):
    count = lax.axis_size(axis)
    return lax.ppermute(x, axis, [(i, (i + by) % count) for i in range(count)])


def exchanged(x, axes):
    return lax.all_to_all(x, axes, split_axis=0, concat_axis=0, tiled=True)


def dot(a, b, dims=((1,), (0,))):
    return lax.dot_general(a, b, (dims, ((), ())), preferred_element_type=F32)


def silu(v):
    return v / (1.0 + jnp.exp(-v))


def vmem(count):
    return [pl.BlockSpec(memory_space=pltpu.VMEM)] * count


def placed_inside(x):
    return pltpu.with_memory_space_constraint(x, pltpu.VMEM)


def outside(x):
    return pltpu.with_memory_space_constraint(x, pltpu.HBM)


def limit(mib):
    return pltpu.CompilerParams(vmem_limit_bytes=mib * 2**20)


def call(kernel, name, out_shape, *args, scratch=(), mib=24):
    several = isinstance(out_shape, (list, tuple))
    return pl.pallas_call(
        kernel,
        out_shape=out_shape,
        in_specs=vmem(len(args)),
        out_specs=vmem(len(out_shape)) if several else vmem(1)[0],
        scratch_shapes=list(scratch),
        compiler_params=limit(mib),
        name=name,
    )(*args)


def route_kernel(ids_ref, ids_t_ref, weight_ref, send_ref, sum_ref):
    rows = ids_ref.shape[0]
    ids = ids_ref[...]
    ids_t = ids_t_ref[...]
    weights = weight_ref[...]
    across = lax.broadcasted_iota(jnp.int32, (rows, EXPERTS), 1)
    down = lax.broadcasted_iota(jnp.int32, (EXPERTS, rows), 0)
    named = jnp.zeros((rows, EXPERTS), F32)
    named_t = jnp.zeros((EXPERTS, rows), F32)
    weight = jnp.zeros((rows, EXPERTS), F32)
    for j in range(TOP):
        hit = ids[:, j : j + 1] == across
        named = named + jnp.where(hit, 1.0, 0.0)
        weight = weight + jnp.where(hit, weights[:, j : j + 1], 0.0)
        named_t = named_t + jnp.where(ids_t[j : j + 1, :] == down, 1.0, 0.0)
    i0 = lax.broadcasted_iota(jnp.int32, (rows, rows), 0)
    i1 = lax.broadcasted_iota(jnp.int32, (rows, rows), 1)
    before = dot(jnp.where(i1 < i0, 1.0, 0.0).astype(BF), named.astype(BF))
    before_t = dot(named_t.astype(BF), jnp.where(i0 < i1, 1.0, 0.0).astype(BF))
    slot = jnp.where(named > 0.5, before, 128.0)
    slot_t = jnp.where(named_t > 0.5, before_t, 128.0)
    def placed(slots, q):
        return jnp.where(slots < WIDE - 0.5, slots + float(WIDE * q), slots + float(WIDE * (QUART - 1) + REST * q))

    slot_all = jnp.concatenate([placed(slot, q) for q in range(QUART)], axis=0).astype(BF)
    slot_all_t = jnp.concatenate([placed(slot_t, q) for q in range(QUART)], axis=1).astype(BF)

    def split(shape, dim, other):
        index = lax.broadcasted_iota(jnp.int32, shape, dim).astype(F32)
        expert = jnp.floor((index + 0.5) * (1.0 / PACK))
        spread = jnp.where(expert == lax.broadcasted_iota(jnp.int32, shape, other).astype(F32), 1.0, 0.0)
        return spread.astype(BF), index - expert * PACK

    spread_t, place_t = split((COLS, EXPERTS), 0, 1)
    send_ref[...] = jnp.where(dot(spread_t, slot_all_t) == place_t[:, :1], 1.0, 0.0).astype(BF)
    spread, place = split((EXPERTS, COLS), 1, 0)
    match = dot(slot_all, spread) == place[:1, :]
    weight_all = dot(weight.astype(BF), spread)
    sum_ref[...] = jnp.where(match, jnp.concatenate([weight_all] * QUART, axis=0), 0.0).astype(BF)


def local_kernel(*refs):
    pieces, refs = refs[:10], refs[10:]
    wk_ref, wv_ref, gain_ref, normed_ref, k_ref, v_ref, state_ref, own_ref = refs
    y = lax.axis_index("y")
    c = lax.axis_index("c")
    rows, width = pieces[0].shape
    half = rows // 2
    blocks = []
    for part, core in ((pieces[:5], c), (pieces[5:], 1 - c)):
        for ref, away, lo, hi in (
            (part[0], 0, 0, rows),
            (part[1], 3, 0, rows),
            (part[2], 1, 0, rows),
            (part[3], 2, 0, half),
            (part[4], 2, half, rows),
        ):
            blocks.append((ref, ((y + away) & 3) * 2 + core, lo, hi))
    total = [jnp.zeros((half, 1), F32), jnp.zeros((half, 1), F32)]
    for ref, block, lo, hi in blocks:
        for h in range(lo // half, hi // half):
            values = ref[pl.ds(h * half - lo, half), :].astype(F32)
            total[h] = total[h] + jnp.sum(values * values, axis=1, keepdims=True)
    scale = [lax.rsqrt(t / (8 * width) + norm_eps) for t in total]
    mine = y * 2 + c
    own_rows = rows // 8
    for ref, block, lo, hi in blocks:
        gain = gain_ref[block]
        columns = pl.ds(pl.multiple_of(block * width, width), width)
        for h in range(lo // half, hi // half):
            values = ref[pl.ds(h * half - lo, half), :].astype(F32)
            normed_ref[pl.ds(h * half, half), columns] = (values * scale[h] * gain).astype(BF)
        if lo == 0 and hi == rows:
            own_ref[:, columns] = ref[pl.ds(pl.multiple_of(mine * own_rows, own_rows), own_rows), :]
        else:
            @pl.when((mine >= 4) == (lo > 0))
            def _():
                start = pl.multiple_of((mine & 3) * own_rows, own_rows)
                own_ref[:, columns] = ref[pl.ds(start, own_rows), :]
    normed = normed_ref[...]
    k = silu(dot(normed, wk_ref[...])).astype(BF)
    v = dot(normed, wv_ref[...]).astype(BF)
    k_ref[...] = k
    v_ref[...] = v
    sequence = lax.broadcasted_iota(jnp.int32, (rows, 128), 0) & 3
    for h in range(2):
        cols = slice(h * 128, (h + 1) * 128)
        keys = k[:, cols].astype(F32)
        apart = jnp.concatenate([jnp.where(sequence == b, keys, 0.0).astype(BF) for b in range(4)], axis=1)
        state_ref[h * rows : (h + 1) * rows, :] = dot(apart, v[:, cols], ((0,), (0,))).astype(BF)


def score_kernel(normed_ref, wq_ref, k_ref, v_ref, q_ref, local_ref):
    rows = normed_ref.shape[0]
    q = silu(dot(normed_ref[...], wq_ref[...])).astype(BF)
    q_ref[...] = q
    i0 = lax.broadcasted_iota(jnp.int32, (rows, rows), 0)
    i1 = lax.broadcasted_iota(jnp.int32, (rows, rows), 1)
    seen = (((i0 ^ i1) & 3) == 0) & (i1 <= i0)
    for h in range(2):
        cols = slice(h * 128, (h + 1) * 128)
        scores = jnp.where(seen, dot(q[:, cols], k_ref[:, cols], ((1,), (1,))), 0.0).astype(BF)
        local_ref[:, cols] = dot(scores, v_ref[:, cols])


def prefix_kernel(states_ref, before_ref):
    running = jnp.zeros(states_ref.shape[1:], F32)
    for i in range(states_ref.shape[0]):
        before_ref[i] = running.astype(BF)
        running = running + states_ref[i].astype(F32)


def mix_kernel(q_ref, local_ref, carried_ref, gain_ref, keep_ref, pass_ref):
    c = lax.axis_index("c")
    rows = q_ref.shape[0]
    own_rows = rows // 8
    sequence = lax.broadcasted_iota(jnp.int32, (rows, 128), 0) & 3
    for h in range(2):
        cols = slice(h * 128, (h + 1) * 128)
        q = q_ref[:, cols].astype(F32)
        apart = jnp.concatenate([jnp.where(sequence == b, q, 0.0).astype(BF) for b in range(4)], axis=1)
        mixed = local_ref[:, cols] + dot(apart, carried_ref[h * rows : (h + 1) * rows, :])
        mean = jnp.mean(mixed * mixed, axis=1, keepdims=True)
        attended = mixed * lax.rsqrt(mean + head_eps) * gain_ref[:, cols].astype(F32)
        for i in range(4):
            even = attended[2 * i * own_rows : (2 * i + 1) * own_rows]
            odd = attended[(2 * i + 1) * own_rows : (2 * i + 2) * own_rows]
            target = slice(i * own_rows, (i + 1) * own_rows)
            keep_ref[target, cols] = jnp.where(c == 0, even, odd).astype(BF)
            pass_ref[target, cols] = jnp.where(c == 0, odd, even).astype(BF)


def project_kernel(keep_ref, other_ref, own_weight_ref, other_weight_ref, out_ref):
    out_ref[...] = (dot(keep_ref[...], own_weight_ref[...]) + dot(other_ref[...], other_weight_ref[...])).astype(BF)


def dispatch_kernel(parts_ref, own_ref, gain_ref, send_table_ref, residual_ref, out_ref):
    rows, width = own_ref.shape
    residual = own_ref[...].astype(F32)
    for i in range(parts_ref.shape[0]):
        residual = residual + parts_ref[i].astype(F32)
    residual_ref[...] = residual
    mean = jnp.mean(residual * residual, axis=1, keepdims=True)
    entering = (residual * lax.rsqrt(mean + norm_eps) * gain_ref[...].astype(F32)).astype(BF)
    step = width // QUART
    stacked = jnp.concatenate([entering[:, q * step : (q + 1) * step] for q in range(QUART)], axis=0)
    out_ref[...] = dot(send_table_ref[...], stacked).astype(BF)


def expert_kernel(
    rows_ref, order_ref, back_ref, gate_hbm, up_hbm, down_hbm, gate_b_hbm, up_b_hbm, down_b_hbm, out_ref,
    x_ref, gate_ref, up_ref, down_ref, weight_sem,
):
    copies = [
        pltpu.make_async_copy(source, target.at[half], weight_sem.at[half, i])
        for half, given in enumerate(((gate_hbm, up_hbm, down_hbm), (gate_b_hbm, up_b_hbm, down_b_hbm)))
        for i, (source, target) in enumerate(zip(given, (gate_ref, up_ref, down_ref)))
    ]
    for copy in copies:
        copy.start()
    sources, _, step = rows_ref.shape
    head = sources * WIDE
    part = GROUP * REST
    wide = WIDE * QUART
    for q in range(QUART):
        for i in range(sources):
            x_ref[i * WIDE : (i + 1) * WIDE, q * step : (q + 1) * step] = rows_ref[i, q * WIDE : (q + 1) * WIDE, :]
    for g in range(sources // GROUP):
        rest = rows_ref[g * GROUP : (g + 1) * GROUP, wide:, :].reshape(GROUP * REST * QUART, step)
        rest = dot(order_ref[...], rest).astype(BF)
        for q in range(QUART):
            at = head + g * part
            x_ref[at : at + part, q * step : (q + 1) * step] = rest[q * part : (q + 1) * part]
    for first, lines in ((True, slice(0, head)), (False, slice(head, sources * CAP))):
        halves = []
        for half in range(2):
            if first:
                copies[3 * half].wait()
                copies[3 * half + 1].wait()
            gated = dot(x_ref[lines, :], gate_ref[half])
            active = (silu(gated) * dot(x_ref[lines, :], up_ref[half])).astype(BF)
            if first:
                copies[3 * half + 2].wait()
            halves.append(dot(active, down_ref[half]).astype(BF))
        x_ref[lines, :] = (halves[0].astype(F32) + halves[1].astype(F32)).astype(BF)
    for q in range(QUART):
        for i in range(sources):
            out_ref[i, q * WIDE : (q + 1) * WIDE, :] = x_ref[i * WIDE : (i + 1) * WIDE, q * step : (q + 1) * step]
    for g in range(sources // GROUP):
        at = head + g * part
        rest = jnp.concatenate([x_ref[at : at + part, q * step : (q + 1) * step] for q in range(QUART)], axis=0)
        rest = dot(back_ref[...], rest).astype(BF)
        out_ref[g * GROUP : (g + 1) * GROUP, wide:, :] = rest.reshape(GROUP, REST * QUART, step)


def combine_kernel(rows_ref, table_ref, residual_ref, out_ref):
    rows = residual_ref.shape[0]
    step = rows_ref.shape[1]
    total = dot(table_ref[...], rows_ref[...])
    for q in range(QUART):
        cols = slice(q * step, (q + 1) * step)
        out_ref[:, cols] = (residual_ref[:, cols] + total[q * rows : (q + 1) * rows]).astype(BF)


def sorting():
    size = GROUP * REST * QUART
    order = np.zeros((size, size), np.float32)
    for q in range(QUART):
        for s in range(GROUP):
            for r in range(REST):
                order[(q * GROUP + s) * REST + r, (s * QUART + q) * REST + r] = 1.0
    return order


def body(
    tokens, attn_gain, query_weight, key_weight, value_weight, head_gain, out_weight, moe_gain,
    route_ids, route_weight, expert_gate, expert_up, expert_down,
):
    shape = jax.ShapeDtypeStruct
    block_len, batch, width = tokens.shape
    rows = block_len * batch
    model = attn_gain.shape[0]
    own_rows = rows // 8
    hidden = expert_gate.shape[2]
    order = sorting()

    mine = tokens.reshape(rows, width)
    from_left = shifted(mine, "y", 1)
    from_right = shifted(mine, "y", -1)
    far_low = shifted(from_left[: rows // 2], "y", 1)
    far_high = shifted(from_right[rows // 2 :], "y", -1)
    pieces = [mine, from_left, from_right, far_low, far_high]
    pieces = pieces + [shifted(p, "c", 1) for p in pieces]

    other_out = shifted(out_weight, "c", 1)
    gate = expert_gate.reshape(model, hidden)
    up = expert_up.reshape(model, hidden)
    down = expert_down.reshape(hidden, model)
    other_gate = shifted(gate, "c", 1)
    other_up = shifted(up, "c", 1)
    other_down = shifted(down, "c", 1)

    ids = route_ids.reshape(own_rows, TOP)
    send_table, sum_table = call(
        route_kernel,
        "route",
        (shape((COLS, QUART * own_rows), BF), shape((QUART * own_rows, COLS), BF)),
        ids,
        ids.T,
        route_weight.reshape(own_rows, TOP),
    )

    normed, k, v, state, own = call(
        local_kernel,
        "local",
        (
            shape((rows, model), BF),
            shape((rows, width), BF),
            shape((rows, width), BF),
            pltpu.VMEM((2 * rows, 128), BF),
            shape((own_rows, model), BF),
        ),
        *[placed_inside(p) for p in pieces],
        key_weight,
        value_weight,
        attn_gain.astype(F32).reshape(8, 1, width),
    )
    q, local_mix = call(
        score_kernel,
        "score",
        (pltpu.HBM((rows, width), BF), pltpu.HBM((rows, width), F32)),
        normed,
        query_weight,
        k,
        v,
    )
    blocks = lax.axis_size(("x", "z"))
    states = placed_inside(exchanged(state.reshape(blocks, 2 * rows // blocks, 128), ("x", "z")))
    before = call(prefix_kernel, "prefix", pltpu.HBM(states.shape, BF), states)
    carried = placed_inside(exchanged(before, ("x", "z")).reshape(2 * rows, 128))
    keep, passed = call(
        mix_kernel,
        "mix",
        (shape((rows // 2, width), BF), pltpu.VMEM((rows // 2, width), BF)),
        q,
        local_mix,
        carried,
        head_gain.reshape(1, width),
    )
    other = shifted(passed, "c", 1)
    partial = call(
        project_kernel, "project", shape((rows // 2, model), BF), keep, placed_inside(other), out_weight, other_out
    )
    parts = exchanged(partial.reshape(4, own_rows, model), "y")
    step = model // QUART
    residual, sending = call(
        dispatch_kernel,
        "dispatch",
        (pltpu.HBM((own_rows, model), F32), pltpu.HBM((COLS, step), BF)),
        placed_inside(parts),
        own,
        moe_gain.reshape(1, model),
        send_table,
    )
    chips = ("x", "z", "y")
    received = placed_inside(exchanged(sending.reshape(EXPERTS, PACK, step), chips))
    inside, anywhere = vmem(1)[0], pl.BlockSpec(memory_space=pltpu.HBM)
    results = pl.pallas_call(
        expert_kernel,
        out_shape=pltpu.VMEM((EXPERTS, PACK, step), BF),
        in_specs=[inside] * 3 + [anywhere] * 6,
        out_specs=inside,
        scratch_shapes=[
            pltpu.VMEM((EXPERTS * CAP, model), BF),
            pltpu.VMEM((2, model, hidden), BF),
            pltpu.VMEM((2, model, hidden), BF),
            pltpu.VMEM((2, hidden, model), BF),
            pltpu.SemaphoreType.DMA((2, 3)),
        ],
        compiler_params=limit(36),
        name="experts",
    )(received, jnp.asarray(order, BF), jnp.asarray(order.T, BF), *[outside(w) for w in (gate, up, down, other_gate, other_up, other_down)])
    returned = placed_inside(exchanged(results, chips).reshape(COLS, step))
    out = call(
        combine_kernel, "combine", shape((own_rows, model), BF), returned, sum_table, residual
    )
    return out.reshape(own_rows // batch, batch, model)


def solution(mesh):
    fine = Mesh(mesh.devices.reshape(4, 4, 4, 2), ("x", "z", "y", "c"))
    seq, head, every = ("x", "z"), ("y", "c"), ("x", "z", "y", "c")
    in_specs = (
        P(seq, None, head),
        P(),
        P(None, head),
        P(None, head),
        P(None, head),
        P(head),
        P(head, None),
        P(),
        P(every, None, None),
        P(every, None, None),
        P(every, None, None),
        P(every, None, None),
        P(every, None, None),
    )
    return jax.shard_map(body, mesh=fine, in_specs=in_specs, out_specs=P(every, None, None), check_vma=False)
```

```python
import jax
import jax.numpy as jnp
import numpy as np
from jax import lax
from jax.experimental import pallas as pl
from jax.experimental.pallas import tpu as pltpu
from jax.sharding import Mesh, PartitionSpec as P


EXPERTS = 64
TOP = 8
CAP = 12
QUART = 4
PACK = CAP * QUART
COLS = EXPERTS * PACK
WIDE = 8
REST = CAP - WIDE
GROUP = 16

norm_eps = 1e-05
head_eps = 1e-06

BF = jnp.bfloat16
F32 = jnp.float32


def shifted(x, axis, by):
    count = lax.axis_size(axis)
    return lax.ppermute(x, axis, [(i, (i + by) % count) for i in range(count)])


def exchanged(x, axes):
    return lax.all_to_all(x, axes, split_axis=0, concat_axis=0, tiled=True)


def dot(a, b, dims=((1,), (0,))):
    return lax.dot_general(a, b, (dims, ((), ())), preferred_element_type=F32)


def silu(v):
    return v / (1.0 + jnp.exp(-v))


def vmem(count):
    return [pl.BlockSpec(memory_space=pltpu.VMEM)] * count


class Inside:
    def __init__(self, x):
        self.x = x


def placed_inside(x):
    return Inside(pltpu.with_memory_space_constraint(x, pltpu.VMEM))


def outside(x):
    return pltpu.with_memory_space_constraint(x, pltpu.HBM)


def limit(mib):
    return pltpu.CompilerParams(vmem_limit_bytes=mib * 2**20)


def call(kernel, out_shape, *args, scratch=(), mib=24):
    several = isinstance(out_shape, (list, tuple))
    args = [x.x if isinstance(x, Inside) else outside(x) for x in args]
    return pl.pallas_call(
        kernel,
        out_shape=out_shape,
        in_specs=vmem(len(args)),
        out_specs=vmem(len(out_shape)) if several else vmem(1)[0],
        scratch_shapes=list(scratch),
        compiler_params=limit(mib),
    )(*args)


def route_kernel(ids_ref, ids_t_ref, weight_ref, send_ref, sum_ref):
    rows = ids_ref.shape[0]
    ids = ids_ref[...]
    ids_t = ids_t_ref[...]
    weights = weight_ref[...]
    across = lax.broadcasted_iota(jnp.int32, (rows, EXPERTS), 1)
    down = lax.broadcasted_iota(jnp.int32, (EXPERTS, rows), 0)
    named = jnp.zeros((rows, EXPERTS), F32)
    named_t = jnp.zeros((EXPERTS, rows), F32)
    weight = jnp.zeros((rows, EXPERTS), F32)
    for j in range(TOP):
        hit = ids[:, j : j + 1] == across
        named = named + jnp.where(hit, 1.0, 0.0)
        weight = weight + jnp.where(hit, weights[:, j : j + 1], 0.0)
        named_t = named_t + jnp.where(ids_t[j : j + 1, :] == down, 1.0, 0.0)
    i0 = lax.broadcasted_iota(jnp.int32, (rows, rows), 0)
    i1 = lax.broadcasted_iota(jnp.int32, (rows, rows), 1)
    before = dot(jnp.where(i1 < i0, 1.0, 0.0).astype(BF), named.astype(BF))
    before_t = dot(named_t.astype(BF), jnp.where(i0 < i1, 1.0, 0.0).astype(BF))
    slot = jnp.where(named > 0.5, before, 128.0)
    slot_t = jnp.where(named_t > 0.5, before_t, 128.0)

    def placed(slots, q):
        return jnp.where(slots < WIDE - 0.5, slots + float(WIDE * q), slots + float(WIDE * (QUART - 1) + REST * q))

    slot_all = jnp.concatenate([placed(slot, q) for q in range(QUART)], axis=0).astype(BF)
    slot_all_t = jnp.concatenate([placed(slot_t, q) for q in range(QUART)], axis=1).astype(BF)

    def split(shape, dim, other):
        index = lax.broadcasted_iota(jnp.int32, shape, dim).astype(F32)
        expert = jnp.floor((index + 0.5) * (1.0 / PACK))
        spread = jnp.where(expert == lax.broadcasted_iota(jnp.int32, shape, other).astype(F32), 1.0, 0.0)
        return spread.astype(BF), index - expert * PACK

    spread_t, place_t = split((COLS, EXPERTS), 0, 1)
    send_ref[...] = jnp.where(dot(spread_t, slot_all_t) == place_t[:, :1], 1.0, 0.0).astype(BF)
    spread, place = split((EXPERTS, COLS), 1, 0)
    match = dot(slot_all, spread) == place[:1, :]
    weight_all = dot(weight.astype(BF), spread)
    sum_ref[...] = jnp.where(match, jnp.concatenate([weight_all] * QUART, axis=0), 0.0).astype(BF)


def local_kernel(*refs):
    pieces, refs = refs[:10], refs[10:]
    wk_ref, wv_ref, gain_ref, normed_ref, k_ref, v_ref, state_ref, own_ref = refs
    y = lax.axis_index("y")
    c = lax.axis_index("c")
    rows, width = pieces[0].shape
    half = rows // 2
    blocks = []
    for part, core in ((pieces[:5], c), (pieces[5:], 1 - c)):
        for ref, away, lo, hi in (
            (part[0], 0, 0, rows),
            (part[1], 3, 0, rows),
            (part[2], 1, 0, rows),
            (part[3], 2, 0, half),
            (part[4], 2, half, rows),
        ):
            blocks.append((ref, ((y + away) & 3) * 2 + core, lo, hi))
    total = [jnp.zeros((half, 1), F32), jnp.zeros((half, 1), F32)]
    for ref, block, lo, hi in blocks:
        for h in range(lo // half, hi // half):
            values = ref[pl.ds(h * half - lo, half), :].astype(F32)
            total[h] = total[h] + jnp.sum(values * values, axis=1, keepdims=True)
    scale = [lax.rsqrt(t / (8 * width) + norm_eps) for t in total]
    mine = y * 2 + c
    own_rows = rows // 8
    for ref, block, lo, hi in blocks:
        gain = gain_ref[block]
        columns = pl.ds(pl.multiple_of(block * width, width), width)
        for h in range(lo // half, hi // half):
            values = ref[pl.ds(h * half - lo, half), :].astype(F32)
            normed_ref[pl.ds(h * half, half), columns] = (values * scale[h] * gain).astype(BF)
        if lo == 0 and hi == rows:
            own_ref[:, columns] = ref[pl.ds(pl.multiple_of(mine * own_rows, own_rows), own_rows), :]
        else:
            @pl.when((mine >= 4) == (lo > 0))
            def _():
                start = pl.multiple_of((mine & 3) * own_rows, own_rows)
                own_ref[:, columns] = ref[pl.ds(start, own_rows), :]
    normed = normed_ref[...]
    k = silu(dot(normed, wk_ref[...])).astype(BF)
    v = dot(normed, wv_ref[...]).astype(BF)
    k_ref[...] = k
    v_ref[...] = v
    sequence = lax.broadcasted_iota(jnp.int32, (rows, 128), 0) & 3
    for h in range(2):
        cols = slice(h * 128, (h + 1) * 128)
        keys = k[:, cols].astype(F32)
        apart = jnp.concatenate([jnp.where(sequence == b, keys, 0.0).astype(BF) for b in range(4)], axis=1)
        state_ref[h * rows : (h + 1) * rows, :] = dot(apart, v[:, cols], ((0,), (0,))).astype(BF)


def score_kernel(normed_ref, wq_ref, k_ref, v_ref, q_ref, local_ref):
    rows = normed_ref.shape[0]
    q = silu(dot(normed_ref[...], wq_ref[...])).astype(BF)
    q_ref[...] = q
    i0 = lax.broadcasted_iota(jnp.int32, (rows, rows), 0)
    i1 = lax.broadcasted_iota(jnp.int32, (rows, rows), 1)
    seen = (((i0 ^ i1) & 3) == 0) & (i1 <= i0)
    for h in range(2):
        cols = slice(h * 128, (h + 1) * 128)
        scores = jnp.where(seen, dot(q[:, cols], k_ref[:, cols], ((1,), (1,))), 0.0).astype(BF)
        local_ref[:, cols] = dot(scores, v_ref[:, cols])


def prefix_kernel(states_ref, before_ref):
    running = jnp.zeros(states_ref.shape[1:], F32)
    for i in range(states_ref.shape[0]):
        before_ref[i] = running.astype(BF)
        running = running + states_ref[i].astype(F32)


def mix_kernel(q_ref, local_ref, carried_ref, gain_ref, out_ref):
    rows = q_ref.shape[0]
    sequence = lax.broadcasted_iota(jnp.int32, (rows, 128), 0) & 3
    for h in range(2):
        cols = slice(h * 128, (h + 1) * 128)
        q = q_ref[:, cols].astype(F32)
        apart = jnp.concatenate([jnp.where(sequence == b, q, 0.0).astype(BF) for b in range(4)], axis=1)
        mixed = local_ref[:, cols] + dot(apart, carried_ref[h * rows : (h + 1) * rows, :])
        mean = jnp.mean(mixed * mixed, axis=1, keepdims=True)
        out_ref[:, cols] = (mixed * lax.rsqrt(mean + head_eps) * gain_ref[:, cols].astype(F32)).astype(BF)


def dispatch_kernel(*refs):
    weights, refs = refs[:10], refs[10:]
    attended_ref, own_ref, gain_ref, send_table_ref, residual_ref, out_ref = refs
    y = lax.axis_index("y")
    c = lax.axis_index("c")
    _, width = own_ref.shape
    residual = own_ref[...].astype(F32)
    for part, core in ((weights[:5], c), (weights[5:], 1 - c)):
        for ref, away in ((part[0], 0), (part[1], 3), (part[2], 1)):
            attended = attended_ref[((y + away) & 3) * 2 + core]
            residual = residual + dot(attended, ref[...]).astype(BF).astype(F32)
        attended = attended_ref[((y + 2) & 3) * 2 + core]
        half = part[3].shape[0]
        term = dot(attended[:, :half], part[3][...]) + dot(attended[:, half:], part[4][...])
        residual = residual + term.astype(BF).astype(F32)
    residual_ref[...] = residual
    mean = jnp.mean(residual * residual, axis=1, keepdims=True)
    entering = (residual * lax.rsqrt(mean + norm_eps) * gain_ref[...].astype(F32)).astype(BF)
    step = width // QUART
    stacked = jnp.concatenate([entering[:, q * step : (q + 1) * step] for q in range(QUART)], axis=0)
    out_ref[...] = dot(send_table_ref[...], stacked).astype(BF)


def expert_kernel(
    rows_ref, order_ref, back_ref, gate_hbm, up_hbm, down_hbm, gate_b_hbm, up_b_hbm, down_b_hbm, out_ref,
    x_ref, gate_ref, up_ref, down_ref, weight_sem,
):
    copies = [
        pltpu.make_async_copy(source, target.at[half], weight_sem.at[half, i])
        for half, given in enumerate(((gate_hbm, up_hbm, down_hbm), (gate_b_hbm, up_b_hbm, down_b_hbm)))
        for i, (source, target) in enumerate(zip(given, (gate_ref, up_ref, down_ref)))
    ]
    for copy in copies:
        copy.start()
    sources, _, step = rows_ref.shape
    head = sources * WIDE
    part = GROUP * REST
    wide = WIDE * QUART
    for q in range(QUART):
        for i in range(sources):
            x_ref[i * WIDE : (i + 1) * WIDE, q * step : (q + 1) * step] = rows_ref[i, q * WIDE : (q + 1) * WIDE, :]
    for g in range(sources // GROUP):
        rest = rows_ref[g * GROUP : (g + 1) * GROUP, wide:, :].reshape(GROUP * REST * QUART, step)
        rest = dot(order_ref[...], rest).astype(BF)
        for q in range(QUART):
            at = head + g * part
            x_ref[at : at + part, q * step : (q + 1) * step] = rest[q * part : (q + 1) * part]
    for first, lines in ((True, slice(0, head)), (False, slice(head, sources * CAP))):
        halves = []
        for half in range(2):
            if first:
                copies[3 * half].wait()
                copies[3 * half + 1].wait()
            gated = dot(x_ref[lines, :], gate_ref[half])
            active = (silu(gated) * dot(x_ref[lines, :], up_ref[half])).astype(BF)
            if first:
                copies[3 * half + 2].wait()
            halves.append(dot(active, down_ref[half]).astype(BF))
        x_ref[lines, :] = (halves[0].astype(F32) + halves[1].astype(F32)).astype(BF)
    for q in range(QUART):
        for i in range(sources):
            out_ref[i, q * WIDE : (q + 1) * WIDE, :] = x_ref[i * WIDE : (i + 1) * WIDE, q * step : (q + 1) * step]
    for g in range(sources // GROUP):
        at = head + g * part
        rest = jnp.concatenate([x_ref[at : at + part, q * step : (q + 1) * step] for q in range(QUART)], axis=0)
        rest = dot(back_ref[...], rest).astype(BF)
        out_ref[g * GROUP : (g + 1) * GROUP, wide:, :] = rest.reshape(GROUP, REST * QUART, step)


def combine_kernel(rows_ref, table_ref, residual_ref, out_ref):
    rows = residual_ref.shape[0]
    step = rows_ref.shape[1]
    total = dot(table_ref[...], rows_ref[...])
    for q in range(QUART):
        cols = slice(q * step, (q + 1) * step)
        out_ref[:, cols] = (residual_ref[:, cols] + total[q * rows : (q + 1) * rows]).astype(BF)


def sorting():
    size = GROUP * REST * QUART
    order = np.zeros((size, size), np.float32)
    for q in range(QUART):
        for s in range(GROUP):
            for r in range(REST):
                order[(q * GROUP + s) * REST + r, (s * QUART + q) * REST + r] = 1.0
    return order


def body(
    tokens, attn_gain, query_weight, key_weight, value_weight, head_gain, out_weight, moe_gain,
    route_ids, route_weight, expert_gate, expert_up, expert_down,
):
    shape = jax.ShapeDtypeStruct
    block_len, batch, width = tokens.shape
    rows = block_len * batch
    model = attn_gain.shape[0]
    own_rows = rows // 8
    hidden = expert_gate.shape[2]
    order = sorting()

    mine = tokens.reshape(rows, width)
    from_left = shifted(mine, "y", 1)
    from_right = shifted(mine, "y", -1)
    far_low = shifted(from_left[: rows // 2], "y", 1)
    far_high = shifted(from_right[rows // 2 :], "y", -1)
    pieces = [mine, from_left, from_right, far_low, far_high]
    pieces = pieces + [shifted(p, "c", 1) for p in pieces]

    later_out, *pieces[5:] = lax.optimization_barrier((out_weight, *pieces[5:]))
    out_left = shifted(later_out, "y", 1)
    out_right = shifted(later_out, "y", -1)
    out_half = out_weight.shape[0] // 2
    out_low = shifted(out_left[:out_half], "y", 1)
    out_high = shifted(out_right[out_half:], "y", -1)
    projections = [out_weight, out_left, out_right, out_low, out_high]
    projections = projections + [shifted(p, "c", 1) for p in projections[:3]]
    projections = projections + [shifted(p, "c", 1) for p in projections[3:5]]
    gate = expert_gate.reshape(model, hidden)
    up = expert_up.reshape(model, hidden)
    down = expert_down.reshape(hidden, model)
    other_gate = shifted(gate, "c", 1)
    other_up = shifted(up, "c", 1)
    other_down = shifted(down, "c", 1)

    ids = route_ids.reshape(own_rows, TOP)
    send_table, sum_table = call(
        route_kernel,
        (pltpu.HBM((COLS, QUART * own_rows), BF), pltpu.HBM((QUART * own_rows, COLS), BF)),
        ids,
        ids.T,
        route_weight.reshape(own_rows, TOP),
    )

    normed, k, v, state, own = call(
        local_kernel,
        (
            pltpu.HBM((rows, model), BF),
            pltpu.HBM((rows, width), BF),
            pltpu.HBM((rows, width), BF),
            pltpu.VMEM((2 * rows, 128), BF),
            pltpu.HBM((own_rows, model), BF),
        ),
        *[placed_inside(p) for p in pieces],
        key_weight,
        value_weight,
        attn_gain.astype(F32).reshape(8, 1, width),
    )
    q, local_mix = call(
        score_kernel, (pltpu.HBM((rows, width), BF), pltpu.HBM((rows, width), F32)), normed, query_weight, k, v
    )
    blocks = lax.axis_size(("x", "z"))
    states = placed_inside(exchanged(state.reshape(blocks, 2 * rows // blocks, 128), ("x", "z")))
    before = call(prefix_kernel, pltpu.HBM(states.x.shape, BF), states)
    carried = placed_inside(exchanged(before, ("x", "z")).reshape(2 * rows, 128))
    attended = call(mix_kernel, pltpu.VMEM((rows, width), BF), q, local_mix, carried, head_gain.reshape(1, width))
    attended = placed_inside(exchanged(attended.reshape(8, own_rows, width), ("y", "c")))
    step = model // QUART
    residual, sending = call(
        dispatch_kernel,
        (pltpu.HBM((own_rows, model), F32), pltpu.HBM((COLS, step), BF)),
        *projections,
        attended,
        own,
        moe_gain.reshape(1, model),
        send_table,
    )
    chips = ("x", "z", "y")
    received = placed_inside(exchanged(sending.reshape(EXPERTS, PACK, step), chips))
    inside, anywhere = vmem(1)[0], pl.BlockSpec(memory_space=pltpu.HBM)
    results = pl.pallas_call(
        expert_kernel,
        out_shape=pltpu.VMEM((EXPERTS, PACK, step), BF),
        in_specs=[inside] * 3 + [anywhere] * 6,
        out_specs=inside,
        scratch_shapes=[
            pltpu.VMEM((EXPERTS * CAP, model), BF),
            pltpu.VMEM((2, model, hidden), BF),
            pltpu.VMEM((2, model, hidden), BF),
            pltpu.VMEM((2, hidden, model), BF),
            pltpu.SemaphoreType.DMA((2, 3)),
        ],
        compiler_params=limit(36),
        name="experts",
    )(received.x, jnp.asarray(order, BF), jnp.asarray(order.T, BF), *[outside(w) for w in (gate, up, down, other_gate, other_up, other_down)])
    returned = placed_inside(exchanged(results, chips).reshape(COLS, step))
    out = call(combine_kernel, shape((own_rows, model), BF), returned, sum_table, residual)
    return out.reshape(own_rows // batch, batch, model)


def solution(mesh):
    fine = Mesh(mesh.devices.reshape(4, 4, 4, 2), ("x", "z", "y", "c"))
    seq, head, every = ("x", "z"), ("y", "c"), ("x", "z", "y", "c")
    in_specs = (
        P(seq, None, head),
        P(),
        P(None, head),
        P(None, head),
        P(None, head),
        P(head),
        P(head, None),
        P(),
        P(every, None, None),
        P(every, None, None),
        P(every, None, None),
        P(every, None, None),
        P(every, None, None),
    )

    return jax.shard_map(body, mesh=fine, in_specs=in_specs, out_specs=P(every, None, None), check_vma=False)
```

```python
import jax
import jax.numpy as jnp
import numpy as np
from jax import lax
from jax.experimental import pallas as pl
from jax.experimental.pallas import tpu as pltpu
from jax.sharding import Mesh, PartitionSpec as P


EXPERTS = 64
TOP = 8
CAP = 12
QUART = 4
PACK = CAP * QUART
COLS = EXPERTS * PACK
WIDE = 8
REST = CAP - WIDE
GROUP = 16
STEPS = 4

norm_eps = 1e-05
head_eps = 1e-06

BF = jnp.bfloat16
F32 = jnp.float32


def shifted(x, axis, by):
    count = lax.axis_size(axis)
    return lax.ppermute(x, axis, [(i, (i + by) % count) for i in range(count)])


def swirled(x, by):
    ways = lax.axis_size("y")
    pairs = [(2 * y + c, 2 * ((y + (by if c == 0 else -by)) % ways) + c) for y in range(ways) for c in range(2)]
    return lax.ppermute(x, ("y", "c"), pairs)


def exchanged(x, axes):
    return lax.all_to_all(x, axes, split_axis=0, concat_axis=0, tiled=True)


def dot(a, b, dims=((1,), (0,))):
    return lax.dot_general(a, b, (dims, ((), ())), preferred_element_type=F32)


def silu(v):
    return v / (1.0 + jnp.exp(-v))


INSIDE = pl.BlockSpec(memory_space=pltpu.VMEM)
OUTSIDE = pl.BlockSpec(memory_space=pltpu.HBM)


class Placed:
    def __init__(self, x, spec, fixed):
        self.x = x if fixed is None else pltpu.with_memory_space_constraint(x, fixed)
        self.spec = spec


def inside(x):
    return Placed(x, INSIDE, pltpu.VMEM)


def outside(x):
    return Placed(x, OUTSIDE, pltpu.HBM)


def loaded(x):
    return Placed(x, INSIDE, pltpu.HBM)


def either(x):
    return Placed(x, INSIDE, None)


def call(kernel, out_shape, *args, out_specs=INSIDE, scratch=(), mib=24):
    args = [x if isinstance(x, Placed) else loaded(x) for x in args]
    if isinstance(out_shape, (list, tuple)) and not isinstance(out_specs, (list, tuple)):
        out_specs = [out_specs] * len(out_shape)
    return pl.pallas_call(
        kernel,
        out_shape=out_shape,
        in_specs=[x.spec for x in args],
        out_specs=out_specs,
        scratch_shapes=list(scratch),
        compiler_params=pltpu.CompilerParams(vmem_limit_bytes=mib * 2**20),
    )(*[x.x for x in args])


def route_kernel(ids_ref, ids_t_ref, weight_ref, send_ref, sum_ref):
    rows = ids_ref.shape[0]
    ids = ids_ref[...]
    ids_t = ids_t_ref[...]
    weights = weight_ref[...]
    across = lax.broadcasted_iota(jnp.int32, (rows, EXPERTS), 1)
    down = lax.broadcasted_iota(jnp.int32, (EXPERTS, rows), 0)
    named = jnp.zeros((rows, EXPERTS), F32)
    named_t = jnp.zeros((EXPERTS, rows), F32)
    weight = jnp.zeros((rows, EXPERTS), F32)
    for j in range(TOP):
        hit = ids[:, j : j + 1] == across
        named = named + jnp.where(hit, 1.0, 0.0)
        weight = weight + jnp.where(hit, weights[:, j : j + 1], 0.0)
        named_t = named_t + jnp.where(ids_t[j : j + 1, :] == down, 1.0, 0.0)
    i0 = lax.broadcasted_iota(jnp.int32, (rows, rows), 0)
    i1 = lax.broadcasted_iota(jnp.int32, (rows, rows), 1)
    before = dot(jnp.where(i1 < i0, 1.0, 0.0).astype(BF), named.astype(BF))
    before_t = dot(named_t.astype(BF), jnp.where(i0 < i1, 1.0, 0.0).astype(BF))
    slot = jnp.where(named > 0.5, before, 128.0)
    slot_t = jnp.where(named_t > 0.5, before_t, 128.0)

    def placed(slots, q):
        return jnp.where(slots < WIDE - 0.5, slots + float(WIDE * q), slots + float(WIDE * (QUART - 1) + REST * q))

    slot_all = jnp.concatenate([placed(slot, q) for q in range(QUART)], axis=0).astype(BF)
    slot_all_t = jnp.concatenate([placed(slot_t, q) for q in range(QUART)], axis=1).astype(BF)

    def split(shape, dim, other):
        index = lax.broadcasted_iota(jnp.int32, shape, dim).astype(F32)
        expert = jnp.floor((index + 0.5) * (1.0 / PACK))
        spread = jnp.where(expert == lax.broadcasted_iota(jnp.int32, shape, other).astype(F32), 1.0, 0.0)
        return spread.astype(BF), index - expert * PACK

    spread_t, place_t = split((COLS, EXPERTS), 0, 1)
    send_ref[...] = jnp.where(dot(spread_t, slot_all_t) == place_t[:, :1], 1.0, 0.0).astype(BF)
    spread, place = split((EXPERTS, COLS), 1, 0)
    match = dot(slot_all, spread) == place[:1, :]
    weight_all = dot(weight.astype(BF), spread)
    sum_ref[...] = jnp.where(match, jnp.concatenate([weight_all] * QUART, axis=0), 0.0).astype(BF)


def copied(source, target, sem):
    copy = pltpu.make_async_copy(source, target, sem)
    copy.start()
    return copy


def block_order():
    y = lax.axis_index("y")
    c = lax.axis_index("c")
    return [((y + away) & 3) * 2 + core for core in (c, 1 - c) for away in (0, 3 - 2 * core, 1 + 2 * core, 2)]


def local_kernel(*refs):
    pieces, refs = refs[:8], refs[8:]
    wk_hbm, wv_hbm, gain_ref, normed_hbm, k_hbm, v_hbm, state_ref, own_ref, refs = *refs[:8], refs[8:]
    normed_ref, k_ref, v_ref, wk_ref, wv_ref, in_sem, out_sem = refs
    weight_copies = [copied(wk_hbm, wk_ref, in_sem.at[0]), copied(wv_hbm, wv_ref, in_sem.at[1])]
    rows, width = pieces[0].shape
    blocks = block_order()
    total = jnp.zeros((rows, 1), F32)
    for ref in pieces:
        values = ref[...].astype(F32)
        total = total + jnp.sum(values * values, axis=1, keepdims=True)
    scale = lax.rsqrt(total / (8 * width) + norm_eps)
    own_rows = rows // 8
    start = pl.multiple_of((lax.axis_index("y") * 2 + lax.axis_index("c")) * own_rows, own_rows)
    for ref, block in zip(pieces, blocks):
        columns = pl.ds(pl.multiple_of(block * width, width), width)
        normed_ref[:, columns] = (ref[...].astype(F32) * scale * gain_ref[block]).astype(BF)
        own_ref[:, columns] = ref[pl.ds(start, own_rows), :]
    out_copies = [copied(normed_ref, normed_hbm, out_sem.at[0])]
    weight_copies[0].wait()
    k_ref[...] = silu(dot(normed_ref[...], wk_ref[...])).astype(BF)
    out_copies.append(copied(k_ref, k_hbm, out_sem.at[1]))
    weight_copies[1].wait()
    v_ref[...] = dot(normed_ref[...], wv_ref[...]).astype(BF)
    out_copies.append(copied(v_ref, v_hbm, out_sem.at[2]))
    sequence = lax.broadcasted_iota(jnp.int32, (rows, 128), 0) & 3
    for h in range(2):
        cols = slice(h * 128, (h + 1) * 128)
        keys = k_ref[:, cols].astype(F32)
        apart = jnp.concatenate([jnp.where(sequence == b, keys, 0.0).astype(BF) for b in range(4)], axis=1)
        state_ref[h * rows : (h + 1) * rows, :] = dot(apart, v_ref[:, cols], ((0,), (0,))).astype(BF)
    for copy in out_copies:
        copy.wait()


def score_kernel(normed_ref, wq_ref, k_ref, v_ref, q_ref, local_ref):
    rows = normed_ref.shape[0]
    q = silu(dot(normed_ref[...], wq_ref[...])).astype(BF)
    q_ref[...] = q
    i0 = lax.broadcasted_iota(jnp.int32, (rows, rows), 0)
    i1 = lax.broadcasted_iota(jnp.int32, (rows, rows), 1)
    seen = (((i0 ^ i1) & 3) == 0) & (i1 <= i0)
    for h in range(2):
        cols = slice(h * 128, (h + 1) * 128)
        scores = jnp.where(seen, dot(q[:, cols], k_ref[:, cols], ((1,), (1,))), 0.0).astype(BF)
        local_ref[:, cols] = dot(scores, v_ref[:, cols])


def prefix_kernel(states_ref, before_ref):
    running = jnp.zeros(states_ref.shape[1:], F32)
    for i in range(states_ref.shape[0]):
        before_ref[i] = running.astype(BF)
        running = running + states_ref[i].astype(F32)


def mix_kernel(q_ref, local_ref, carried_ref, gain_ref, out_ref):
    rows = q_ref.shape[0]
    sequence = lax.broadcasted_iota(jnp.int32, (rows, 128), 0) & 3
    for h in range(2):
        cols = slice(h * 128, (h + 1) * 128)
        q = q_ref[:, cols].astype(F32)
        apart = jnp.concatenate([jnp.where(sequence == b, q, 0.0).astype(BF) for b in range(4)], axis=1)
        mixed = local_ref[:, cols] + dot(apart, carried_ref[h * rows : (h + 1) * rows, :])
        mean = jnp.mean(mixed * mixed, axis=1, keepdims=True)
        out_ref[:, cols] = (mixed * lax.rsqrt(mean + head_eps) * gain_ref[:, cols].astype(F32)).astype(BF)


def dispatch_kernel(*refs):
    weights, refs = refs[:8], refs[8:]
    attended_ref, own_ref, gain_ref, table_hbm, residual_ref, out_hbm, refs = *refs[:6], refs[6:]
    weight_ref, table_ref, out_ref, weight_sem, table_sem, out_sem = refs
    copies = [copied(source, weight_ref.at[i], weight_sem.at[i]) for i, source in enumerate(weights)]
    table_copy = copied(table_hbm, table_ref, table_sem)
    _, width = own_ref.shape
    residual = own_ref[...].astype(F32)
    for i, block in enumerate(block_order()):
        copies[i].wait()
        residual = residual + dot(attended_ref[block], weight_ref[i]).astype(BF).astype(F32)
    residual_ref[...] = residual
    mean = jnp.mean(residual * residual, axis=1, keepdims=True)
    entering = (residual * lax.rsqrt(mean + norm_eps) * gain_ref[...].astype(F32)).astype(BF)
    step = width // QUART
    stacked = jnp.concatenate([entering[:, q * step : (q + 1) * step] for q in range(QUART)], axis=0)
    table_copy.wait()
    size = COLS // STEPS
    copies = []
    for i in range(STEPS):
        lines = pl.ds(i * size, size)
        out_ref[lines, :] = dot(table_ref[lines, :], stacked).astype(BF)
        copies.append(copied(out_ref.at[lines], out_hbm.at[lines], out_sem.at[i]))
    for copy in copies:
        copy.wait()


def expert_kernel(
    rows_ref, order_ref, back_ref, gate_hbm, up_hbm, down_hbm, gate_b_hbm, up_b_hbm, down_b_hbm, out_ref,
    x_ref, gate_ref, up_ref, down_ref, weight_sem,
):
    copies = [
        pltpu.make_async_copy(source, target.at[half], weight_sem.at[half, i])
        for half, given in enumerate(((gate_hbm, up_hbm, down_hbm), (gate_b_hbm, up_b_hbm, down_b_hbm)))
        for i, (source, target) in enumerate(zip(given, (gate_ref, up_ref, down_ref)))
    ]
    for copy in copies:
        copy.start()
    sources, _, step = rows_ref.shape
    head = sources * WIDE
    part = GROUP * REST
    wide = WIDE * QUART
    for q in range(QUART):
        for i in range(sources):
            x_ref[i * WIDE : (i + 1) * WIDE, q * step : (q + 1) * step] = rows_ref[i, q * WIDE : (q + 1) * WIDE, :]
    for g in range(sources // GROUP):
        rest = rows_ref[g * GROUP : (g + 1) * GROUP, wide:, :].reshape(GROUP * REST * QUART, step)
        rest = dot(order_ref[...], rest).astype(BF)
        for q in range(QUART):
            at = head + g * part
            x_ref[at : at + part, q * step : (q + 1) * step] = rest[q * part : (q + 1) * part]
    for first, lines in ((True, slice(0, head)), (False, slice(head, sources * CAP))):
        halves = []
        for half in range(2):
            if first:
                copies[3 * half].wait()
                copies[3 * half + 1].wait()
            gated = dot(x_ref[lines, :], gate_ref[half])
            active = (silu(gated) * dot(x_ref[lines, :], up_ref[half])).astype(BF)
            if first:
                copies[3 * half + 2].wait()
            halves.append(dot(active, down_ref[half]).astype(BF))
        x_ref[lines, :] = (halves[0].astype(F32) + halves[1].astype(F32)).astype(BF)
    for q in range(QUART):
        for i in range(sources):
            out_ref[i, q * WIDE : (q + 1) * WIDE, :] = x_ref[i * WIDE : (i + 1) * WIDE, q * step : (q + 1) * step]
    for g in range(sources // GROUP):
        at = head + g * part
        rest = jnp.concatenate([x_ref[at : at + part, q * step : (q + 1) * step] for q in range(QUART)], axis=0)
        rest = dot(back_ref[...], rest).astype(BF)
        out_ref[g * GROUP : (g + 1) * GROUP, wide:, :] = rest.reshape(GROUP, REST * QUART, step)


def combine_kernel(rows_ref, table_ref, residual_ref, out_ref):
    rows = residual_ref.shape[0]
    step = rows_ref.shape[1]
    total = dot(table_ref[...], rows_ref[...])
    for q in range(QUART):
        cols = slice(q * step, (q + 1) * step)
        out_ref[:, cols] = (residual_ref[:, cols] + total[q * rows : (q + 1) * rows]).astype(BF)


def sorting():
    size = GROUP * REST * QUART
    order = np.zeros((size, size), np.float32)
    for q in range(QUART):
        for s in range(GROUP):
            for r in range(REST):
                order[(q * GROUP + s) * REST + r, (s * QUART + q) * REST + r] = 1.0
    return order


def body(
    tokens, attn_gain, query_weight, key_weight, value_weight, head_gain, out_weight, moe_gain,
    route_ids, route_weight, expert_gate, expert_up, expert_down,
):
    shape = jax.ShapeDtypeStruct
    block_len, batch, width = tokens.shape
    rows = block_len * batch
    model = attn_gain.shape[0]
    own_rows = rows // 8
    hidden = expert_gate.shape[2]
    order = sorting()

    attn_rows = attn_gain.astype(F32).reshape(8, 1, width)
    head_row = head_gain.reshape(1, width)
    moe_row = moe_gain.reshape(1, model)
    mine = tokens.reshape(rows, width)
    first = swirled(mine, 1)
    second = swirled(mine, -1)
    far = swirled(first, 1)
    pieces = [mine, first, second, far]
    pieces = pieces + [shifted(p, "c", 1) for p in pieces]

    later_out, *pieces[4:] = lax.optimization_barrier((out_weight, *pieces[4:]))
    out_first = swirled(later_out, 1)
    out_second = swirled(later_out, -1)
    out_far = swirled(out_first, 1)
    projections = [out_weight, out_first, out_second, out_far]
    projections = projections + [shifted(p, "c", 1) for p in projections[:3]]
    projections.append(shifted(out_far, "c", 1))
    gate = expert_gate.reshape(model, hidden)
    up = expert_up.reshape(model, hidden)
    down = expert_down.reshape(hidden, model)
    other_gate = shifted(gate, "c", 1)
    other_up = shifted(up, "c", 1)
    other_down = shifted(down, "c", 1)

    ids = route_ids.reshape(own_rows, TOP)
    send_table, sum_table = call(
        route_kernel,
        (pltpu.HBM((COLS, QUART * own_rows), BF), pltpu.HBM((QUART * own_rows, COLS), BF)),
        ids,
        ids.T,
        route_weight.reshape(own_rows, TOP),
    )

    normed, k, v, state, own = call(
        local_kernel,
        (
            pltpu.HBM((rows, model), BF),
            pltpu.HBM((rows, width), BF),
            pltpu.HBM((rows, width), BF),
            pltpu.VMEM((2 * rows, 128), BF),
            pltpu.HBM((own_rows, model), BF),
        ),
        *[inside(p) for p in pieces],
        outside(key_weight),
        outside(value_weight),
        attn_rows,
        out_specs=[OUTSIDE, OUTSIDE, OUTSIDE, INSIDE, INSIDE],
        scratch=[
            pltpu.VMEM((rows, model), BF),
            pltpu.VMEM((rows, width), BF),
            pltpu.VMEM((rows, width), BF),
            pltpu.VMEM((model, width), BF),
            pltpu.VMEM((model, width), BF),
            pltpu.SemaphoreType.DMA((2,)),
            pltpu.SemaphoreType.DMA((3,)),
        ],
    )
    q, local_mix = call(
        score_kernel, (pltpu.HBM((rows, width), BF), pltpu.HBM((rows, width), F32)), normed, query_weight, k, v
    )
    blocks = lax.axis_size(("x", "z"))
    states = inside(exchanged(state.reshape(blocks, 2 * rows // blocks, 128), ("x", "z")))
    before = call(prefix_kernel, pltpu.HBM(states.x.shape, BF), states)
    carried = inside(exchanged(before, ("x", "z")).reshape(2 * rows, 128))
    attended = call(mix_kernel, pltpu.VMEM((rows, width), BF), q, local_mix, carried, head_row)
    attended = inside(exchanged(attended.reshape(8, own_rows, width), ("y", "c")))
    step = model // QUART
    residual, sending = call(
        dispatch_kernel,
        (pltpu.HBM((own_rows, model), F32), pltpu.HBM((COLS, step), BF)),
        *[outside(p) for p in projections],
        attended,
        own,
        moe_row,
        outside(send_table),
        out_specs=[INSIDE, OUTSIDE],
        scratch=[
            pltpu.VMEM((8, width, model), BF),
            pltpu.VMEM((COLS, QUART * own_rows), BF),
            pltpu.VMEM((COLS, step), BF),
            pltpu.SemaphoreType.DMA((8,)),
            pltpu.SemaphoreType.DMA,
            pltpu.SemaphoreType.DMA((STEPS,)),
        ],
    )
    chips = ("x", "z", "y")
    received = inside(exchanged(sending.reshape(EXPERTS, PACK, step), chips))
    results = call(
        expert_kernel,
        pltpu.VMEM((EXPERTS, PACK, step), BF),
        received,
        either(jnp.asarray(order, BF)),
        either(jnp.asarray(order.T, BF)),
        *[outside(w) for w in (gate, up, down, other_gate, other_up, other_down)],
        scratch=[
            pltpu.VMEM((EXPERTS * CAP, model), BF),
            pltpu.VMEM((2, model, hidden), BF),
            pltpu.VMEM((2, model, hidden), BF),
            pltpu.VMEM((2, hidden, model), BF),
            pltpu.SemaphoreType.DMA((2, 3)),
        ],
        mib=36,
    )
    returned = inside(exchanged(results, chips).reshape(COLS, step))
    out = call(combine_kernel, shape((own_rows, model), BF), returned, either(sum_table), either(residual))
    return out.reshape(own_rows // batch, batch, model)


def solution(mesh):
    fine = Mesh(mesh.devices.reshape(4, 4, 4, 2), ("x", "z", "y", "c"))
    seq, head, every = ("x", "z"), ("y", "c"), ("x", "z", "y", "c")
    in_specs = (
        P(seq, None, head),
        P(),
        P(None, head),
        P(None, head),
        P(None, head),
        P(head),
        P(head, None),
        P(),
        P(every, None, None),
        P(every, None, None),
        P(every, None, None),
        P(every, None, None),
        P(every, None, None),
    )

    return jax.shard_map(body, mesh=fine, in_specs=in_specs, out_specs=P(every, None, None), check_vma=False)
```

```python
import jax
import jax.numpy as jnp
import numpy as np
from jax import lax
from jax.experimental import pallas as pl
from jax.experimental.pallas import tpu as pltpu
from jax.sharding import Mesh, PartitionSpec as P


EXPERTS = 64
TOP = 8
CAP = 12
QUART = 4
PACK = CAP * QUART
COLS = EXPERTS * PACK
WIDE = 8
REST = CAP - WIDE
GROUP = 16
PARTS = 4

norm_eps = 1e-05
head_eps = 1e-06

BF = jnp.bfloat16
F32 = jnp.float32


def shifted(x, axis, by):
    count = lax.axis_size(axis)
    return lax.ppermute(x, axis, [(i, (i + by) % count) for i in range(count)])


def swirled(x, by):
    ways = lax.axis_size("y")
    pairs = [(2 * y + c, 2 * ((y + (by if c == 0 else -by)) % ways) + c) for y in range(ways) for c in range(2)]
    return lax.ppermute(x, ("y", "c"), pairs)


def exchanged(x, axes):
    return lax.all_to_all(x, axes, split_axis=0, concat_axis=0, tiled=True)


def dot(a, b, dims=((1,), (0,))):
    return lax.dot_general(a, b, (dims, ((), ())), preferred_element_type=F32)


def silu(v):
    return v / (1.0 + jnp.exp(-v))


INSIDE = pl.BlockSpec(memory_space=pltpu.VMEM)
OUTSIDE = pl.BlockSpec(memory_space=pltpu.HBM)


class Placed:
    def __init__(self, x, spec, fixed):
        self.x = x if fixed is None else pltpu.with_memory_space_constraint(x, fixed)
        self.spec = spec


def inside(x):
    return Placed(x, INSIDE, pltpu.VMEM)


def outside(x):
    return Placed(x, OUTSIDE, pltpu.HBM)


def loaded(x):
    return Placed(x, INSIDE, pltpu.HBM)


def either(x):
    return Placed(x, INSIDE, None)


def call(kernel, out_shape, *args, out_specs=INSIDE, scratch=(), mib=24):
    args = [x if isinstance(x, Placed) else loaded(x) for x in args]
    if isinstance(out_shape, (list, tuple)) and not isinstance(out_specs, (list, tuple)):
        out_specs = [out_specs] * len(out_shape)
    return pl.pallas_call(
        kernel,
        out_shape=out_shape,
        in_specs=[x.spec for x in args],
        out_specs=out_specs,
        scratch_shapes=list(scratch),
        compiler_params=pltpu.CompilerParams(vmem_limit_bytes=mib * 2**20),
    )(*[x.x for x in args])


def route_kernel(ids_ref, weight_ref, send_ref, sum_ref):
    batch, _, span = ids_ref.shape
    rows = batch * span
    ids = jnp.zeros((rows, TOP), F32)
    ids_t = jnp.zeros((TOP, rows), F32)
    weights = jnp.zeros((rows, TOP), F32)
    for b in range(batch):
        row = lax.broadcasted_iota(jnp.int32, (span, rows), 1)
        pick = jnp.where(lax.broadcasted_iota(jnp.int32, (span, rows), 0) * batch + b == row, 1.0, 0.0).astype(BF)
        some = ids_ref[b].astype(F32).astype(BF)
        ids = ids + dot(pick, some, ((0,), (1,)))
        ids_t = ids_t + dot(some, pick)
        weights = weights + dot(pick, weight_ref[b].astype(BF), ((0,), (1,)))
    across = lax.broadcasted_iota(jnp.int32, (rows, EXPERTS), 1).astype(F32)
    down = lax.broadcasted_iota(jnp.int32, (EXPERTS, rows), 0).astype(F32)
    named = jnp.zeros((rows, EXPERTS), F32)
    named_t = jnp.zeros((EXPERTS, rows), F32)
    weight = jnp.zeros((rows, EXPERTS), F32)
    for j in range(TOP):
        hit = ids[:, j : j + 1] == across
        named = named + jnp.where(hit, 1.0, 0.0)
        weight = weight + jnp.where(hit, weights[:, j : j + 1], 0.0)
        named_t = named_t + jnp.where(ids_t[j : j + 1, :] == down, 1.0, 0.0)
    i0 = lax.broadcasted_iota(jnp.int32, (rows, rows), 0)
    i1 = lax.broadcasted_iota(jnp.int32, (rows, rows), 1)
    before = dot(jnp.where(i1 < i0, 1.0, 0.0).astype(BF), named.astype(BF))
    before_t = dot(named_t.astype(BF), jnp.where(i0 < i1, 1.0, 0.0).astype(BF))
    slot = jnp.where(named > 0.5, before, 128.0)
    slot_t = jnp.where(named_t > 0.5, before_t, 128.0)

    def placed(slots, q):
        return jnp.where(slots < WIDE - 0.5, slots + float(WIDE * q), slots + float(WIDE * (QUART - 1) + REST * q))

    slot_all = jnp.concatenate([placed(slot, q) for q in range(QUART)], axis=0).astype(BF)
    slot_all_t = jnp.concatenate([placed(slot_t, q) for q in range(QUART)], axis=1).astype(BF)

    def split(shape, dim, other):
        index = lax.broadcasted_iota(jnp.int32, shape, dim).astype(F32)
        expert = jnp.floor((index + 0.5) * (1.0 / PACK))
        spread = jnp.where(expert == lax.broadcasted_iota(jnp.int32, shape, other).astype(F32), 1.0, 0.0)
        return spread.astype(BF), index - expert * PACK

    spread_t, place_t = split((COLS, EXPERTS), 0, 1)
    send_ref[...] = jnp.where(dot(spread_t, slot_all_t) == place_t[:, :1], 1.0, 0.0).astype(BF)
    spread, place = split((EXPERTS, COLS), 1, 0)
    match = dot(slot_all, spread) == place[:1, :]
    weight_all = dot(weight.astype(BF), spread)
    sum_ref[...] = jnp.where(match, jnp.concatenate([weight_all] * QUART, axis=0), 0.0).astype(BF)


def copied(source, target, sem):
    copy = pltpu.make_async_copy(source, target, sem)
    copy.start()
    return copy


def copied_parts(source, target, sems):
    size = source.shape[0] // PARTS
    lines = [pl.ds(i * size, size) for i in range(PARTS)]
    return [copied(source.at[line], target.at[line], sems.at[i]) for i, line in enumerate(lines)]


def wait_all(copies):
    for copy in copies:
        copy.wait()


def block_order():
    y = lax.axis_index("y")
    c = lax.axis_index("c")
    return [((y + away) & 3) * 2 + core for core in (c, 1 - c) for away in (0, 3 - 2 * core, 1 + 2 * core, 2)]


def local_kernel(*refs):
    pieces, refs = refs[:8], refs[8:]
    wk_hbm, wv_hbm, gain_ref, normed_hbm, k_hbm, v_hbm, state_ref, own_ref, refs = *refs[:8], refs[8:]
    normed_ref, k_ref, v_ref, wk_ref, wv_ref, gain_rows_ref, in_sem, out_sem = refs
    k_copies = copied_parts(wk_hbm, wk_ref, in_sem.at[0])
    v_copies = copied_parts(wv_hbm, wv_ref, in_sem.at[1])
    gain_rows_ref[...] = gain_ref[...].astype(F32)
    rows, width = pieces[0].shape
    blocks = block_order()
    total = jnp.zeros((rows, 1), F32)
    for ref in pieces:
        values = ref[...].astype(F32)
        total = total + jnp.sum(values * values, axis=1, keepdims=True)
    scale = lax.rsqrt(total / (8 * width) + norm_eps)
    own_rows = rows // 8
    start = pl.multiple_of((lax.axis_index("y") * 2 + lax.axis_index("c")) * own_rows, own_rows)
    for ref, block in zip(pieces, blocks):
        columns = pl.ds(pl.multiple_of(block * width, width), width)
        gain = jnp.concatenate([gain_rows_ref[pl.ds(2 * block + i, 1), :] for i in range(2)], axis=1)
        normed_ref[:, columns] = (ref[...].astype(F32) * scale * gain).astype(BF)
        own_ref[:, columns] = ref[pl.ds(start, own_rows), :]
    out_copies = copied_parts(normed_ref, normed_hbm, out_sem.at[0])
    wait_all(k_copies)
    k_ref[...] = silu(dot(normed_ref[...], wk_ref[...])).astype(BF)
    out_copies += copied_parts(k_ref, k_hbm, out_sem.at[1])
    wait_all(v_copies)
    v_ref[...] = dot(normed_ref[...], wv_ref[...]).astype(BF)
    out_copies += copied_parts(v_ref, v_hbm, out_sem.at[2])
    sequence = lax.broadcasted_iota(jnp.int32, (rows, 128), 0) & 3
    for h in range(2):
        cols = slice(h * 128, (h + 1) * 128)
        keys = k_ref[:, cols].astype(F32)
        apart = jnp.concatenate([jnp.where(sequence == b, keys, 0.0).astype(BF) for b in range(4)], axis=1)
        state_ref[h * rows : (h + 1) * rows, :] = dot(apart, v_ref[:, cols], ((0,), (0,))).astype(BF)
    wait_all(out_copies)


def score_kernel(normed_ref, wq_ref, k_ref, v_ref, q_ref, local_ref):
    rows = normed_ref.shape[0]
    q = silu(dot(normed_ref[...], wq_ref[...])).astype(BF)
    q_ref[...] = q
    i0 = lax.broadcasted_iota(jnp.int32, (rows, rows), 0)
    i1 = lax.broadcasted_iota(jnp.int32, (rows, rows), 1)
    seen = (((i0 ^ i1) & 3) == 0) & (i1 <= i0)
    for h in range(2):
        cols = slice(h * 128, (h + 1) * 128)
        scores = jnp.where(seen, dot(q[:, cols], k_ref[:, cols], ((1,), (1,))), 0.0).astype(BF)
        local_ref[:, cols] = dot(scores, v_ref[:, cols])


def prefix_kernel(states_ref, before_ref):
    running = jnp.zeros(states_ref.shape[1:], F32)
    for i in range(states_ref.shape[0]):
        before_ref[i] = running.astype(BF)
        running = running + states_ref[i].astype(F32)


def mix_kernel(q_ref, local_ref, carried_ref, gain_ref, out_ref):
    rows = q_ref.shape[0]
    sequence = lax.broadcasted_iota(jnp.int32, (rows, 128), 0) & 3
    for h in range(2):
        cols = slice(h * 128, (h + 1) * 128)
        q = q_ref[:, cols].astype(F32)
        apart = jnp.concatenate([jnp.where(sequence == b, q, 0.0).astype(BF) for b in range(4)], axis=1)
        mixed = local_ref[:, cols] + dot(apart, carried_ref[h * rows : (h + 1) * rows, :])
        mean = jnp.mean(mixed * mixed, axis=1, keepdims=True)
        out_ref[:, cols] = (mixed * lax.rsqrt(mean + head_eps) * gain_ref[h : h + 1, :].astype(F32)).astype(BF)


def dispatch_kernel(*refs):
    weights, refs = refs[:8], refs[8:]
    attended_ref, own_ref, gain_ref, table_hbm, residual_ref, out_ref, refs = *refs[:6], refs[6:]
    weight_ref, table_ref, weight_sem, table_sem = refs
    copies = [copied(source, weight_ref.at[i], weight_sem.at[i]) for i, source in enumerate(weights[:7])]
    table_copies = copied_parts(table_hbm, table_ref, table_sem)
    _, width = own_ref.shape
    residual = own_ref[...].astype(F32)
    for i, block in enumerate(block_order()):
        if i < 7:
            copies[i].wait()
        weight = weight_ref[i] if i < 7 else weights[7][...]
        residual = residual + dot(attended_ref[block], weight).astype(BF).astype(F32)
    residual_ref[...] = residual
    mean = jnp.mean(residual * residual, axis=1, keepdims=True)
    gain = gain_ref[...].astype(F32)
    gain = jnp.concatenate([gain[i : i + 1, :] for i in range(gain.shape[0])], axis=1)
    entering = (residual * lax.rsqrt(mean + norm_eps) * gain).astype(BF)
    step = width // QUART
    stacked = jnp.concatenate([entering[:, q * step : (q + 1) * step] for q in range(QUART)], axis=0)
    wait_all(table_copies)
    out_ref[...] = dot(table_ref[...], stacked).astype(BF)


def expert_kernel(
    rows_ref, order_ref, back_ref, gate_hbm, up_hbm, down_hbm, gate_b_hbm, up_b_hbm, down_b_hbm, out_ref,
    x_ref, gate_ref, up_ref, down_ref, weight_sem,
):
    targets = (gate_ref, up_ref, down_ref)
    given = ((gate_hbm, up_hbm, down_hbm), (gate_b_hbm, up_b_hbm, down_b_hbm))
    copies = [
        [copied_parts(source, targets[i].at[half], weight_sem.at[half, i]) for i, source in enumerate(given[half])]
        for half in range(2)
    ]
    sources, _, step = rows_ref.shape
    head = sources * WIDE
    part = GROUP * REST
    wide = WIDE * QUART
    for q in range(QUART):
        for i in range(sources):
            x_ref[i * WIDE : (i + 1) * WIDE, q * step : (q + 1) * step] = rows_ref[i, q * WIDE : (q + 1) * WIDE, :]
    for g in range(sources // GROUP):
        rest = rows_ref[g * GROUP : (g + 1) * GROUP, wide:, :].reshape(GROUP * REST * QUART, step)
        rest = dot(order_ref[...], rest).astype(BF)
        for q in range(QUART):
            at = head + g * part
            x_ref[at : at + part, q * step : (q + 1) * step] = rest[q * part : (q + 1) * part]
    for first, lines in ((True, slice(0, head)), (False, slice(head, sources * CAP))):
        halves = []
        for half in range(2):
            if first:
                wait_all(copies[half][0] + copies[half][1])
            gated = dot(x_ref[lines, :], gate_ref[half])
            active = (silu(gated) * dot(x_ref[lines, :], up_ref[half])).astype(BF)
            if first:
                wait_all(copies[half][2])
            halves.append(dot(active, down_ref[half]).astype(BF))
        x_ref[lines, :] = (halves[0].astype(F32) + halves[1].astype(F32)).astype(BF)
    for q in range(QUART):
        for i in range(sources):
            out_ref[i, q * WIDE : (q + 1) * WIDE, :] = x_ref[i * WIDE : (i + 1) * WIDE, q * step : (q + 1) * step]
    for g in range(sources // GROUP):
        at = head + g * part
        rest = jnp.concatenate([x_ref[at : at + part, q * step : (q + 1) * step] for q in range(QUART)], axis=0)
        rest = dot(back_ref[...], rest).astype(BF)
        out_ref[g * GROUP : (g + 1) * GROUP, wide:, :] = rest.reshape(GROUP, REST * QUART, step)


def combine_kernel(rows_ref, table_ref, residual_ref, out_ref):
    rows = residual_ref.shape[0]
    step = rows_ref.shape[1]
    total = dot(table_ref[...], rows_ref[...])
    for q in range(QUART):
        cols = slice(q * step, (q + 1) * step)
        out_ref[:, cols] = (residual_ref[:, cols] + total[q * rows : (q + 1) * rows]).astype(BF)


def sorting():
    size = GROUP * REST * QUART
    order = np.zeros((size, size), np.float32)
    for q in range(QUART):
        for s in range(GROUP):
            for r in range(REST):
                order[(q * GROUP + s) * REST + r, (s * QUART + q) * REST + r] = 1.0
    return order


def body(
    tokens, attn_gain, query_weight, key_weight, value_weight, head_gain, out_weight, moe_gain,
    route_ids, route_weight, expert_gate, expert_up, expert_down,
):
    shape = jax.ShapeDtypeStruct
    block_len, batch, width = tokens.shape
    rows = block_len * batch
    model = attn_gain.shape[0]
    own_rows = rows // 8
    hidden = expert_gate.shape[2]
    order = sorting()

    attn_rows = attn_gain.reshape(-1, 128)
    head_rows = head_gain.reshape(-1, 128)
    moe_rows = moe_gain.reshape(-1, 128)
    mine = tokens.reshape(rows, width)
    first = swirled(mine, 1)
    second = swirled(mine, -1)
    far = swirled(first, 1)
    pieces = [mine, first, second, far]
    pieces = pieces + [shifted(p, "c", 1) for p in pieces]

    later_out, *pieces[4:] = lax.optimization_barrier((out_weight, *pieces[4:]))
    out_first = swirled(later_out, 1)
    out_second = swirled(later_out, -1)
    out_far = swirled(out_first, 1)
    projections = [out_weight, out_first, out_second, out_far]
    projections = projections + [shifted(p, "c", 1) for p in projections[:3]]
    projections.append(shifted(out_far, "c", 1))
    gate = expert_gate.reshape(model, hidden)
    up = expert_up.reshape(model, hidden)
    down = expert_down.reshape(hidden, model)
    other_gate = shifted(gate, "c", 1)
    other_up = shifted(up, "c", 1)
    other_down = shifted(down, "c", 1)

    send_table, sum_table = call(
        route_kernel,
        (pltpu.HBM((COLS, QUART * own_rows), BF), pltpu.HBM((QUART * own_rows, COLS), BF)),
        route_ids.transpose(1, 2, 0),
        route_weight.transpose(1, 2, 0),
    )

    normed, k, v, state, own = call(
        local_kernel,
        (
            pltpu.HBM((rows, model), BF),
            pltpu.HBM((rows, width), BF),
            pltpu.HBM((rows, width), BF),
            pltpu.VMEM((2 * rows, 128), BF),
            pltpu.HBM((own_rows, model), BF),
        ),
        *[inside(p) for p in pieces],
        outside(key_weight),
        outside(value_weight),
        attn_rows,
        out_specs=[OUTSIDE, OUTSIDE, OUTSIDE, INSIDE, INSIDE],
        scratch=[
            pltpu.VMEM((rows, model), BF),
            pltpu.VMEM((rows, width), BF),
            pltpu.VMEM((rows, width), BF),
            pltpu.VMEM((model, width), BF),
            pltpu.VMEM((model, width), BF),
            pltpu.VMEM(attn_rows.shape, F32),
            pltpu.SemaphoreType.DMA((2, PARTS)),
            pltpu.SemaphoreType.DMA((3, PARTS)),
        ],
    )
    q, local_mix = call(
        score_kernel, (pltpu.HBM((rows, width), BF), pltpu.HBM((rows, width), F32)), normed, query_weight, k, v
    )
    blocks = lax.axis_size(("x", "z"))
    states = inside(exchanged(state.reshape(blocks, 2 * rows // blocks, 128), ("x", "z")))
    before = call(prefix_kernel, pltpu.HBM(states.x.shape, BF), states)
    carried = inside(exchanged(before, ("x", "z")).reshape(2 * rows, 128))
    attended = call(mix_kernel, pltpu.VMEM((rows, width), BF), q, local_mix, carried, head_rows)
    attended = inside(exchanged(attended.reshape(8, own_rows, width), ("y", "c")))
    step = model // QUART
    residual, sending = call(
        dispatch_kernel,
        (pltpu.HBM((own_rows, model), F32), pltpu.VMEM((COLS, step), BF)),
        *[outside(p) for p in projections[:7]],
        inside(projections[7]),
        attended,
        own,
        moe_rows,
        outside(send_table),
        scratch=[
            pltpu.VMEM((7, width, model), BF),
            pltpu.VMEM((COLS, QUART * own_rows), BF),
            pltpu.SemaphoreType.DMA((7,)),
            pltpu.SemaphoreType.DMA((PARTS,)),
        ],
    )
    chips = ("x", "z", "y")
    received = inside(exchanged(sending.reshape(EXPERTS, PACK, step), chips))
    results = call(
        expert_kernel,
        pltpu.VMEM((EXPERTS, PACK, step), BF),
        received,
        either(jnp.asarray(order, BF)),
        either(jnp.asarray(order.T, BF)),
        *[outside(w) for w in (gate, up, down, other_gate, other_up, other_down)],
        scratch=[
            pltpu.VMEM((EXPERTS * CAP, model), BF),
            pltpu.VMEM((2, model, hidden), BF),
            pltpu.VMEM((2, model, hidden), BF),
            pltpu.VMEM((2, hidden, model), BF),
            pltpu.SemaphoreType.DMA((2, 3, PARTS)),
        ],
        mib=36,
    )
    returned = inside(exchanged(results, chips).reshape(COLS, step))
    out = call(combine_kernel, shape((own_rows, model), BF), returned, either(sum_table), either(residual))
    return out.reshape(own_rows // batch, batch, model)


def solution(mesh):
    fine = Mesh(mesh.devices.reshape(4, 4, 4, 2), ("x", "z", "y", "c"))
    seq, head, every = ("x", "z"), ("y", "c"), ("x", "z", "y", "c")
    in_specs = (
        P(seq, None, head),
        P(),
        P(None, head),
        P(None, head),
        P(None, head),
        P(head),
        P(head, None),
        P(),
        P(every, None, None),
        P(every, None, None),
        P(every, None, None),
        P(every, None, None),
        P(every, None, None),
    )

    return jax.shard_map(body, mesh=fine, in_specs=in_specs, out_specs=P(every, None, None), check_vma=False)
```

```python
import jax
import jax.numpy as jnp
import numpy as np
from jax import lax
from jax.experimental import pallas as pl
from jax.experimental.pallas import tpu as pltpu
from jax.sharding import Mesh, PartitionSpec as P


EXPERTS = 64
TOP = 8
CAP = 12
QUART = 4
PACK = CAP * QUART
COLS = EXPERTS * PACK
WIDE = 8
REST = CAP - WIDE
GROUP = 16
PARTS = 4

norm_eps = 1e-05
head_eps = 1e-06

BF = jnp.bfloat16
F32 = jnp.float32


def shifted(x, axis, by):
    count = lax.axis_size(axis)
    return lax.ppermute(x, axis, [(i, (i + by) % count) for i in range(count)])


def swirled(x, by):
    ways = lax.axis_size("y")
    pairs = [(2 * y + c, 2 * ((y + (by if c == 0 else -by)) % ways) + c) for y in range(ways) for c in range(2)]
    return lax.ppermute(x, ("y", "c"), pairs)


def exchanged(x, axes):
    return lax.all_to_all(x, axes, split_axis=0, concat_axis=0, tiled=True)


def dot(a, b, dims=((1,), (0,))):
    return lax.dot_general(a, b, (dims, ((), ())), preferred_element_type=F32)


def silu(v):
    return v / (1.0 + jnp.exp(-v))


INSIDE = pl.BlockSpec(memory_space=pltpu.VMEM)
OUTSIDE = pl.BlockSpec(memory_space=pltpu.HBM)


class Placed:
    def __init__(self, x, spec, fixed):
        self.x = x if fixed is None else pltpu.with_memory_space_constraint(x, fixed)
        self.spec = spec


def inside(x):
    return Placed(x, INSIDE, pltpu.VMEM)


def outside(x):
    return Placed(x, OUTSIDE, pltpu.HBM)


def loaded(x):
    return Placed(x, INSIDE, pltpu.HBM)


def either(x):
    return Placed(x, INSIDE, None)


def call(kernel, out_shape, *args, out_specs=INSIDE, scratch=(), mib=24):
    args = [x if isinstance(x, Placed) else loaded(x) for x in args]
    if isinstance(out_shape, (list, tuple)) and not isinstance(out_specs, (list, tuple)):
        out_specs = [out_specs] * len(out_shape)
    return pl.pallas_call(
        kernel,
        out_shape=out_shape,
        in_specs=[x.spec for x in args],
        out_specs=out_specs,
        scratch_shapes=list(scratch),
        compiler_params=pltpu.CompilerParams(vmem_limit_bytes=mib * 2**20),
    )(*[x.x for x in args])


def route_kernel(ids_ref, weight_ref, send_ref, sum_ref):
    batch, _, span = ids_ref.shape
    rows = batch * span
    ids = jnp.zeros((rows, TOP), F32)
    ids_t = jnp.zeros((TOP, rows), F32)
    weights = jnp.zeros((rows, TOP), F32)
    for b in range(batch):
        row = lax.broadcasted_iota(jnp.int32, (span, rows), 1)
        pick = jnp.where(lax.broadcasted_iota(jnp.int32, (span, rows), 0) * batch + b == row, 1.0, 0.0).astype(BF)
        some = ids_ref[b].astype(F32).astype(BF)
        ids = ids + dot(pick, some, ((0,), (1,)))
        ids_t = ids_t + dot(some, pick)
        weights = weights + dot(pick, weight_ref[b].astype(BF), ((0,), (1,)))
    across = lax.broadcasted_iota(jnp.int32, (rows, EXPERTS), 1).astype(F32)
    down = lax.broadcasted_iota(jnp.int32, (EXPERTS, rows), 0).astype(F32)
    named = jnp.zeros((rows, EXPERTS), F32)
    named_t = jnp.zeros((EXPERTS, rows), F32)
    weight = jnp.zeros((rows, EXPERTS), F32)
    for j in range(TOP):
        hit = ids[:, j : j + 1] == across
        named = named + jnp.where(hit, 1.0, 0.0)
        weight = weight + jnp.where(hit, weights[:, j : j + 1], 0.0)
        named_t = named_t + jnp.where(ids_t[j : j + 1, :] == down, 1.0, 0.0)
    i0 = lax.broadcasted_iota(jnp.int32, (rows, rows), 0)
    i1 = lax.broadcasted_iota(jnp.int32, (rows, rows), 1)
    before = dot(jnp.where(i1 < i0, 1.0, 0.0).astype(BF), named.astype(BF))
    before_t = dot(named_t.astype(BF), jnp.where(i0 < i1, 1.0, 0.0).astype(BF))
    slot = jnp.where(named > 0.5, before, 128.0)
    slot_t = jnp.where(named_t > 0.5, before_t, 128.0)

    def placed(slots, q):
        return jnp.where(slots < WIDE - 0.5, slots + float(WIDE * q), slots + float(WIDE * (QUART - 1) + REST * q))

    slot_all = jnp.concatenate([placed(slot, q) for q in range(QUART)], axis=0).astype(BF)
    slot_all_t = jnp.concatenate([placed(slot_t, q) for q in range(QUART)], axis=1).astype(BF)

    def split(shape, dim, other):
        index = lax.broadcasted_iota(jnp.int32, shape, dim).astype(F32)
        expert = jnp.floor((index + 0.5) * (1.0 / PACK))
        spread = jnp.where(expert == lax.broadcasted_iota(jnp.int32, shape, other).astype(F32), 1.0, 0.0)
        return spread.astype(BF), index - expert * PACK

    spread_t, place_t = split((COLS, EXPERTS), 0, 1)
    send_ref[...] = jnp.where(dot(spread_t, slot_all_t) == place_t[:, :1], 1.0, 0.0).astype(BF)
    spread, place = split((EXPERTS, COLS), 1, 0)
    match = dot(slot_all, spread) == place[:1, :]
    weight_all = dot(weight.astype(BF), spread)
    sum_ref[...] = jnp.where(match, jnp.concatenate([weight_all] * QUART, axis=0), 0.0).astype(BF)


def copied(source, target, sem):
    copy = pltpu.make_async_copy(source, target, sem)
    copy.start()
    return copy


def copied_parts(source, target, sems):
    size = source.shape[0] // PARTS
    lines = [pl.ds(i * size, size) for i in range(PARTS)]
    return [copied(source.at[line], target.at[line], sems.at[i]) for i, line in enumerate(lines)]


def wait_all(copies):
    for copy in copies:
        copy.wait()


def block_order():
    y = lax.axis_index("y")
    c = lax.axis_index("c")
    return [((y + away) & 3) * 2 + core for core in (c, 1 - c) for away in (0, 3 - 2 * core, 1 + 2 * core, 2)]


def local_kernel(*refs):
    pieces, refs = refs[:8], refs[8:]
    wk_hbm, wv_hbm, wq_hbm, gain_ref, k_hbm, v_hbm, q_hbm, state_ref, own_ref, refs = *refs[:9], refs[9:]
    normed_ref, k_ref, v_ref, q_ref, wk_ref, wv_ref, wq_ref, gain_rows_ref, in_sem, out_sem = refs
    k_copies = copied_parts(wk_hbm, wk_ref, in_sem.at[0])
    v_copies = copied_parts(wv_hbm, wv_ref, in_sem.at[1])
    q_copies = copied_parts(wq_hbm, wq_ref, in_sem.at[2])
    gain_rows_ref[...] = gain_ref[...].astype(F32)
    rows, width = pieces[0].shape
    blocks = block_order()
    total = jnp.zeros((rows, 1), F32)
    for ref in pieces:
        values = ref[...].astype(F32)
        total = total + jnp.sum(values * values, axis=1, keepdims=True)
    scale = lax.rsqrt(total / (8 * width) + norm_eps)
    own_rows = rows // 8
    start = pl.multiple_of((lax.axis_index("y") * 2 + lax.axis_index("c")) * own_rows, own_rows)
    for ref, block in zip(pieces, blocks):
        columns = pl.ds(pl.multiple_of(block * width, width), width)
        gain = jnp.concatenate([gain_rows_ref[pl.ds(2 * block + i, 1), :] for i in range(2)], axis=1)
        normed_ref[:, columns] = (ref[...].astype(F32) * scale * gain).astype(BF)
        own_ref[:, columns] = ref[pl.ds(start, own_rows), :]
    wait_all(k_copies)
    k_ref[...] = silu(dot(normed_ref[...], wk_ref[...])).astype(BF)
    out_copies = copied_parts(k_ref, k_hbm, out_sem.at[0])
    wait_all(v_copies)
    v_ref[...] = dot(normed_ref[...], wv_ref[...]).astype(BF)
    out_copies += copied_parts(v_ref, v_hbm, out_sem.at[1])
    wait_all(q_copies)
    q_ref[...] = silu(dot(normed_ref[...], wq_ref[...])).astype(BF)
    out_copies += copied_parts(q_ref, q_hbm, out_sem.at[2])
    sequence = lax.broadcasted_iota(jnp.int32, (rows, 128), 0) & 3
    for h in range(2):
        cols = slice(h * 128, (h + 1) * 128)
        keys = k_ref[:, cols].astype(F32)
        apart = jnp.concatenate([jnp.where(sequence == b, keys, 0.0).astype(BF) for b in range(4)], axis=1)
        state_ref[h * rows : (h + 1) * rows, :] = dot(apart, v_ref[:, cols], ((0,), (0,))).astype(BF)
    wait_all(out_copies)


def score_kernel(q_ref, k_ref, v_ref, local_ref):
    rows = q_ref.shape[0]
    i0 = lax.broadcasted_iota(jnp.int32, (rows, rows), 0)
    i1 = lax.broadcasted_iota(jnp.int32, (rows, rows), 1)
    seen = (((i0 ^ i1) & 3) == 0) & (i1 <= i0)
    for h in range(2):
        cols = slice(h * 128, (h + 1) * 128)
        scores = jnp.where(seen, dot(q_ref[:, cols], k_ref[:, cols], ((1,), (1,))), 0.0).astype(BF)
        local_ref[:, cols] = dot(scores, v_ref[:, cols])


def prefix_kernel(states_ref, before_ref):
    running = jnp.zeros(states_ref.shape[1:], F32)
    for i in range(states_ref.shape[0]):
        before_ref[i] = running.astype(BF)
        running = running + states_ref[i].astype(F32)


def mix_kernel(q_ref, local_ref, carried_ref, gain_ref, out_ref):
    rows = q_ref.shape[0]
    sequence = lax.broadcasted_iota(jnp.int32, (rows, 128), 0) & 3
    for h in range(2):
        cols = slice(h * 128, (h + 1) * 128)
        q = q_ref[:, cols].astype(F32)
        apart = jnp.concatenate([jnp.where(sequence == b, q, 0.0).astype(BF) for b in range(4)], axis=1)
        mixed = local_ref[:, cols] + dot(apart, carried_ref[h * rows : (h + 1) * rows, :])
        mean = jnp.mean(mixed * mixed, axis=1, keepdims=True)
        out_ref[:, cols] = (mixed * lax.rsqrt(mean + head_eps) * gain_ref[h : h + 1, :].astype(F32)).astype(BF)


def dispatch_kernel(*refs):
    weights, refs = refs[:8], refs[8:]
    attended_ref, own_ref, gain_ref, table_hbm, residual_ref, out_ref, refs = *refs[:6], refs[6:]
    weight_ref, table_ref, weight_sem, table_sem = refs
    copies = [copied_parts(source, weight_ref.at[i], weight_sem.at[i]) for i, source in enumerate(weights[:7])]
    table_copies = copied_parts(table_hbm, table_ref, table_sem)
    _, width = own_ref.shape
    residual = own_ref[...].astype(F32)
    blocks = block_order()
    for i in (7, 0, 1, 2, 3, 4, 5, 6):
        if i < 7:
            wait_all(copies[i])
        weight = weight_ref[i] if i < 7 else weights[7][...]
        residual = residual + dot(attended_ref[blocks[i]], weight).astype(BF).astype(F32)
    residual_ref[...] = residual
    mean = jnp.mean(residual * residual, axis=1, keepdims=True)
    gain = gain_ref[...].astype(F32)
    gain = jnp.concatenate([gain[i : i + 1, :] for i in range(gain.shape[0])], axis=1)
    entering = (residual * lax.rsqrt(mean + norm_eps) * gain).astype(BF)
    step = width // QUART
    stacked = jnp.concatenate([entering[:, q * step : (q + 1) * step] for q in range(QUART)], axis=0)
    wait_all(table_copies)
    out_ref[...] = dot(table_ref[...], stacked).astype(BF)


def expert_kernel(
    rows_ref, order_ref, back_ref, gate_hbm, up_hbm, down_hbm, gate_b_hbm, up_b_hbm, down_b_hbm, out_ref,
    x_ref, gate_ref, up_ref, down_ref, weight_sem,
):
    targets = (gate_ref, up_ref, down_ref)
    given = ((gate_hbm, up_hbm, down_hbm), (gate_b_hbm, up_b_hbm, down_b_hbm))
    copies = [
        [copied_parts(source, targets[i].at[half], weight_sem.at[half, i]) for i, source in enumerate(given[half])]
        for half in range(2)
    ]
    sources, _, step = rows_ref.shape
    head = sources * WIDE
    part = GROUP * REST
    wide = WIDE * QUART
    for q in range(QUART):
        for i in range(sources):
            x_ref[i * WIDE : (i + 1) * WIDE, q * step : (q + 1) * step] = rows_ref[i, q * WIDE : (q + 1) * WIDE, :]
    for g in range(sources // GROUP):
        rest = rows_ref[g * GROUP : (g + 1) * GROUP, wide:, :].reshape(GROUP * REST * QUART, step)
        rest = dot(order_ref[...], rest).astype(BF)
        for q in range(QUART):
            at = head + g * part
            x_ref[at : at + part, q * step : (q + 1) * step] = rest[q * part : (q + 1) * part]
    for first, lines in ((True, slice(0, head)), (False, slice(head, sources * CAP))):
        halves = []
        for half in range(2):
            if first:
                wait_all(copies[half][0] + copies[half][1])
            gated = dot(x_ref[lines, :], gate_ref[half])
            active = (silu(gated) * dot(x_ref[lines, :], up_ref[half])).astype(BF)
            if first:
                wait_all(copies[half][2])
            halves.append(dot(active, down_ref[half]).astype(BF))
        x_ref[lines, :] = (halves[0].astype(F32) + halves[1].astype(F32)).astype(BF)
    for q in range(QUART):
        for i in range(sources):
            out_ref[i, q * WIDE : (q + 1) * WIDE, :] = x_ref[i * WIDE : (i + 1) * WIDE, q * step : (q + 1) * step]
    for g in range(sources // GROUP):
        at = head + g * part
        rest = jnp.concatenate([x_ref[at : at + part, q * step : (q + 1) * step] for q in range(QUART)], axis=0)
        rest = dot(back_ref[...], rest).astype(BF)
        out_ref[g * GROUP : (g + 1) * GROUP, wide:, :] = rest.reshape(GROUP, REST * QUART, step)


def combine_kernel(rows_ref, table_ref, residual_ref, out_ref):
    rows = residual_ref.shape[0]
    step = rows_ref.shape[1]
    total = dot(table_ref[...], rows_ref[...])
    for q in range(QUART):
        cols = slice(q * step, (q + 1) * step)
        out_ref[:, cols] = (residual_ref[:, cols] + total[q * rows : (q + 1) * rows]).astype(BF)


def sorting():
    size = GROUP * REST * QUART
    order = np.zeros((size, size), np.float32)
    for q in range(QUART):
        for s in range(GROUP):
            for r in range(REST):
                order[(q * GROUP + s) * REST + r, (s * QUART + q) * REST + r] = 1.0
    return order


def body(
    tokens, attn_gain, query_weight, key_weight, value_weight, head_gain, out_weight, moe_gain,
    route_ids, route_weight, expert_gate, expert_up, expert_down,
):
    shape = jax.ShapeDtypeStruct
    block_len, batch, width = tokens.shape
    rows = block_len * batch
    model = attn_gain.shape[0]
    own_rows = rows // 8
    hidden = expert_gate.shape[2]
    order = sorting()

    attn_rows = attn_gain.reshape(-1, 128)
    head_rows = head_gain.reshape(-1, 128)
    moe_rows = moe_gain.reshape(-1, 128)
    mine = tokens.reshape(rows, width)
    first = swirled(mine, 1)
    second = swirled(mine, -1)
    far = swirled(first, 1)
    pieces = [mine, first, second, far]
    pieces = pieces + [shifted(p, "c", 1) for p in pieces]

    later_out, *pieces[4:] = lax.optimization_barrier((out_weight, *pieces[4:]))
    out_first = swirled(later_out, 1)
    out_second = swirled(later_out, -1)
    out_far = swirled(out_first, 1)
    projections = [out_weight, out_first, out_second, out_far]
    projections = projections + [shifted(p, "c", 1) for p in projections[:3]]
    projections.append(shifted(out_far, "c", 1))
    gate = expert_gate.reshape(model, hidden)
    up = expert_up.reshape(model, hidden)
    down = expert_down.reshape(hidden, model)
    other_gate = shifted(gate, "c", 1)
    other_up = shifted(up, "c", 1)
    other_down = shifted(down, "c", 1)

    send_table, sum_table = call(
        route_kernel,
        (pltpu.HBM((COLS, QUART * own_rows), BF), pltpu.HBM((QUART * own_rows, COLS), BF)),
        route_ids.transpose(1, 2, 0),
        route_weight.transpose(1, 2, 0),
    )

    k, v, q, state, own = call(
        local_kernel,
        (
            pltpu.HBM((rows, width), BF),
            pltpu.HBM((rows, width), BF),
            pltpu.HBM((rows, width), BF),
            pltpu.VMEM((2 * rows, 128), BF),
            pltpu.HBM((own_rows, model), BF),
        ),
        *[inside(p) for p in pieces],
        outside(key_weight),
        outside(value_weight),
        outside(query_weight),
        attn_rows,
        out_specs=[OUTSIDE, OUTSIDE, OUTSIDE, INSIDE, INSIDE],
        scratch=[
            pltpu.VMEM((rows, model), BF),
            pltpu.VMEM((rows, width), BF),
            pltpu.VMEM((rows, width), BF),
            pltpu.VMEM((rows, width), BF),
            pltpu.VMEM((model, width), BF),
            pltpu.VMEM((model, width), BF),
            pltpu.VMEM((model, width), BF),
            pltpu.VMEM(attn_rows.shape, F32),
            pltpu.SemaphoreType.DMA((3, PARTS)),
            pltpu.SemaphoreType.DMA((3, PARTS)),
        ],
    )
    local_mix = call(score_kernel, pltpu.HBM((rows, width), F32), q, k, v)
    blocks = lax.axis_size(("x", "z"))
    states = inside(exchanged(state.reshape(blocks, 2 * rows // blocks, 128), ("x", "z")))
    before = call(prefix_kernel, pltpu.HBM(states.x.shape, BF), states)
    carried = inside(exchanged(before, ("x", "z")).reshape(2 * rows, 128))
    attended = call(mix_kernel, pltpu.VMEM((rows, width), BF), q, local_mix, carried, head_rows)
    attended = inside(exchanged(attended.reshape(8, own_rows, width), ("y", "c")))
    step = model // QUART
    residual, sending = call(
        dispatch_kernel,
        (pltpu.HBM((own_rows, model), F32), pltpu.VMEM((COLS, step), BF)),
        *[outside(p) for p in projections[:7]],
        inside(projections[7]),
        attended,
        own,
        moe_rows,
        outside(send_table),
        scratch=[
            pltpu.VMEM((7, width, model), BF),
            pltpu.VMEM((COLS, QUART * own_rows), BF),
            pltpu.SemaphoreType.DMA((7, PARTS)),
            pltpu.SemaphoreType.DMA((PARTS,)),
        ],
    )
    chips = ("x", "z", "y")
    received = inside(exchanged(sending.reshape(EXPERTS, PACK, step), chips))
    results = call(
        expert_kernel,
        pltpu.VMEM((EXPERTS, PACK, step), BF),
        received,
        either(jnp.asarray(order, BF)),
        either(jnp.asarray(order.T, BF)),
        *[outside(w) for w in (gate, up, down, other_gate, other_up, other_down)],
        scratch=[
            pltpu.VMEM((EXPERTS * CAP, model), BF),
            pltpu.VMEM((2, model, hidden), BF),
            pltpu.VMEM((2, model, hidden), BF),
            pltpu.VMEM((2, hidden, model), BF),
            pltpu.SemaphoreType.DMA((2, 3, PARTS)),
        ],
        mib=36,
    )
    returned = inside(exchanged(results, chips).reshape(COLS, step))
    out = call(combine_kernel, shape((own_rows, model), BF), returned, either(sum_table), either(residual))
    return out.reshape(own_rows // batch, batch, model)


def solution(mesh):
    fine = Mesh(mesh.devices.reshape(4, 4, 4, 2), ("x", "z", "y", "c"))
    seq, head, every = ("x", "z"), ("y", "c"), ("x", "z", "y", "c")
    in_specs = (
        P(seq, None, head),
        P(),
        P(None, head),
        P(None, head),
        P(None, head),
        P(head),
        P(head, None),
        P(),
        P(every, None, None),
        P(every, None, None),
        P(every, None, None),
        P(every, None, None),
        P(every, None, None),
    )

    return jax.shard_map(body, mesh=fine, in_specs=in_specs, out_specs=P(every, None, None), check_vma=False)
```

```python
import jax
import jax.numpy as jnp
import numpy as np
from jax import lax
from jax.experimental import pallas as pl
from jax.experimental.pallas import tpu as pltpu
from jax.sharding import Mesh, PartitionSpec as P


EXPERTS = 64
TOP = 8
CAP = 12
QUART = 4
PACK = CAP * QUART
COLS = EXPERTS * PACK
WIDE = 8
REST = CAP - WIDE
GROUP = 16

norm_eps = 1e-05
head_eps = 1e-06

BF = jnp.bfloat16
F32 = jnp.float32


def shifted(x, axis, by):
    count = lax.axis_size(axis)
    return lax.ppermute(x, axis, [(i, (i + by) % count) for i in range(count)])


def swirled(x, by):
    ways = lax.axis_size("y")
    pairs = [(2 * y + c, 2 * ((y + (by if c == 0 else -by)) % ways) + c) for y in range(ways) for c in range(2)]
    return lax.ppermute(x, ("y", "c"), pairs)


def exchanged(x, axes):
    return lax.all_to_all(x, axes, split_axis=0, concat_axis=0, tiled=True)


def dot(a, b, dims=((1,), (0,))):
    return lax.dot_general(a, b, (dims, ((), ())), preferred_element_type=F32)


def silu(v):
    return v / (1.0 + jnp.exp(-v))


INSIDE = pl.BlockSpec(memory_space=pltpu.VMEM)
OUTSIDE = pl.BlockSpec(memory_space=pltpu.HBM)


class Placed:
    def __init__(self, x, spec, fixed):
        self.x = x if fixed is None else pltpu.with_memory_space_constraint(x, fixed)
        self.spec = spec


def inside(x):
    return Placed(x, INSIDE, pltpu.VMEM)


def outside(x):
    return Placed(x, OUTSIDE, pltpu.HBM)


def loaded(x):
    return Placed(x, INSIDE, pltpu.HBM)


def either(x):
    return Placed(x, INSIDE, None)


def call(kernel, out_shape, *args, out_specs=INSIDE, scratch=(), mib=24):
    args = [x if isinstance(x, Placed) else loaded(x) for x in args]
    if isinstance(out_shape, (list, tuple)) and not isinstance(out_specs, (list, tuple)):
        out_specs = [out_specs] * len(out_shape)
    return pl.pallas_call(
        kernel,
        out_shape=out_shape,
        in_specs=[x.spec for x in args],
        out_specs=out_specs,
        scratch_shapes=list(scratch),
        compiler_params=pltpu.CompilerParams(vmem_limit_bytes=mib * 2**20),
    )(*[x.x for x in args])


def route_kernel(ids_ref, weight_ref, send_ref, sum_ref):
    batch, _, span = ids_ref.shape
    rows = batch * span
    ids = jnp.zeros((rows, TOP), F32)
    ids_t = jnp.zeros((TOP, rows), F32)
    weights = jnp.zeros((rows, TOP), F32)
    for b in range(batch):
        row = lax.broadcasted_iota(jnp.int32, (span, rows), 1)
        pick = jnp.where(lax.broadcasted_iota(jnp.int32, (span, rows), 0) * batch + b == row, 1.0, 0.0).astype(BF)
        some = ids_ref[b].astype(F32).astype(BF)
        ids = ids + dot(pick, some, ((0,), (1,)))
        ids_t = ids_t + dot(some, pick)
        weights = weights + dot(pick, weight_ref[b].astype(BF), ((0,), (1,)))
    across = lax.broadcasted_iota(jnp.int32, (rows, EXPERTS), 1).astype(F32)
    down = lax.broadcasted_iota(jnp.int32, (EXPERTS, rows), 0).astype(F32)
    named = jnp.zeros((rows, EXPERTS), F32)
    named_t = jnp.zeros((EXPERTS, rows), F32)
    weight = jnp.zeros((rows, EXPERTS), F32)
    for j in range(TOP):
        hit = ids[:, j : j + 1] == across
        named = named + jnp.where(hit, 1.0, 0.0)
        weight = weight + jnp.where(hit, weights[:, j : j + 1], 0.0)
        named_t = named_t + jnp.where(ids_t[j : j + 1, :] == down, 1.0, 0.0)
    i0 = lax.broadcasted_iota(jnp.int32, (rows, rows), 0)
    i1 = lax.broadcasted_iota(jnp.int32, (rows, rows), 1)
    before = dot(jnp.where(i1 < i0, 1.0, 0.0).astype(BF), named.astype(BF))
    before_t = dot(named_t.astype(BF), jnp.where(i0 < i1, 1.0, 0.0).astype(BF))
    slot = jnp.where(named > 0.5, before, 128.0)
    slot_t = jnp.where(named_t > 0.5, before_t, 128.0)

    def placed(slots, q):
        return jnp.where(slots < WIDE - 0.5, slots + float(WIDE * q), slots + float(WIDE * (QUART - 1) + REST * q))

    slot_all = jnp.concatenate([placed(slot, q) for q in range(QUART)], axis=0).astype(BF)
    slot_all_t = jnp.concatenate([placed(slot_t, q) for q in range(QUART)], axis=1).astype(BF)

    def split(shape, dim, other):
        index = lax.broadcasted_iota(jnp.int32, shape, dim).astype(F32)
        expert = jnp.floor((index + 0.5) * (1.0 / PACK))
        spread = jnp.where(expert == lax.broadcasted_iota(jnp.int32, shape, other).astype(F32), 1.0, 0.0)
        return spread.astype(BF), index - expert * PACK

    spread_t, place_t = split((COLS, EXPERTS), 0, 1)
    send_ref[...] = jnp.where(dot(spread_t, slot_all_t) == place_t[:, :1], 1.0, 0.0).astype(BF)
    spread, place = split((EXPERTS, COLS), 1, 0)
    match = dot(slot_all, spread) == place[:1, :]
    weight_all = dot(weight.astype(BF), spread)
    sum_ref[...] = jnp.where(match, jnp.concatenate([weight_all] * QUART, axis=0), 0.0).astype(BF)


def copied(source, target, sem):
    copy = pltpu.make_async_copy(source, target, sem)
    copy.start()
    return copy


def wait_all(copies):
    for copy in copies:
        copy.wait()


def block_order():
    y = lax.axis_index("y")
    c = lax.axis_index("c")
    return [((y + away) & 3) * 2 + core for core in (c, 1 - c) for away in (0, 3 - 2 * core, 1 + 2 * core, 2)]


def load_kernel(*refs):
    count = len(refs) // 2
    copies = [copied(refs[i], refs[count + i], refs[-1].at[i]) for i in range(count)]
    wait_all(copies)


def local_kernel(*refs):
    pieces, refs = refs[:8], refs[8:]
    wk_ref, wv_ref, wq_ref, gain_ref, q_ref, local_ref, state_ref, own_ref, normed_ref, gain_rows_ref = refs
    gain_rows_ref[...] = gain_ref[...].astype(F32)
    rows, width = pieces[0].shape
    blocks = block_order()
    total = jnp.zeros((rows, 1), F32)
    for ref in pieces:
        values = ref[...].astype(F32)
        total = total + jnp.sum(values * values, axis=1, keepdims=True)
    scale = lax.rsqrt(total / (8 * width) + norm_eps)
    own_rows = rows // 8
    start = pl.multiple_of((lax.axis_index("y") * 2 + lax.axis_index("c")) * own_rows, own_rows)
    for ref, block in zip(pieces, blocks):
        columns = pl.ds(pl.multiple_of(block * width, width), width)
        gain = jnp.concatenate([gain_rows_ref[pl.ds(2 * block + i, 1), :] for i in range(2)], axis=1)
        normed_ref[:, columns] = (ref[...].astype(F32) * scale * gain).astype(BF)
        own_ref[:, columns] = ref[pl.ds(start, own_rows), :]
    k = silu(dot(normed_ref[...], wk_ref[...])).astype(BF)
    v = dot(normed_ref[...], wv_ref[...]).astype(BF)
    q = silu(dot(normed_ref[...], wq_ref[...])).astype(BF)
    q_ref[...] = q
    i0 = lax.broadcasted_iota(jnp.int32, (rows, rows), 0)
    i1 = lax.broadcasted_iota(jnp.int32, (rows, rows), 1)
    seen = (((i0 ^ i1) & 3) == 0) & (i1 <= i0)
    sequence = lax.broadcasted_iota(jnp.int32, (rows, 128), 0) & 3
    for h in range(2):
        cols = slice(h * 128, (h + 1) * 128)
        keys = k[:, cols].astype(F32)
        apart = jnp.concatenate([jnp.where(sequence == b, keys, 0.0).astype(BF) for b in range(4)], axis=1)
        state_ref[h * rows : (h + 1) * rows, :] = dot(apart, v[:, cols], ((0,), (0,))).astype(BF)
        scores = jnp.where(seen, dot(q[:, cols], k[:, cols], ((1,), (1,))), 0.0).astype(BF)
        local_ref[:, cols] = dot(scores, v[:, cols])


def prefix_kernel(states_ref, before_ref):
    running = jnp.zeros(states_ref.shape[1:], F32)
    for i in range(states_ref.shape[0]):
        before_ref[i] = running.astype(BF)
        running = running + states_ref[i].astype(F32)


def mix_kernel(q_ref, local_ref, carried_ref, gain_ref, out_ref):
    rows = q_ref.shape[0]
    sequence = lax.broadcasted_iota(jnp.int32, (rows, 128), 0) & 3
    for h in range(2):
        cols = slice(h * 128, (h + 1) * 128)
        q = q_ref[:, cols].astype(F32)
        apart = jnp.concatenate([jnp.where(sequence == b, q, 0.0).astype(BF) for b in range(4)], axis=1)
        mixed = local_ref[:, cols] + dot(apart, carried_ref[h * rows : (h + 1) * rows, :])
        mean = jnp.mean(mixed * mixed, axis=1, keepdims=True)
        out_ref[:, cols] = (mixed * lax.rsqrt(mean + head_eps) * gain_ref[h : h + 1, :].astype(F32)).astype(BF)


def dispatch_kernel(*refs):
    weights, refs = refs[:8], refs[8:]
    attended_ref, own_ref, gain_ref, table_ref, residual_ref, out_ref = refs
    _, width = own_ref.shape
    residual = own_ref[...].astype(F32)
    for ref, block in zip(weights, block_order()):
        residual = residual + dot(attended_ref[block], ref[...]).astype(BF).astype(F32)
    residual_ref[...] = residual
    mean = jnp.mean(residual * residual, axis=1, keepdims=True)
    gain = gain_ref[...].astype(F32)
    gain = jnp.concatenate([gain[i : i + 1, :] for i in range(gain.shape[0])], axis=1)
    entering = (residual * lax.rsqrt(mean + norm_eps) * gain).astype(BF)
    step = width // QUART
    stacked = jnp.concatenate([entering[:, q * step : (q + 1) * step] for q in range(QUART)], axis=0)
    out_ref[...] = dot(table_ref[...], stacked).astype(BF)


def expert_kernel(
    rows_ref, order_ref, back_ref, gate_ref, up_ref, down_ref, gate_b_ref, up_b_ref, down_b_ref, out_ref, x_ref
):
    sources, _, step = rows_ref.shape
    head = sources * WIDE
    part = GROUP * REST
    wide = WIDE * QUART
    for q in range(QUART):
        for i in range(sources):
            x_ref[i * WIDE : (i + 1) * WIDE, q * step : (q + 1) * step] = rows_ref[i, q * WIDE : (q + 1) * WIDE, :]
    for g in range(sources // GROUP):
        rest = rows_ref[g * GROUP : (g + 1) * GROUP, wide:, :].reshape(GROUP * REST * QUART, step)
        rest = dot(order_ref[...], rest).astype(BF)
        for q in range(QUART):
            at = head + g * part
            x_ref[at : at + part, q * step : (q + 1) * step] = rest[q * part : (q + 1) * part]
    for lines in (slice(0, head), slice(head, sources * CAP)):
        halves = []
        for gate, up, down in ((gate_ref, up_ref, down_ref), (gate_b_ref, up_b_ref, down_b_ref)):
            gated = dot(x_ref[lines, :], gate[...])
            active = (silu(gated) * dot(x_ref[lines, :], up[...])).astype(BF)
            halves.append(dot(active, down[...]).astype(BF))
        x_ref[lines, :] = (halves[0].astype(F32) + halves[1].astype(F32)).astype(BF)
    for q in range(QUART):
        for i in range(sources):
            out_ref[i, q * WIDE : (q + 1) * WIDE, :] = x_ref[i * WIDE : (i + 1) * WIDE, q * step : (q + 1) * step]
    for g in range(sources // GROUP):
        at = head + g * part
        rest = jnp.concatenate([x_ref[at : at + part, q * step : (q + 1) * step] for q in range(QUART)], axis=0)
        rest = dot(back_ref[...], rest).astype(BF)
        out_ref[g * GROUP : (g + 1) * GROUP, wide:, :] = rest.reshape(GROUP, REST * QUART, step)


def combine_kernel(rows_ref, table_ref, residual_ref, out_ref):
    rows = residual_ref.shape[0]
    step = rows_ref.shape[1]
    total = dot(table_ref[...], rows_ref[...])
    for q in range(QUART):
        cols = slice(q * step, (q + 1) * step)
        out_ref[:, cols] = (residual_ref[:, cols] + total[q * rows : (q + 1) * rows]).astype(BF)


def sorting():
    size = GROUP * REST * QUART
    order = np.zeros((size, size), np.float32)
    for q in range(QUART):
        for s in range(GROUP):
            for r in range(REST):
                order[(q * GROUP + s) * REST + r, (s * QUART + q) * REST + r] = 1.0
    return order


def body(
    tokens, attn_gain, query_weight, key_weight, value_weight, head_gain, out_weight, moe_gain,
    route_ids, route_weight, expert_gate, expert_up, expert_down,
):
    shape = jax.ShapeDtypeStruct
    block_len, batch, width = tokens.shape
    rows = block_len * batch
    model = attn_gain.shape[0]
    own_rows = rows // 8
    hidden = expert_gate.shape[2]
    order = sorting()

    attn_rows = attn_gain.reshape(-1, 128)
    head_rows = head_gain.reshape(-1, 128)
    moe_rows = moe_gain.reshape(-1, 128)
    near_weights = call(
        load_kernel,
        [pltpu.VMEM(w.shape, BF) for w in (key_weight, value_weight, query_weight, out_weight)],
        *[outside(w) for w in (key_weight, value_weight, query_weight, out_weight)],
        scratch=[pltpu.SemaphoreType.DMA((4,))],
        mib=4,
    )
    mine = tokens.reshape(rows, width)
    first = swirled(mine, 1)
    second = swirled(mine, -1)
    far = swirled(first, 1)
    pieces = [mine, first, second, far]
    pieces = pieces + [shifted(p, "c", 1) for p in pieces]

    later_out, *pieces[4:] = lax.optimization_barrier((out_weight, *pieces[4:]))
    out_first = swirled(later_out, 1)
    out_second = swirled(later_out, -1)
    out_far = swirled(out_first, 1)
    projections = [near_weights[3], out_first, out_second, out_far]
    projections = projections + [shifted(p, "c", 1) for p in (out_weight, out_first, out_second)]
    projections.append(shifted(out_far, "c", 1))
    gate = expert_gate.reshape(model, hidden)
    up = expert_up.reshape(model, hidden)
    down = expert_down.reshape(hidden, model)
    other_gate = shifted(gate, "c", 1)
    other_up = shifted(up, "c", 1)
    other_down = shifted(down, "c", 1)

    send_table, sum_table = call(
        route_kernel,
        (pltpu.VMEM((COLS, QUART * own_rows), BF), pltpu.HBM((QUART * own_rows, COLS), BF)),
        route_ids.transpose(1, 2, 0),
        route_weight.transpose(1, 2, 0),
    )

    q, local_mix, state, own = call(
        local_kernel,
        (
            pltpu.VMEM((rows, width), BF),
            pltpu.VMEM((rows, width), F32),
            pltpu.VMEM((2 * rows, 128), BF),
            pltpu.VMEM((own_rows, model), BF),
        ),
        *[inside(p) for p in pieces],
        *[inside(w) for w in near_weights[:3]],
        attn_rows,
        scratch=[pltpu.VMEM((rows, model), BF), pltpu.VMEM(attn_rows.shape, F32)],
        mib=20,
    )
    blocks = lax.axis_size(("x", "z"))
    states = inside(exchanged(state.reshape(blocks, 2 * rows // blocks, 128), ("x", "z")))
    before = call(prefix_kernel, pltpu.VMEM(states.x.shape, BF), states)
    carried = inside(exchanged(before, ("x", "z")).reshape(2 * rows, 128))
    attended = call(mix_kernel, pltpu.VMEM((rows, width), BF), inside(q), inside(local_mix), carried, head_rows)
    attended = inside(exchanged(attended.reshape(8, own_rows, width), ("y", "c")))
    step = model // QUART
    residual, sending = call(
        dispatch_kernel,
        (pltpu.HBM((own_rows, model), F32), pltpu.VMEM((COLS, step), BF)),
        *[inside(p) for p in projections],
        attended,
        inside(own),
        moe_rows,
        inside(send_table),
    )
    chips = ("x", "z", "y")
    received = inside(exchanged(sending.reshape(EXPERTS, PACK, step), chips))
    results = call(
        expert_kernel,
        pltpu.VMEM((EXPERTS, PACK, step), BF),
        received,
        either(jnp.asarray(order, BF)),
        either(jnp.asarray(order.T, BF)),
        *[inside(w) for w in (gate, up, down, other_gate, other_up, other_down)],
        scratch=[pltpu.VMEM((EXPERTS * CAP, model), BF)],
        mib=20,
    )
    returned = inside(exchanged(results, chips).reshape(COLS, step))
    out = call(combine_kernel, shape((own_rows, model), BF), returned, either(sum_table), either(residual))
    return out.reshape(own_rows // batch, batch, model)


def solution(mesh):
    fine = Mesh(mesh.devices.reshape(4, 4, 4, 2), ("x", "z", "y", "c"))
    seq, head, every = ("x", "z"), ("y", "c"), ("x", "z", "y", "c")
    in_specs = (
        P(seq, None, head),
        P(),
        P(None, head),
        P(None, head),
        P(None, head),
        P(head),
        P(head, None),
        P(),
        P(every, None, None),
        P(every, None, None),
        P(every, None, None),
        P(every, None, None),
        P(every, None, None),
    )

    return jax.shard_map(body, mesh=fine, in_specs=in_specs, out_specs=P(every, None, None), check_vma=False)
```

```python
import jax
import jax.numpy as jnp
import numpy as np
from jax import lax
from jax.experimental import pallas as pl
from jax.experimental.pallas import tpu as pltpu
from jax.sharding import Mesh, PartitionSpec as P


EXPERTS = 64
TOP = 8
CAP = 12
QUART = 4
PACK = CAP * QUART
COLS = EXPERTS * PACK
WIDE = 8
REST = CAP - WIDE
GROUP = 16

norm_eps = 1e-05
head_eps = 1e-06

BF = jnp.bfloat16
F32 = jnp.float32


def shifted(x, axis, by):
    count = lax.axis_size(axis)
    return lax.ppermute(x, axis, [(i, (i + by) % count) for i in range(count)])


def swirled(x, by):
    ways = lax.axis_size("y")
    pairs = [(2 * y + c, 2 * ((y + (by if c == 0 else -by)) % ways) + c) for y in range(ways) for c in range(2)]
    return lax.ppermute(x, ("y", "c"), pairs)


def exchanged(x, axes):
    return lax.all_to_all(x, axes, split_axis=0, concat_axis=0, tiled=True)


def dot(a, b, dims=((1,), (0,))):
    return lax.dot_general(a, b, (dims, ((), ())), preferred_element_type=F32)


def silu(v):
    return v / (1.0 + jnp.exp(-v))


INSIDE = pl.BlockSpec(memory_space=pltpu.VMEM)
OUTSIDE = pl.BlockSpec(memory_space=pltpu.HBM)


class Placed:
    def __init__(self, x, spec, fixed):
        self.x = x if fixed is None else pltpu.with_memory_space_constraint(x, fixed)
        self.spec = spec


def inside(x):
    return Placed(x, INSIDE, pltpu.VMEM)


def outside(x):
    return Placed(x, OUTSIDE, pltpu.HBM)


def loaded(x):
    return Placed(x, INSIDE, pltpu.HBM)


def either(x):
    return Placed(x, INSIDE, None)


def call(kernel, out_shape, *args, out_specs=INSIDE, scratch=(), mib=24):
    args = [x if isinstance(x, Placed) else loaded(x) for x in args]
    if isinstance(out_shape, (list, tuple)) and not isinstance(out_specs, (list, tuple)):
        out_specs = [out_specs] * len(out_shape)
    return pl.pallas_call(
        kernel,
        out_shape=out_shape,
        in_specs=[x.spec for x in args],
        out_specs=out_specs,
        scratch_shapes=list(scratch),
        compiler_params=pltpu.CompilerParams(vmem_limit_bytes=mib * 2**20),
    )(*[x.x for x in args])


def route_kernel(ids_ref, weight_ref, send_ref, sum_ref):
    batch, _, span = ids_ref.shape
    rows = batch * span
    ids = jnp.zeros((rows, TOP), F32)
    ids_t = jnp.zeros((TOP, rows), F32)
    weights = jnp.zeros((rows, TOP), F32)
    for b in range(batch):
        row = lax.broadcasted_iota(jnp.int32, (span, rows), 1)
        pick = jnp.where(lax.broadcasted_iota(jnp.int32, (span, rows), 0) * batch + b == row, 1.0, 0.0).astype(BF)
        some = ids_ref[b].astype(F32).astype(BF)
        ids = ids + dot(pick, some, ((0,), (1,)))
        ids_t = ids_t + dot(some, pick)
        weights = weights + dot(pick, weight_ref[b].astype(BF), ((0,), (1,)))
    across = lax.broadcasted_iota(jnp.int32, (rows, EXPERTS), 1).astype(F32)
    down = lax.broadcasted_iota(jnp.int32, (EXPERTS, rows), 0).astype(F32)
    named = jnp.zeros((rows, EXPERTS), F32)
    named_t = jnp.zeros((EXPERTS, rows), F32)
    weight = jnp.zeros((rows, EXPERTS), F32)
    for j in range(TOP):
        hit = ids[:, j : j + 1] == across
        named = named + jnp.where(hit, 1.0, 0.0)
        weight = weight + jnp.where(hit, weights[:, j : j + 1], 0.0)
        named_t = named_t + jnp.where(ids_t[j : j + 1, :] == down, 1.0, 0.0)
    i0 = lax.broadcasted_iota(jnp.int32, (rows, rows), 0)
    i1 = lax.broadcasted_iota(jnp.int32, (rows, rows), 1)
    before = dot(jnp.where(i1 < i0, 1.0, 0.0).astype(BF), named.astype(BF))
    before_t = dot(named_t.astype(BF), jnp.where(i0 < i1, 1.0, 0.0).astype(BF))
    slot = jnp.where(named > 0.5, before, 128.0)
    slot_t = jnp.where(named_t > 0.5, before_t, 128.0)

    def placed(slots, q):
        return jnp.where(slots < WIDE - 0.5, slots + float(WIDE * q), slots + float(WIDE * (QUART - 1) + REST * q))

    slot_all = jnp.concatenate([placed(slot, q) for q in range(QUART)], axis=0).astype(BF)
    slot_all_t = jnp.concatenate([placed(slot_t, q) for q in range(QUART)], axis=1).astype(BF)

    def split(shape, dim, other):
        index = lax.broadcasted_iota(jnp.int32, shape, dim).astype(F32)
        expert = jnp.floor((index + 0.5) * (1.0 / PACK))
        spread = jnp.where(expert == lax.broadcasted_iota(jnp.int32, shape, other).astype(F32), 1.0, 0.0)
        return spread.astype(BF), index - expert * PACK

    spread_t, place_t = split((COLS, EXPERTS), 0, 1)
    send_ref[...] = jnp.where(dot(spread_t, slot_all_t) == place_t[:, :1], 1.0, 0.0).astype(BF)
    spread, place = split((EXPERTS, COLS), 1, 0)
    match = dot(slot_all, spread) == place[:1, :]
    weight_all = dot(weight.astype(BF), spread)
    sum_ref[...] = jnp.where(match, jnp.concatenate([weight_all] * QUART, axis=0), 0.0).astype(BF)


def copied(source, target, sem):
    copy = pltpu.make_async_copy(source, target, sem)
    copy.start()
    return copy


def wait_all(copies):
    for copy in copies:
        copy.wait()


def block_order():
    y = lax.axis_index("y")
    c = lax.axis_index("c")
    return [((y + away) & 3) * 2 + core for core in (c, 1 - c) for away in (0, 3 - 2 * core, 1 + 2 * core, 2)]


def load_kernel(*refs):
    count = len(refs) // 2
    copies = [copied(refs[i], refs[count + i], refs[-1].at[i]) for i in range(count)]
    wait_all(copies)


def local_kernel(*refs):
    pieces, refs = refs[:8], refs[8:]
    wk_ref, wv_ref, wq_ref, gain_ref, q_ref, local_ref, state_ref, own_ref, normed_ref, gain_rows_ref = refs
    gain_rows_ref[...] = gain_ref[...].astype(F32)
    rows, width = pieces[0].shape
    blocks = block_order()
    total = jnp.zeros((rows, 1), F32)
    for ref in pieces:
        values = ref[...].astype(F32)
        total = total + jnp.sum(values * values, axis=1, keepdims=True)
    scale = lax.rsqrt(total / (8 * width) + norm_eps)
    own_rows = rows // 8
    start = pl.multiple_of((lax.axis_index("y") * 2 + lax.axis_index("c")) * own_rows, own_rows)
    for ref, block in zip(pieces, blocks):
        columns = pl.ds(pl.multiple_of(block * width, width), width)
        gain = jnp.concatenate([gain_rows_ref[pl.ds(2 * block + i, 1), :] for i in range(2)], axis=1)
        normed_ref[:, columns] = (ref[...].astype(F32) * scale * gain).astype(BF)
        own_ref[:, columns] = ref[pl.ds(start, own_rows), :]
    k = silu(dot(normed_ref[...], wk_ref[...])).astype(BF)
    v = dot(normed_ref[...], wv_ref[...]).astype(BF)
    q = silu(dot(normed_ref[...], wq_ref[...])).astype(BF)
    q_ref[...] = q
    i0 = lax.broadcasted_iota(jnp.int32, (rows, rows), 0)
    i1 = lax.broadcasted_iota(jnp.int32, (rows, rows), 1)
    seen = (((i0 ^ i1) & 3) == 0) & (i1 <= i0)
    sequence = lax.broadcasted_iota(jnp.int32, (rows, 128), 0) & 3
    for h in range(2):
        cols = slice(h * 128, (h + 1) * 128)
        keys = k[:, cols].astype(F32)
        apart = jnp.concatenate([jnp.where(sequence == b, keys, 0.0).astype(BF) for b in range(4)], axis=1)
        state_ref[h * rows : (h + 1) * rows, :] = dot(apart, v[:, cols], ((0,), (0,))).astype(BF)
        scores = jnp.where(seen, dot(q[:, cols], k[:, cols], ((1,), (1,))), 0.0).astype(BF)
        local_ref[:, cols] = dot(scores, v[:, cols])


def prefix_kernel(states_ref, before_ref):
    running = jnp.zeros(states_ref.shape[1:], F32)
    for i in range(states_ref.shape[0]):
        before_ref[i] = running.astype(BF)
        running = running + states_ref[i].astype(F32)


def mix_kernel(q_ref, local_ref, carried_ref, gain_ref, out_ref):
    rows = q_ref.shape[0]
    sequence = lax.broadcasted_iota(jnp.int32, (rows, 128), 0) & 3
    for h in range(2):
        cols = slice(h * 128, (h + 1) * 128)
        q = q_ref[:, cols].astype(F32)
        apart = jnp.concatenate([jnp.where(sequence == b, q, 0.0).astype(BF) for b in range(4)], axis=1)
        mixed = local_ref[:, cols] + dot(apart, carried_ref[h * rows : (h + 1) * rows, :])
        mean = jnp.mean(mixed * mixed, axis=1, keepdims=True)
        out_ref[:, cols] = (mixed * lax.rsqrt(mean + head_eps) * gain_ref[h : h + 1, :].astype(F32)).astype(BF)


def dispatch_kernel(*refs):
    weights, refs = refs[:8], refs[8:]
    attended_ref, own_ref, gain_ref, table_ref, residual_ref, out_ref = refs
    _, width = own_ref.shape
    residual = own_ref[...].astype(F32)
    for ref, block in zip(weights, block_order()):
        residual = residual + dot(attended_ref[block], ref[...]).astype(BF).astype(F32)
    residual_ref[...] = residual
    mean = jnp.mean(residual * residual, axis=1, keepdims=True)
    gain = gain_ref[...].astype(F32)
    gain = jnp.concatenate([gain[i : i + 1, :] for i in range(gain.shape[0])], axis=1)
    entering = (residual * lax.rsqrt(mean + norm_eps) * gain).astype(BF)
    step = width // QUART
    stacked = jnp.concatenate([entering[:, q * step : (q + 1) * step] for q in range(QUART)], axis=0)
    out_ref[...] = dot(table_ref[...], stacked).astype(BF)


def expert_kernel(
    rows_ref, order_ref, back_ref, gate_ref, up_ref, down_ref, gate_b_ref, up_b_ref, down_b_ref, out_ref, x_ref
):
    sources, _, step = rows_ref.shape
    head = sources * WIDE
    part = GROUP * REST
    wide = WIDE * QUART
    for q in range(QUART):
        for i in range(sources):
            x_ref[i * WIDE : (i + 1) * WIDE, q * step : (q + 1) * step] = rows_ref[i, q * WIDE : (q + 1) * WIDE, :]
    for g in range(sources // GROUP):
        rest = rows_ref[g * GROUP : (g + 1) * GROUP, wide:, :].reshape(GROUP * REST * QUART, step)
        rest = dot(order_ref[...], rest).astype(BF)
        for q in range(QUART):
            at = head + g * part
            x_ref[at : at + part, q * step : (q + 1) * step] = rest[q * part : (q + 1) * part]
    for lines in (slice(0, head), slice(head, sources * CAP)):
        halves = []
        for gate, up, down in ((gate_ref, up_ref, down_ref), (gate_b_ref, up_b_ref, down_b_ref)):
            gated = dot(x_ref[lines, :], gate[...])
            active = (silu(gated) * dot(x_ref[lines, :], up[...])).astype(BF)
            halves.append(dot(active, down[...]).astype(BF))
        x_ref[lines, :] = (halves[0].astype(F32) + halves[1].astype(F32)).astype(BF)
    for q in range(QUART):
        for i in range(sources):
            out_ref[i, q * WIDE : (q + 1) * WIDE, :] = x_ref[i * WIDE : (i + 1) * WIDE, q * step : (q + 1) * step]
    for g in range(sources // GROUP):
        at = head + g * part
        rest = jnp.concatenate([x_ref[at : at + part, q * step : (q + 1) * step] for q in range(QUART)], axis=0)
        rest = dot(back_ref[...], rest).astype(BF)
        out_ref[g * GROUP : (g + 1) * GROUP, wide:, :] = rest.reshape(GROUP, REST * QUART, step)


def combine_kernel(rows_ref, table_ref, residual_ref, out_ref):
    rows = residual_ref.shape[0]
    step = rows_ref.shape[1]
    total = dot(table_ref[...], rows_ref[...])
    for q in range(QUART):
        cols = slice(q * step, (q + 1) * step)
        out_ref[:, cols] = (residual_ref[:, cols] + total[q * rows : (q + 1) * rows]).astype(BF)


def sorting():
    size = GROUP * REST * QUART
    order = np.zeros((size, size), np.float32)
    for q in range(QUART):
        for s in range(GROUP):
            for r in range(REST):
                order[(q * GROUP + s) * REST + r, (s * QUART + q) * REST + r] = 1.0
    return order


def body(
    tokens, attn_gain, query_weight, key_weight, value_weight, head_gain, out_weight, moe_gain,
    route_ids, route_weight, expert_gate, expert_up, expert_down,
):
    shape = jax.ShapeDtypeStruct
    block_len, batch, width = tokens.shape
    rows = block_len * batch
    model = attn_gain.shape[0]
    own_rows = rows // 8
    hidden = expert_gate.shape[2]
    order = sorting()

    attn_rows = attn_gain.reshape(-1, 128)
    head_rows = head_gain.reshape(-1, 128)
    moe_rows = moe_gain.reshape(-1, 128)
    near_weights = call(
        load_kernel,
        [pltpu.VMEM(w.shape, BF) for w in (key_weight, value_weight, query_weight, out_weight)],
        *[outside(w) for w in (key_weight, value_weight, query_weight, out_weight)],
        scratch=[pltpu.SemaphoreType.DMA((4,))],
        mib=4,
    )
    mine = tokens.reshape(rows, width)
    first = swirled(mine, 1)
    second = swirled(mine, -1)
    far = swirled(first, 1)
    pieces = [mine, first, second, far]
    pieces = pieces + [shifted(mine, "c", 1)]
    pieces = pieces + [shifted(p, "c", 1) for p in (first, second, far)]

    out_first = swirled(out_weight, 1)
    out_second = swirled(out_weight, -1)
    out_far = swirled(out_first, 1)
    projections = [near_weights[3], out_first, out_second, out_far]
    projections = projections + [shifted(p, "c", 1) for p in (out_weight, out_first, out_second)]
    projections.append(shifted(out_far, "c", 1))
    gate = expert_gate.reshape(model, hidden)
    up = expert_up.reshape(model, hidden)
    down = expert_down.reshape(hidden, model)
    other_gate = shifted(gate, "c", 1)
    other_up = shifted(up, "c", 1)
    other_down = shifted(down, "c", 1)

    send_table, sum_table = call(
        route_kernel,
        (pltpu.VMEM((COLS, QUART * own_rows), BF), pltpu.HBM((QUART * own_rows, COLS), BF)),
        route_ids.transpose(1, 2, 0),
        route_weight.transpose(1, 2, 0),
    )

    q, local_mix, state, own = call(
        local_kernel,
        (
            pltpu.VMEM((rows, width), BF),
            pltpu.VMEM((rows, width), F32),
            pltpu.VMEM((2 * rows, 128), BF),
            pltpu.VMEM((own_rows, model), BF),
        ),
        *[inside(p) for p in pieces],
        *[inside(w) for w in near_weights[:3]],
        attn_rows,
        scratch=[pltpu.VMEM((rows, model), BF), pltpu.VMEM(attn_rows.shape, F32)],
        mib=20,
    )
    blocks = lax.axis_size(("x", "z"))
    states = inside(exchanged(state.reshape(blocks, 2 * rows // blocks, 128), ("x", "z")))
    before = call(prefix_kernel, pltpu.VMEM(states.x.shape, BF), states)
    carried = inside(exchanged(before, ("x", "z")).reshape(2 * rows, 128))
    attended = call(mix_kernel, pltpu.VMEM((rows, width), BF), inside(q), inside(local_mix), carried, head_rows)
    attended = inside(exchanged(attended.reshape(8, own_rows, width), ("y", "c")))
    step = model // QUART
    residual, sending = call(
        dispatch_kernel,
        (pltpu.HBM((own_rows, model), F32), pltpu.VMEM((COLS, step), BF)),
        *[inside(p) for p in projections],
        attended,
        inside(own),
        moe_rows,
        inside(send_table),
    )
    chips = ("x", "z", "y")
    received = inside(exchanged(sending.reshape(EXPERTS, PACK, step), chips))
    results = call(
        expert_kernel,
        pltpu.VMEM((EXPERTS, PACK, step), BF),
        received,
        either(jnp.asarray(order, BF)),
        either(jnp.asarray(order.T, BF)),
        *[inside(w) for w in (gate, up, down, other_gate, other_up, other_down)],
        scratch=[pltpu.VMEM((EXPERTS * CAP, model), BF)],
        mib=20,
    )
    returned = inside(exchanged(results, chips).reshape(COLS, step))
    out = call(combine_kernel, shape((own_rows, model), BF), returned, either(sum_table), either(residual))
    return out.reshape(own_rows // batch, batch, model)


def solution(mesh):
    fine = Mesh(mesh.devices.reshape(4, 4, 4, 2), ("x", "z", "y", "c"))
    seq, head, every = ("x", "z"), ("y", "c"), ("x", "z", "y", "c")
    in_specs = (
        P(seq, None, head),
        P(),
        P(None, head),
        P(None, head),
        P(None, head),
        P(head),
        P(head, None),
        P(),
        P(every, None, None),
        P(every, None, None),
        P(every, None, None),
        P(every, None, None),
        P(every, None, None),
    )

    return jax.shard_map(body, mesh=fine, in_specs=in_specs, out_specs=P(every, None, None), check_vma=False)
```

```python
import jax
import jax.numpy as jnp
import numpy as np
from jax import lax
from jax.experimental import pallas as pl
from jax.experimental.pallas import tpu as pltpu
from jax.sharding import Mesh, PartitionSpec as P


EXPERTS = 64
TOP = 8
CAP = 12
QUART = 4
PACK = CAP * QUART
COLS = EXPERTS * PACK
WIDE = 8
REST = CAP - WIDE
GROUP = 16
EARLY = (0, 1, 2, 4)

norm_eps = 1e-05
head_eps = 1e-06

BF = jnp.bfloat16
F32 = jnp.float32


def shifted(x, axis, by):
    count = lax.axis_size(axis)
    return lax.ppermute(x, axis, [(i, (i + by) % count) for i in range(count)])


def swirled(x, by):
    ways = lax.axis_size("y")
    pairs = [(2 * y + c, 2 * ((y + (by if c == 0 else -by)) % ways) + c) for y in range(ways) for c in range(2)]
    return lax.ppermute(x, ("y", "c"), pairs)


def exchanged(x, axes):
    return lax.all_to_all(x, axes, split_axis=0, concat_axis=0, tiled=True)


def dot(a, b, dims=((1,), (0,))):
    return lax.dot_general(a, b, (dims, ((), ())), preferred_element_type=F32)


def silu(v):
    return v / (1.0 + jnp.exp(-v))


INSIDE = pl.BlockSpec(memory_space=pltpu.VMEM)
OUTSIDE = pl.BlockSpec(memory_space=pltpu.HBM)


class Placed:
    def __init__(self, x, spec, fixed):
        self.x = x if fixed is None else pltpu.with_memory_space_constraint(x, fixed)
        self.spec = spec


def inside(x):
    return Placed(x, INSIDE, pltpu.VMEM)


def outside(x):
    return Placed(x, OUTSIDE, pltpu.HBM)


def loaded(x):
    return Placed(x, INSIDE, pltpu.HBM)


def either(x):
    return Placed(x, INSIDE, None)


def call(kernel, out_shape, *args, out_specs=INSIDE, scratch=(), mib=24):
    args = [x if isinstance(x, Placed) else loaded(x) for x in args]
    if isinstance(out_shape, (list, tuple)) and not isinstance(out_specs, (list, tuple)):
        out_specs = [out_specs] * len(out_shape)
    return pl.pallas_call(
        kernel,
        out_shape=out_shape,
        in_specs=[x.spec for x in args],
        out_specs=out_specs,
        scratch_shapes=list(scratch),
        compiler_params=pltpu.CompilerParams(vmem_limit_bytes=mib * 2**20),
    )(*[x.x for x in args])


def route_kernel(ids_ref, weight_ref, *refs):
    given, (send_ref, sum_ref), taken, sem = refs[:4], refs[4:6], refs[6:10], refs[10]
    copies = [copied(source, target, sem.at[i]) for i, (source, target) in enumerate(zip(given, taken))]
    batch, _, span = ids_ref.shape
    rows = batch * span
    ids = jnp.zeros((rows, TOP), F32)
    ids_t = jnp.zeros((TOP, rows), F32)
    weights = jnp.zeros((rows, TOP), F32)
    for b in range(batch):
        row = lax.broadcasted_iota(jnp.int32, (span, rows), 1)
        pick = jnp.where(lax.broadcasted_iota(jnp.int32, (span, rows), 0) * batch + b == row, 1.0, 0.0).astype(BF)
        some = ids_ref[b].astype(F32).astype(BF)
        ids = ids + dot(pick, some, ((0,), (1,)))
        ids_t = ids_t + dot(some, pick)
        weights = weights + dot(pick, weight_ref[b].astype(BF), ((0,), (1,)))
    across = lax.broadcasted_iota(jnp.int32, (rows, EXPERTS), 1).astype(F32)
    down = lax.broadcasted_iota(jnp.int32, (EXPERTS, rows), 0).astype(F32)
    named = jnp.zeros((rows, EXPERTS), F32)
    named_t = jnp.zeros((EXPERTS, rows), F32)
    weight = jnp.zeros((rows, EXPERTS), F32)
    for j in range(TOP):
        hit = ids[:, j : j + 1] == across
        named = named + jnp.where(hit, 1.0, 0.0)
        weight = weight + jnp.where(hit, weights[:, j : j + 1], 0.0)
        named_t = named_t + jnp.where(ids_t[j : j + 1, :] == down, 1.0, 0.0)
    i0 = lax.broadcasted_iota(jnp.int32, (rows, rows), 0)
    i1 = lax.broadcasted_iota(jnp.int32, (rows, rows), 1)
    before = dot(jnp.where(i1 < i0, 1.0, 0.0).astype(BF), named.astype(BF))
    before_t = dot(named_t.astype(BF), jnp.where(i0 < i1, 1.0, 0.0).astype(BF))
    slot = jnp.where(named > 0.5, before, 128.0)
    slot_t = jnp.where(named_t > 0.5, before_t, 128.0)

    def placed(slots, q):
        return jnp.where(slots < WIDE - 0.5, slots + float(WIDE * q), slots + float(WIDE * (QUART - 1) + REST * q))

    slot_all = jnp.concatenate([placed(slot, q) for q in range(QUART)], axis=0).astype(BF)
    slot_all_t = jnp.concatenate([placed(slot_t, q) for q in range(QUART)], axis=1).astype(BF)

    def split(shape, dim, other):
        index = lax.broadcasted_iota(jnp.int32, shape, dim).astype(F32)
        expert = jnp.floor((index + 0.5) * (1.0 / PACK))
        spread = jnp.where(expert == lax.broadcasted_iota(jnp.int32, shape, other).astype(F32), 1.0, 0.0)
        return spread.astype(BF), index - expert * PACK

    spread_t, place_t = split((COLS, EXPERTS), 0, 1)
    send_ref[...] = jnp.where(dot(spread_t, slot_all_t) == place_t[:, :1], 1.0, 0.0).astype(BF)
    spread, place = split((EXPERTS, COLS), 1, 0)
    match = dot(slot_all, spread) == place[:1, :]
    weight_all = dot(weight.astype(BF), spread)
    sum_ref[...] = jnp.where(match, jnp.concatenate([weight_all] * QUART, axis=0), 0.0).astype(BF)
    wait_all(copies)


def copied(source, target, sem):
    copy = pltpu.make_async_copy(source, target, sem)
    copy.start()
    return copy


def wait_all(copies):
    for copy in copies:
        copy.wait()


def block_order():
    y = lax.axis_index("y")
    c = lax.axis_index("c")
    return [((y + away) & 3) * 2 + core for core in (c, 1 - c) for away in (0, 3 - 2 * core, 1 + 2 * core, 2)]


def products(pieces, blocks, weight_refs, gain_ref, scaled_ref, rows_ref):
    rows, width = pieces[0].shape
    total = jnp.zeros((rows, 1), F32)
    for i, (ref, block) in enumerate(zip(pieces, blocks)):
        values = ref[...].astype(F32)
        total = total + jnp.sum(values * values, axis=1, keepdims=True)
        gain = jnp.concatenate([gain_ref[pl.ds(2 * block + j, 1), :] for j in range(2)], axis=1)
        scaled_ref[:, i * width : (i + 1) * width] = (values * gain).astype(BF)
    out = []
    for w, ref in enumerate(weight_refs):
        for i, block in enumerate(blocks):
            start = pl.multiple_of(block * width, width)
            rows_ref[w, i * width : (i + 1) * width, :] = ref[pl.ds(start, width), :]
        out.append(dot(scaled_ref[...], rows_ref[w]))
    return total, out


def early_kernel(*refs):
    pieces, weights = refs[:4], refs[4:7]
    gain_ref, total_ref, sum_ref, gain_rows_ref, scaled_ref, rows_ref = refs[7:]
    gain_rows_ref[...] = gain_ref[...].astype(F32)
    blocks = block_order()
    total, out = products(pieces, [blocks[i] for i in EARLY], weights, gain_rows_ref, scaled_ref, rows_ref)
    total_ref[...] = jnp.broadcast_to(total, total_ref.shape)
    for w in range(3):
        sum_ref[w] = out[w]


def local_kernel(*refs):
    pieces, weights, refs = refs[:8], refs[8:11], refs[11:]
    gain_ref, total_ref, sum_ref, q_ref, local_ref, state_ref, own_ref, gain_rows_ref, scaled_ref, rows_ref = refs
    gain_rows_ref[...] = gain_ref[...].astype(F32)
    rows, width = pieces[0].shape
    blocks = block_order()
    late = [i for i in range(8) if i not in EARLY]
    total, out = products(
        [pieces[i] for i in late], [blocks[i] for i in late], weights, gain_rows_ref, scaled_ref, rows_ref
    )
    scale = lax.rsqrt((total + total_ref[:, :1]) / (8 * width) + norm_eps)
    own_rows = rows // 8
    start = pl.multiple_of((lax.axis_index("y") * 2 + lax.axis_index("c")) * own_rows, own_rows)
    for ref, block in zip(pieces, blocks):
        own_ref[:, pl.ds(pl.multiple_of(block * width, width), width)] = ref[pl.ds(start, own_rows), :]
    k = silu((out[0] + sum_ref[0]) * scale).astype(BF)
    v = ((out[1] + sum_ref[1]) * scale).astype(BF)
    q = silu((out[2] + sum_ref[2]) * scale).astype(BF)
    q_ref[...] = q
    i0 = lax.broadcasted_iota(jnp.int32, (rows, rows), 0)
    i1 = lax.broadcasted_iota(jnp.int32, (rows, rows), 1)
    seen = (((i0 ^ i1) & 3) == 0) & (i1 <= i0)
    sequence = lax.broadcasted_iota(jnp.int32, (rows, 128), 0) & 3
    for h in range(2):
        cols = slice(h * 128, (h + 1) * 128)
        keys = k[:, cols].astype(F32)
        apart = jnp.concatenate([jnp.where(sequence == b, keys, 0.0).astype(BF) for b in range(4)], axis=1)
        state_ref[h * rows : (h + 1) * rows, :] = dot(apart, v[:, cols], ((0,), (0,))).astype(BF)
        scores = jnp.where(seen, dot(q[:, cols], k[:, cols], ((1,), (1,))), 0.0).astype(BF)
        local_ref[:, cols] = dot(scores, v[:, cols])


def prefix_kernel(states_ref, before_ref):
    running = jnp.zeros(states_ref.shape[1:], F32)
    for i in range(states_ref.shape[0]):
        before_ref[i] = running.astype(BF)
        running = running + states_ref[i].astype(F32)


def mix_kernel(q_ref, local_ref, carried_ref, gain_ref, out_ref):
    rows = q_ref.shape[0]
    sequence = lax.broadcasted_iota(jnp.int32, (rows, 128), 0) & 3
    for h in range(2):
        cols = slice(h * 128, (h + 1) * 128)
        q = q_ref[:, cols].astype(F32)
        apart = jnp.concatenate([jnp.where(sequence == b, q, 0.0).astype(BF) for b in range(4)], axis=1)
        mixed = local_ref[:, cols] + dot(apart, carried_ref[h * rows : (h + 1) * rows, :])
        mean = jnp.mean(mixed * mixed, axis=1, keepdims=True)
        out_ref[:, cols] = (mixed * lax.rsqrt(mean + head_eps) * gain_ref[h : h + 1, :].astype(F32)).astype(BF)


def dispatch_kernel(*refs):
    weights, refs = refs[:8], refs[8:]
    attended_ref, own_ref, gain_ref, table_ref, residual_ref, out_ref = refs
    _, width = own_ref.shape
    residual = own_ref[...].astype(F32)
    for ref, block in zip(weights, block_order()):
        residual = residual + dot(attended_ref[block], ref[...]).astype(BF).astype(F32)
    residual_ref[...] = residual
    mean = jnp.mean(residual * residual, axis=1, keepdims=True)
    gain = gain_ref[...].astype(F32)
    gain = jnp.concatenate([gain[i : i + 1, :] for i in range(gain.shape[0])], axis=1)
    entering = (residual * lax.rsqrt(mean + norm_eps) * gain).astype(BF)
    step = width // QUART
    stacked = jnp.concatenate([entering[:, q * step : (q + 1) * step] for q in range(QUART)], axis=0)
    out_ref[...] = dot(table_ref[...], stacked).astype(BF)


def expert_kernel(
    rows_ref, order_ref, back_ref, gate_ref, up_ref, down_ref, gate_b_ref, up_b_ref, down_b_ref, out_ref, x_ref
):
    sources, _, step = rows_ref.shape
    head = sources * WIDE
    part = GROUP * REST
    wide = WIDE * QUART
    for q in range(QUART):
        for i in range(sources):
            x_ref[i * WIDE : (i + 1) * WIDE, q * step : (q + 1) * step] = rows_ref[i, q * WIDE : (q + 1) * WIDE, :]
    for g in range(sources // GROUP):
        rest = rows_ref[g * GROUP : (g + 1) * GROUP, wide:, :].reshape(GROUP * REST * QUART, step)
        rest = dot(order_ref[...], rest).astype(BF)
        for q in range(QUART):
            at = head + g * part
            x_ref[at : at + part, q * step : (q + 1) * step] = rest[q * part : (q + 1) * part]
    for lines in (slice(0, head), slice(head, sources * CAP)):
        halves = []
        for gate, up, down in ((gate_ref, up_ref, down_ref), (gate_b_ref, up_b_ref, down_b_ref)):
            gated = dot(x_ref[lines, :], gate[...])
            active = (silu(gated) * dot(x_ref[lines, :], up[...])).astype(BF)
            halves.append(dot(active, down[...]).astype(BF))
        x_ref[lines, :] = (halves[0].astype(F32) + halves[1].astype(F32)).astype(BF)
    for q in range(QUART):
        for i in range(sources):
            out_ref[i, q * WIDE : (q + 1) * WIDE, :] = x_ref[i * WIDE : (i + 1) * WIDE, q * step : (q + 1) * step]
    for g in range(sources // GROUP):
        at = head + g * part
        rest = jnp.concatenate([x_ref[at : at + part, q * step : (q + 1) * step] for q in range(QUART)], axis=0)
        rest = dot(back_ref[...], rest).astype(BF)
        out_ref[g * GROUP : (g + 1) * GROUP, wide:, :] = rest.reshape(GROUP, REST * QUART, step)


def combine_kernel(rows_ref, table_ref, residual_ref, out_ref):
    rows = residual_ref.shape[0]
    step = rows_ref.shape[1]
    total = dot(table_ref[...], rows_ref[...])
    batch = out_ref.shape[1]
    for q in range(QUART):
        cols = slice(q * step, (q + 1) * step)
        out = residual_ref[:, cols] + total[q * rows : (q + 1) * rows]
        for i in range(rows // batch):
            out_ref[i, :, cols] = out[i * batch : (i + 1) * batch].astype(BF)


def sorting():
    size = GROUP * REST * QUART
    order = np.zeros((size, size), np.float32)
    for q in range(QUART):
        for s in range(GROUP):
            for r in range(REST):
                order[(q * GROUP + s) * REST + r, (s * QUART + q) * REST + r] = 1.0
    return order


def body(
    tokens, attn_gain, query_weight, key_weight, value_weight, head_gain, out_weight, moe_gain,
    route_ids, route_weight, expert_gate, expert_up, expert_down,
):
    shape = jax.ShapeDtypeStruct
    block_len, batch, width = tokens.shape
    rows = block_len * batch
    model = attn_gain.shape[0]
    own_rows = rows // 8
    hidden = expert_gate.shape[2]
    order = sorting()

    attn_rows = attn_gain.reshape(-1, 128)
    head_rows = head_gain.reshape(-1, 128)
    moe_rows = moe_gain.reshape(-1, 128)
    mine = tokens.reshape(rows, width)
    first = swirled(mine, 1)
    second = swirled(mine, -1)
    far = swirled(first, 1)
    pieces = [mine, first, second, far]
    pieces = pieces + [shifted(mine, "c", 1)]
    pieces = pieces + [shifted(p, "c", 1) for p in (first, second)]
    pieces = pieces + [shifted(far, "c", 1)]

    out_first = swirled(out_weight, 1)
    out_second = swirled(out_weight, -1)
    out_far = swirled(out_first, 1)
    projections = [None, out_first, out_second, out_far]
    out_other = shifted(out_weight, "c", 1)
    projections = projections + [out_other, shifted(out_first, "c", 1)]
    projections.append(shifted(out_second, "c", 1))
    projections.append(shifted(out_far, "c", 1))
    gate = expert_gate.reshape(model, hidden)
    up = expert_up.reshape(model, hidden)
    down = expert_down.reshape(hidden, model)
    other_gate = shifted(gate, "c", 1)
    other_up = shifted(up, "c", 1)
    other_down = shifted(down, "c", 1)

    early_weights = (key_weight, value_weight, query_weight, out_weight)
    send_table, sum_table, *near_weights = call(
        route_kernel,
        [
            pltpu.VMEM((COLS, QUART * own_rows), BF),
            pltpu.HBM((QUART * own_rows, COLS), BF),
            *[pltpu.VMEM(w.shape, BF) for w in early_weights],
        ],
        route_ids.transpose(1, 2, 0),
        route_weight.transpose(1, 2, 0),
        *[outside(w) for w in early_weights],
        scratch=[pltpu.SemaphoreType.DMA((4,))],
        mib=12,
    )
    projections[0] = near_weights[3]
    scratch = [
        pltpu.VMEM(attn_rows.shape, F32),
        pltpu.VMEM((rows, model // 2), BF),
        pltpu.VMEM((3, model // 2, width), BF),
    ]
    early_total, early_sum = call(
        early_kernel,
        [pltpu.VMEM((rows, 128), F32), pltpu.VMEM((3, rows, width), F32)],
        *[inside(pieces[i]) for i in EARLY],
        *[inside(w) for w in near_weights[:3]],
        attn_rows,
        scratch=scratch,
        mib=16,
    )
    q, local_mix, state, own = call(
        local_kernel,
        (
            pltpu.VMEM((rows, width), BF),
            pltpu.VMEM((rows, width), F32),
            pltpu.VMEM((2 * rows, 128), BF),
            pltpu.VMEM((own_rows, model), BF),
        ),
        *[inside(p) for p in pieces],
        *[inside(w) for w in near_weights[:3]],
        attn_rows,
        inside(early_total),
        inside(early_sum),
        scratch=scratch,
        mib=20,
    )
    blocks = lax.axis_size(("x", "z"))
    states = inside(exchanged(state.reshape(blocks, 2 * rows // blocks, 128), ("x", "z")))
    before = call(prefix_kernel, pltpu.VMEM(states.x.shape, BF), states)
    carried = inside(exchanged(before, ("x", "z")).reshape(2 * rows, 128))
    attended = call(mix_kernel, pltpu.VMEM((rows, width), BF), inside(q), inside(local_mix), carried, head_rows)
    attended = inside(exchanged(attended.reshape(8, own_rows, width), ("y", "c")))
    step = model // QUART
    residual, sending = call(
        dispatch_kernel,
        (pltpu.HBM((own_rows, model), F32), pltpu.VMEM((COLS, step), BF)),
        *[inside(p) for p in projections],
        attended,
        inside(own),
        moe_rows,
        inside(send_table),
    )
    chips = ("x", "z", "y")
    received = inside(exchanged(sending.reshape(EXPERTS, PACK, step), chips))
    results = call(
        expert_kernel,
        pltpu.VMEM((EXPERTS, PACK, step), BF),
        received,
        either(jnp.asarray(order, BF)),
        either(jnp.asarray(order.T, BF)),
        *[inside(w) for w in (gate, up, down, other_gate, other_up, other_down)],
        scratch=[pltpu.VMEM((EXPERTS * CAP, model), BF)],
        mib=20,
    )
    returned = inside(exchanged(results, chips).reshape(COLS, step))
    out = call(combine_kernel, shape((own_rows // batch, batch, model), BF), returned, either(sum_table), either(residual))
    return out


def solution(mesh):
    fine = Mesh(mesh.devices.reshape(4, 4, 4, 2), ("x", "z", "y", "c"))
    seq, head, every = ("x", "z"), ("y", "c"), ("x", "z", "y", "c")
    in_specs = (
        P(seq, None, head),
        P(),
        P(None, head),
        P(None, head),
        P(None, head),
        P(head),
        P(head, None),
        P(),
        P(every, None, None),
        P(every, None, None),
        P(every, None, None),
        P(every, None, None),
        P(every, None, None),
    )

    return jax.shard_map(body, mesh=fine, in_specs=in_specs, out_specs=P(every, None, None), check_vma=False)
```

```python
import jax
import jax.numpy as jnp
import numpy as np
from jax import lax
from jax.experimental import pallas as pl
from jax.experimental.pallas import tpu as pltpu
from jax.sharding import Mesh, PartitionSpec as P


EXPERTS = 64
TOP = 8
CAP = 12
QUART = 4
PACK = CAP * QUART
COLS = EXPERTS * PACK
WIDE = 8
REST = CAP - WIDE
GROUP = 16
EARLY = (0, 1, 4, 5)

norm_eps = 1e-05
head_eps = 1e-06

BF = jnp.bfloat16
F32 = jnp.float32


def shifted(x, axis, by):
    count = lax.axis_size(axis)
    return lax.ppermute(x, axis, [(i, (i + by) % count) for i in range(count)])


def swirled(x, by):
    ways = lax.axis_size("y")
    pairs = [(2 * y + c, 2 * ((y + (by if c == 0 else -by)) % ways) + c) for y in range(ways) for c in range(2)]
    return lax.ppermute(x, ("y", "c"), pairs)


def exchanged(x, axes):
    return lax.all_to_all(x, axes, split_axis=0, concat_axis=0, tiled=True)


def dot(a, b, dims=((1,), (0,))):
    return lax.dot_general(a, b, (dims, ((), ())), preferred_element_type=F32)


def silu(v):
    return v / (1.0 + jnp.exp(-v))


INSIDE = pl.BlockSpec(memory_space=pltpu.VMEM)
OUTSIDE = pl.BlockSpec(memory_space=pltpu.HBM)


class Placed:
    def __init__(self, x, spec, fixed):
        self.x = x if fixed is None else pltpu.with_memory_space_constraint(x, fixed)
        self.spec = spec


def inside(x):
    return Placed(x, INSIDE, pltpu.VMEM)


def outside(x):
    return Placed(x, OUTSIDE, pltpu.HBM)


def loaded(x):
    return Placed(x, INSIDE, pltpu.HBM)


def either(x):
    return Placed(x, INSIDE, None)


def call(kernel, out_shape, *args, out_specs=INSIDE, scratch=(), mib=24):
    args = [x if isinstance(x, Placed) else loaded(x) for x in args]
    if isinstance(out_shape, (list, tuple)) and not isinstance(out_specs, (list, tuple)):
        out_specs = [out_specs] * len(out_shape)
    return pl.pallas_call(
        kernel,
        out_shape=out_shape,
        in_specs=[x.spec for x in args],
        out_specs=out_specs,
        scratch_shapes=list(scratch),
        compiler_params=pltpu.CompilerParams(vmem_limit_bytes=mib * 2**20),
    )(*[x.x for x in args])


def route_kernel(ids_ref, weight_ref, *refs):
    given, (send_ref, sum_ref), taken, sem = refs[:4], refs[4:6], refs[6:10], refs[10]
    copies = [copied(source, target, sem.at[i]) for i, (source, target) in enumerate(zip(given, taken))]
    batch, _, span = ids_ref.shape
    rows = batch * span
    ids = jnp.zeros((rows, TOP), F32)
    ids_t = jnp.zeros((TOP, rows), F32)
    weights = jnp.zeros((rows, TOP), F32)
    for b in range(batch):
        row = lax.broadcasted_iota(jnp.int32, (span, rows), 1)
        pick = jnp.where(lax.broadcasted_iota(jnp.int32, (span, rows), 0) * batch + b == row, 1.0, 0.0).astype(BF)
        some = ids_ref[b].astype(F32).astype(BF)
        ids = ids + dot(pick, some, ((0,), (1,)))
        ids_t = ids_t + dot(some, pick)
        weights = weights + dot(pick, weight_ref[b].astype(BF), ((0,), (1,)))
    across = lax.broadcasted_iota(jnp.int32, (rows, EXPERTS), 1).astype(F32)
    down = lax.broadcasted_iota(jnp.int32, (EXPERTS, rows), 0).astype(F32)
    named = jnp.zeros((rows, EXPERTS), F32)
    named_t = jnp.zeros((EXPERTS, rows), F32)
    weight = jnp.zeros((rows, EXPERTS), F32)
    for j in range(TOP):
        hit = ids[:, j : j + 1] == across
        named = named + jnp.where(hit, 1.0, 0.0)
        weight = weight + jnp.where(hit, weights[:, j : j + 1], 0.0)
        named_t = named_t + jnp.where(ids_t[j : j + 1, :] == down, 1.0, 0.0)
    i0 = lax.broadcasted_iota(jnp.int32, (rows, rows), 0)
    i1 = lax.broadcasted_iota(jnp.int32, (rows, rows), 1)
    before = dot(jnp.where(i1 < i0, 1.0, 0.0).astype(BF), named.astype(BF))
    before_t = dot(named_t.astype(BF), jnp.where(i0 < i1, 1.0, 0.0).astype(BF))
    slot = jnp.where(named > 0.5, before, 128.0)
    slot_t = jnp.where(named_t > 0.5, before_t, 128.0)

    def placed(slots, q):
        return jnp.where(slots < WIDE - 0.5, slots + float(WIDE * q), slots + float(WIDE * (QUART - 1) + REST * q))

    slot_all = jnp.concatenate([placed(slot, q) for q in range(QUART)], axis=0).astype(BF)
    slot_all_t = jnp.concatenate([placed(slot_t, q) for q in range(QUART)], axis=1).astype(BF)

    def split(shape, dim, other):
        index = lax.broadcasted_iota(jnp.int32, shape, dim).astype(F32)
        expert = jnp.floor((index + 0.5) * (1.0 / PACK))
        spread = jnp.where(expert == lax.broadcasted_iota(jnp.int32, shape, other).astype(F32), 1.0, 0.0)
        return spread.astype(BF), index - expert * PACK

    spread_t, place_t = split((COLS, EXPERTS), 0, 1)
    send_ref[...] = jnp.where(dot(spread_t, slot_all_t) == place_t[:, :1], 1.0, 0.0).astype(BF)
    spread, place = split((EXPERTS, COLS), 1, 0)
    match = dot(slot_all, spread) == place[:1, :]
    weight_all = dot(weight.astype(BF), spread)
    sum_ref[...] = jnp.where(match, jnp.concatenate([weight_all] * QUART, axis=0), 0.0).astype(BF)
    wait_all(copies)


def copied(source, target, sem):
    copy = pltpu.make_async_copy(source, target, sem)
    copy.start()
    return copy


def wait_all(copies):
    for copy in copies:
        copy.wait()


def block_order():
    y = lax.axis_index("y")
    c = lax.axis_index("c")
    return [((y + away) & 3) * 2 + core for core in (c, 1 - c) for away in (0, 3 - 2 * core, 1 + 2 * core, 2)]


def products(pieces, blocks, weight_refs, gain_ref, scaled_ref, rows_ref):
    rows, width = pieces[0].shape
    total = jnp.zeros((rows, 1), F32)
    for i, (ref, block) in enumerate(zip(pieces, blocks)):
        values = ref[...].astype(F32)
        total = total + jnp.sum(values * values, axis=1, keepdims=True)
        gain = jnp.concatenate([gain_ref[pl.ds(2 * block + j, 1), :] for j in range(2)], axis=1)
        scaled_ref[:, i * width : (i + 1) * width] = (values * gain).astype(BF)
    out = []
    for w, ref in enumerate(weight_refs):
        for i, block in enumerate(blocks):
            start = pl.multiple_of(block * width, width)
            rows_ref[w, i * width : (i + 1) * width, :] = ref[pl.ds(start, width), :]
        out.append(dot(scaled_ref[...], rows_ref[w]))
    return total, out


def early_kernel(*refs):
    pieces, weights = refs[:4], refs[4:7]
    gain_ref, total_ref, sum_ref, gain_rows_ref, scaled_ref, rows_ref = refs[7:]
    gain_rows_ref[...] = gain_ref[...].astype(F32)
    blocks = block_order()
    total, out = products(pieces, [blocks[i] for i in EARLY], weights, gain_rows_ref, scaled_ref, rows_ref)
    total_ref[...] = jnp.broadcast_to(total, total_ref.shape)
    for w in range(3):
        sum_ref[w] = out[w]


def local_kernel(*refs):
    pieces, weights, refs = refs[:8], refs[8:11], refs[11:]
    gain_ref, total_ref, sum_ref, q_ref, local_ref, state_ref, own_ref, gain_rows_ref, scaled_ref, rows_ref = refs
    gain_rows_ref[...] = gain_ref[...].astype(F32)
    rows, width = pieces[0].shape
    blocks = block_order()
    late = [i for i in range(8) if i not in EARLY]
    total, out = products(
        [pieces[i] for i in late], [blocks[i] for i in late], weights, gain_rows_ref, scaled_ref, rows_ref
    )
    scale = lax.rsqrt((total + total_ref[:, :1]) / (8 * width) + norm_eps)
    own_rows = rows // 8
    start = pl.multiple_of((lax.axis_index("y") * 2 + lax.axis_index("c")) * own_rows, own_rows)
    for ref, block in zip(pieces, blocks):
        own_ref[:, pl.ds(pl.multiple_of(block * width, width), width)] = ref[pl.ds(start, own_rows), :]
    k = silu((out[0] + sum_ref[0]) * scale).astype(BF)
    v = ((out[1] + sum_ref[1]) * scale).astype(BF)
    q = silu((out[2] + sum_ref[2]) * scale).astype(BF)
    q_ref[...] = q
    i0 = lax.broadcasted_iota(jnp.int32, (rows, rows), 0)
    i1 = lax.broadcasted_iota(jnp.int32, (rows, rows), 1)
    seen = (((i0 ^ i1) & 3) == 0) & (i1 <= i0)
    sequence = lax.broadcasted_iota(jnp.int32, (rows, 128), 0) & 3
    for h in range(2):
        cols = slice(h * 128, (h + 1) * 128)
        keys = k[:, cols].astype(F32)
        apart = jnp.concatenate([jnp.where(sequence == b, keys, 0.0).astype(BF) for b in range(4)], axis=1)
        state_ref[h * rows : (h + 1) * rows, :] = dot(apart, v[:, cols], ((0,), (0,))).astype(BF)
        scores = jnp.where(seen, dot(q[:, cols], k[:, cols], ((1,), (1,))), 0.0).astype(BF)
        local_ref[:, cols] = dot(scores, v[:, cols])


def prefix_kernel(states_ref, before_ref):
    running = jnp.zeros(states_ref.shape[1:], F32)
    for i in range(states_ref.shape[0]):
        before_ref[i] = running.astype(BF)
        running = running + states_ref[i].astype(F32)


def mix_kernel(q_ref, local_ref, carried_ref, gain_ref, out_ref):
    rows = q_ref.shape[0]
    sequence = lax.broadcasted_iota(jnp.int32, (rows, 128), 0) & 3
    for h in range(2):
        cols = slice(h * 128, (h + 1) * 128)
        q = q_ref[:, cols].astype(F32)
        apart = jnp.concatenate([jnp.where(sequence == b, q, 0.0).astype(BF) for b in range(4)], axis=1)
        mixed = local_ref[:, cols] + dot(apart, carried_ref[h * rows : (h + 1) * rows, :])
        mean = jnp.mean(mixed * mixed, axis=1, keepdims=True)
        out_ref[:, cols] = (mixed * lax.rsqrt(mean + head_eps) * gain_ref[h : h + 1, :].astype(F32)).astype(BF)


def dispatch_kernel(*refs):
    weights, refs = refs[:8], refs[8:]
    attended_ref, own_ref, gain_ref, table_ref, residual_ref, out_ref = refs
    _, width = own_ref.shape
    residual = own_ref[...].astype(F32)
    for ref, block in zip(weights, block_order()):
        residual = residual + dot(attended_ref[block], ref[...]).astype(BF).astype(F32)
    residual_ref[...] = residual
    mean = jnp.mean(residual * residual, axis=1, keepdims=True)
    gain = gain_ref[...].astype(F32)
    gain = jnp.concatenate([gain[i : i + 1, :] for i in range(gain.shape[0])], axis=1)
    entering = (residual * lax.rsqrt(mean + norm_eps) * gain).astype(BF)
    step = width // QUART
    stacked = jnp.concatenate([entering[:, q * step : (q + 1) * step] for q in range(QUART)], axis=0)
    out_ref[...] = dot(table_ref[...], stacked).astype(BF)


def expert_kernel(
    rows_ref, order_ref, back_ref, gate_ref, up_ref, down_ref, gate_b_ref, up_b_ref, down_b_ref, out_ref, x_ref
):
    sources, _, step = rows_ref.shape
    head = sources * WIDE
    part = GROUP * REST
    wide = WIDE * QUART
    for q in range(QUART):
        for i in range(sources):
            x_ref[i * WIDE : (i + 1) * WIDE, q * step : (q + 1) * step] = rows_ref[i, q * WIDE : (q + 1) * WIDE, :]
    for g in range(sources // GROUP):
        rest = rows_ref[g * GROUP : (g + 1) * GROUP, wide:, :].reshape(GROUP * REST * QUART, step)
        rest = dot(order_ref[...], rest).astype(BF)
        for q in range(QUART):
            at = head + g * part
            x_ref[at : at + part, q * step : (q + 1) * step] = rest[q * part : (q + 1) * part]
    for lines in (slice(0, head), slice(head, sources * CAP)):
        halves = []
        for gate, up, down in ((gate_ref, up_ref, down_ref), (gate_b_ref, up_b_ref, down_b_ref)):
            gated = dot(x_ref[lines, :], gate[...])
            active = (silu(gated) * dot(x_ref[lines, :], up[...])).astype(BF)
            halves.append(dot(active, down[...]).astype(BF))
        x_ref[lines, :] = (halves[0].astype(F32) + halves[1].astype(F32)).astype(BF)
    for q in range(QUART):
        for i in range(sources):
            out_ref[i, q * WIDE : (q + 1) * WIDE, :] = x_ref[i * WIDE : (i + 1) * WIDE, q * step : (q + 1) * step]
    for g in range(sources // GROUP):
        at = head + g * part
        rest = jnp.concatenate([x_ref[at : at + part, q * step : (q + 1) * step] for q in range(QUART)], axis=0)
        rest = dot(back_ref[...], rest).astype(BF)
        out_ref[g * GROUP : (g + 1) * GROUP, wide:, :] = rest.reshape(GROUP, REST * QUART, step)


def combine_kernel(rows_ref, table_ref, residual_ref, out_ref):
    rows = residual_ref.shape[0]
    step = rows_ref.shape[1]
    total = dot(table_ref[...], rows_ref[...])
    batch = out_ref.shape[1]
    for q in range(QUART):
        cols = slice(q * step, (q + 1) * step)
        out = residual_ref[:, cols] + total[q * rows : (q + 1) * rows]
        for i in range(rows // batch):
            out_ref[i, :, cols] = out[i * batch : (i + 1) * batch].astype(BF)


def sorting():
    size = GROUP * REST * QUART
    order = np.zeros((size, size), np.float32)
    for q in range(QUART):
        for s in range(GROUP):
            for r in range(REST):
                order[(q * GROUP + s) * REST + r, (s * QUART + q) * REST + r] = 1.0
    return order


def body(
    tokens, attn_gain, query_weight, key_weight, value_weight, head_gain, out_weight, moe_gain,
    route_ids, route_weight, expert_gate, expert_up, expert_down,
):
    shape = jax.ShapeDtypeStruct
    block_len, batch, width = tokens.shape
    rows = block_len * batch
    model = attn_gain.shape[0]
    own_rows = rows // 8
    hidden = expert_gate.shape[2]
    order = sorting()

    attn_rows = attn_gain.reshape(-1, 128)
    head_rows = head_gain.reshape(-1, 128)
    moe_rows = moe_gain.reshape(-1, 128)
    mine = tokens.reshape(rows, width)
    first = swirled(mine, 1)
    second = swirled(mine, -1)
    far = swirled(first, 1)
    pieces = [mine, first, second, far]
    pieces = pieces + [shifted(mine, "c", 1)]
    pieces = pieces + [shifted(first, "c", 1)]
    pieces = pieces + [shifted(second, "c", 1)]
    pieces = pieces + [shifted(far, "c", 1)]

    out_first = swirled(out_weight, 1)
    out_second = swirled(out_weight, -1)
    out_far = swirled(out_first, 1)
    projections = [None, out_first, out_second, out_far]
    out_other = shifted(out_weight, "c", 1)
    projections = projections + [out_other, shifted(out_first, "c", 1)]
    projections.append(shifted(out_second, "c", 1))
    projections.append(shifted(out_far, "c", 1))
    gate = expert_gate.reshape(model, hidden)
    up = expert_up.reshape(model, hidden)
    down = expert_down.reshape(hidden, model)
    other_gate = shifted(gate, "c", 1)
    other_up = shifted(up, "c", 1)
    other_down = shifted(down, "c", 1)

    early_weights = (key_weight, value_weight, query_weight, out_weight)
    send_table, sum_table, *near_weights = call(
        route_kernel,
        [
            pltpu.VMEM((COLS, QUART * own_rows), BF),
            pltpu.HBM((QUART * own_rows, COLS), BF),
            *[pltpu.VMEM(w.shape, BF) for w in early_weights],
        ],
        route_ids.transpose(1, 2, 0),
        route_weight.transpose(1, 2, 0),
        *[outside(w) for w in early_weights],
        scratch=[pltpu.SemaphoreType.DMA((4,))],
        mib=12,
    )
    projections[0] = near_weights[3]
    scratch = [
        pltpu.VMEM(attn_rows.shape, F32),
        pltpu.VMEM((rows, model // 2), BF),
        pltpu.VMEM((3, model // 2, width), BF),
    ]
    early_total, early_sum = call(
        early_kernel,
        [pltpu.VMEM((rows, 128), F32), pltpu.VMEM((3, rows, width), F32)],
        *[inside(pieces[i]) for i in EARLY],
        *[inside(w) for w in near_weights[:3]],
        attn_rows,
        scratch=scratch,
        mib=16,
    )
    q, local_mix, state, own = call(
        local_kernel,
        (
            pltpu.VMEM((rows, width), BF),
            pltpu.VMEM((rows, width), F32),
            pltpu.VMEM((2 * rows, 128), BF),
            pltpu.VMEM((own_rows, model), BF),
        ),
        *[inside(p) for p in pieces],
        *[inside(w) for w in near_weights[:3]],
        attn_rows,
        inside(early_total),
        inside(early_sum),
        scratch=scratch,
        mib=20,
    )
    blocks = lax.axis_size(("x", "z"))
    states = inside(exchanged(state.reshape(blocks, 2 * rows // blocks, 128), ("x", "z")))
    before = call(prefix_kernel, pltpu.VMEM(states.x.shape, BF), states)
    carried = inside(exchanged(before, ("x", "z")).reshape(2 * rows, 128))
    attended = call(mix_kernel, pltpu.VMEM((rows, width), BF), inside(q), inside(local_mix), carried, head_rows)
    attended = inside(exchanged(attended.reshape(8, own_rows, width), ("y", "c")))
    step = model // QUART
    residual, sending = call(
        dispatch_kernel,
        (pltpu.HBM((own_rows, model), F32), pltpu.VMEM((COLS, step), BF)),
        *[inside(p) for p in projections],
        attended,
        inside(own),
        moe_rows,
        inside(send_table),
    )
    chips = ("x", "z", "y")
    received = inside(exchanged(sending.reshape(EXPERTS, PACK, step), chips))
    results = call(
        expert_kernel,
        pltpu.VMEM((EXPERTS, PACK, step), BF),
        received,
        either(jnp.asarray(order, BF)),
        either(jnp.asarray(order.T, BF)),
        *[inside(w) for w in (gate, up, down, other_gate, other_up, other_down)],
        scratch=[pltpu.VMEM((EXPERTS * CAP, model), BF)],
        mib=20,
    )
    returned = inside(exchanged(results, chips).reshape(COLS, step))
    out = call(combine_kernel, shape((own_rows // batch, batch, model), BF), returned, either(sum_table), either(residual))
    return out


def solution(mesh):
    fine = Mesh(mesh.devices.reshape(4, 4, 4, 2), ("x", "z", "y", "c"))
    seq, head, every = ("x", "z"), ("y", "c"), ("x", "z", "y", "c")
    in_specs = (
        P(seq, None, head),
        P(),
        P(None, head),
        P(None, head),
        P(None, head),
        P(head),
        P(head, None),
        P(),
        P(every, None, None),
        P(every, None, None),
        P(every, None, None),
        P(every, None, None),
        P(every, None, None),
    )

    return jax.shard_map(body, mesh=fine, in_specs=in_specs, out_specs=P(every, None, None), check_vma=False)
```
